128 devices in a mesh: seq: 32 (over x, y, core), head: 4 (over z).
Axes of the slice: x: 4, y: 4, z: 4, core: 2. Of those that a mesh axis runs over, the one named last changes fastest.
Arguments:
- group_of: int32 [32], replicated, may hold values from 0 to 31, as said below
- soft_query: bfloat16 [8192, 1536], P('seq', 'head'), may hold values from -8 to 8
- soft_key: bfloat16 [8192, 1536], P('seq', 'head'), may hold values from -8 to 8
- soft_value: bfloat16 [8192, 1536], P('seq', 'head'), may hold values from -6 to 6
- soft_grad: bfloat16 [8192, 1536], P('seq', 'head'), may hold values from -6 to 6
- lin_query: bfloat16 [8192, 1536], P('seq', 'head'), may hold values from -6 to 6
- lin_key: bfloat16 [8192, 1536], P('seq', 'head'), may hold values from -0.59765625 to 0.59765625
- lin_value: bfloat16 [8192, 1536], P('seq', 'head'), may hold values from -40 to 40
- log_decay: float32 [8192, 12], P('seq', 'head'), may hold values from -1 to 0
- lin_grad: bfloat16 [8192, 1536], P('seq', 'head'), may hold values from -6 to 6
Outputs:
- soft_out: bfloat16 [8192, 1536], P('seq', 'head')
- soft_dq: bfloat16 [8192, 1536], P('seq', 'head')
- soft_dk: bfloat16 [8192, 1536], P('seq', 'head')
- soft_dv: bfloat16 [8192, 1536], P('seq', 'head')
- lin_out: float32 [8192, 1536], P('seq', 'head')
- lin_dq: float32 [8192, 1536], P('seq', 'head')
- lin_dk: float32 [8192, 1536], P('seq', 'head')
- lin_dv: float32 [8192, 1536], P('seq', 'head')
The draws below stay inside these ranges and needn't reach their ends.
Inputs may be any that keep to these rules, and one draw needn't show every extreme that they name: group_of[d] = (group_of[0] + d) mod 32: the indices of seq hold the sequence's blocks in order around the axis, from a drawn first index.
All inputs are finite; a program needn't handle non-finite values.
Results may differ from the reference program's by a relative error of at most 0.017.
Values may be sent and summed in bfloat16 or wider, within the bound.
No kernel may reach another device: no remote copies, remote signals or barrier semaphores. Data moves between devices by JAX's collectives and lax.ppermute only.
A program may use at most 128 MiB of HBM per device.

```python
import math
import jax
import jax.numpy as jnp
from jax import lax

HEAD_TOTAL = 12
HEAD_DIM = 128
TOK_DEV = 256
SEQUENCE_LENGTH = 8192
N_SEQ = 32


def base_field(key):
    values_drawn = jnp.clip(jax.random.normal(key, (SEQUENCE_LENGTH, HEAD_TOTAL * HEAD_DIM), jnp.float32), -6.0, 6.0)
    return values_drawn


def draw_group_of(key, part):
    first_part = jax.random.randint(jax.random.fold_in(key, 211), (), 0, N_SEQ)
    mixing = jax.random.permutation(jax.random.fold_in(key, 223), N_SEQ)
    offset = (first_part + mixing[0]) % N_SEQ
    return ((jnp.arange(N_SEQ, dtype=jnp.int32) + offset) % N_SEQ).astype(jnp.int32)


def draw_soft_query(key, part):
    values_drawn = base_field(jax.random.fold_in(key, 1))
    return values_drawn.astype(jnp.bfloat16)


def draw_soft_key(key, part):
    values_drawn = base_field(jax.random.fold_in(key, 2))
    return values_drawn.astype(jnp.bfloat16)


def draw_lin_value(key, part):
    values_drawn = base_field(jax.random.fold_in(key, 3))
    row_scale = jnp.exp(jax.random.uniform(jax.random.fold_in(key, 4), (SEQUENCE_LENGTH, 1), jnp.float32, math.log(0.5), math.log(2.0)))
    head_share = (jnp.arange(HEAD_TOTAL * HEAD_DIM) // HEAD_DIM).astype(jnp.float32) / (HEAD_TOTAL - 1)
    rising = 0.5
    spread = jax.random.uniform(jax.random.fold_in(key, 5), (HEAD_TOTAL * HEAD_DIM,), jnp.float32, 0.0, 0.5)
    column_scale = jnp.power(10.0, rising * head_share + spread) / math.sqrt(10.0)
    return (values_drawn * row_scale * column_scale[None, :]).astype(jnp.bfloat16)


def draw_log_decay(key, part):
    order = jax.random.permutation(jax.random.fold_in(key, 8), HEAD_TOTAL)
    slow_count = HEAD_TOTAL // 2
    slow_heads = order < slow_count
    slow_rate = jax.random.uniform(jax.random.fold_in(key, 9), (HEAD_TOTAL,), jnp.float32, 0.02, 0.12) / SEQUENCE_LENGTH
    fast_rate = jax.random.uniform(jax.random.fold_in(key, 10), (HEAD_TOTAL,), jnp.float32, math.log(10.0) / 50.0, math.log(10.0) / 30.0)
    head_rate = jnp.where(slow_heads, slow_rate, fast_rate)
    jitter = jax.random.uniform(jax.random.fold_in(key, 11), (SEQUENCE_LENGTH, HEAD_TOTAL), jnp.float32, 0.5, 1.5)
    stable_phase = -head_rate[None, :] * jitter
    rotation_rows = jax.random.randint(jax.random.fold_in(key, 12), (3,), 0, SEQUENCE_LENGTH)
    rotation_match = jnp.any(jnp.arange(SEQUENCE_LENGTH)[:, None] == rotation_rows[None, :], axis=1)
    rotation_depth = jnp.log(jax.random.uniform(jax.random.fold_in(key, 13), (SEQUENCE_LENGTH, HEAD_TOTAL), jnp.float32, 0.5, 0.8))
    return (stable_phase + jnp.where(rotation_match[:, None], rotation_depth, 0.0)).astype(jnp.float32)


def shard_levels(stream_key, extent, split, smallest, high):
    level, own = 1.0, jax.random.fold_in(stream_key, 6)
    for position, parts in split:
        heights = jnp.exp(jax.random.uniform(jax.random.fold_in(own, position), (parts,), jnp.float32, smallest / len(split), high / len(split)))
        level = level * jnp.repeat(heights, extent[position] // parts).reshape([-1 if axis == position else 1 for axis in range(len(extent))])
    return level


def bell_draw(rng, dims, scale, limit, cuts=(), kind=jnp.bfloat16):
    drawn = scale * jax.random.normal(rng, dims, jnp.float32)
    if cuts:
        drawn = drawn * shard_levels(rng, dims, cuts, -0.22, 0.18)
    return jnp.clip(drawn, -limit, limit).astype(kind)


def setup_inputs(seed: int = 0) -> dict:
    splits = jax.random.split(jax.random.key(seed), 11)
    return {
        "group_of": draw_group_of(jax.random.fold_in(splits[10], 71), 0),
        "soft_query": draw_soft_query(jax.random.fold_in(splits[10], 71), 0),
        "soft_key": draw_soft_key(jax.random.fold_in(splits[10], 71), 0),
        "soft_value": bell_draw(splits[3], (SEQUENCE_LENGTH, HEAD_TOTAL * HEAD_DIM), 1.0, 6.0, ((0, 32), (1, 4))),
        "soft_grad": bell_draw(splits[4], (SEQUENCE_LENGTH, HEAD_TOTAL * HEAD_DIM), 1.0, 6.0, ((0, 32), (1, 4))),
        "lin_query": bell_draw(splits[5], (SEQUENCE_LENGTH, HEAD_TOTAL * HEAD_DIM), 1.0, 6.0, ((0, 32), (1, 4))),
        "lin_key": bell_draw(splits[6], (SEQUENCE_LENGTH, HEAD_TOTAL * HEAD_DIM), 0.1, 0.59765625, ((0, 32), (1, 4))),
        "lin_value": draw_lin_value(jax.random.fold_in(splits[10], 71), 0),
        "log_decay": draw_log_decay(jax.random.fold_in(splits[10], 71), 0),
        "lin_grad": bell_draw(splits[9], (SEQUENCE_LENGTH, HEAD_TOTAL * HEAD_DIM), 1.0, 6.0, ((0, 32), (1, 4))),
    }


EPS = 1e-06
HIGHEST = lax.Precision.HIGHEST

def device_to_sequence(matrix, order):
    blocks = matrix.reshape((N_SEQ, TOK_DEV) + matrix.shape[1:])
    return blocks[order].reshape(matrix.shape)

def sequence_to_device(matrix, group_of):
    blocks = matrix.reshape((N_SEQ, TOK_DEV) + matrix.shape[1:])
    return blocks[group_of].reshape(matrix.shape)

def by_heads(matrix):
    return matrix.reshape(SEQUENCE_LENGTH, HEAD_TOTAL, HEAD_DIM).transpose(1, 0, 2)

def from_heads(stacked):
    return stacked.transpose(1, 0, 2).reshape(SEQUENCE_LENGTH, HEAD_TOTAL * HEAD_DIM)

def softmax_head(inputs):
    query_head, key_head, value_head, grad_head = inputs
    score_scale = HEAD_DIM ** (-0.5)
    positions = jnp.arange(SEQUENCE_LENGTH, dtype=jnp.int32)
    causal = positions[:, None] >= positions[None, :]
    scores = jnp.dot(query_head, key_head.T, preferred_element_type=jnp.float32) * score_scale
    scores = jnp.where(causal, scores, -jnp.inf)
    row_max = lax.optimization_barrier(jnp.max(scores, axis=1, keepdims=True))
    log_total = row_max + jnp.log(lax.optimization_barrier(jnp.sum(jnp.exp(scores - row_max), axis=1, keepdims=True)))
    probs_full = jnp.exp(scores - log_total)
    probs_half = probs_full.astype(jnp.bfloat16)
    out_head = jnp.dot(probs_half, value_head, preferred_element_type=jnp.float32).astype(jnp.bfloat16)
    delta_rows = lax.optimization_barrier(jnp.sum(grad_head.astype(jnp.float32) * out_head.astype(jnp.float32), axis=1, keepdims=True))
    dprobs = jnp.dot(grad_head, value_head.T, preferred_element_type=jnp.float32)
    dscores = (probs_full * (dprobs - delta_rows)).astype(jnp.bfloat16)
    value_grad = jnp.dot(probs_half.T, grad_head, preferred_element_type=jnp.float32).astype(jnp.bfloat16)
    query_grad = (jnp.dot(dscores, key_head, preferred_element_type=jnp.float32) * score_scale).astype(jnp.bfloat16)
    key_grad = (jnp.dot(dscores.T, query_head, preferred_element_type=jnp.float32) * score_scale).astype(jnp.bfloat16)
    return (out_head, query_grad, key_grad, value_grad)

def linear_core(queries, keys, values, decays):
    block_dimensions = (N_SEQ, TOK_DEV, HEAD_TOTAL, HEAD_DIM)
    lower_mask = jnp.arange(TOK_DEV)[:, None] >= jnp.arange(TOK_DEV)[None, :]

    def block_step(carried, inputs):
        query_block, key_block, value_block, decay_block = inputs
        cumulative = jnp.cumsum(decay_block, axis=0)
        log_gap = cumulative[:, None, :] - cumulative[None, :, :]
        inner_decay = jnp.where(lower_mask[:, :, None], jnp.exp(jnp.where(lower_mask[:, :, None], log_gap, 0.0)), 0.0)
        inner_scores = jnp.einsum('thd,shd->tsh', query_block, key_block, precision=HIGHEST) * inner_decay
        local_out = jnp.einsum('tsh,shd->thd', inner_scores, value_block, precision=HIGHEST)
        carried_out = jnp.exp(cumulative)[:, :, None] * jnp.einsum('thd,hde->the', query_block, carried, precision=HIGHEST)
        block_log = cumulative[-1]
        scaled_keys = key_block * jnp.exp(block_log[None, :] - cumulative)[:, :, None]
        carried = jnp.exp(block_log)[:, None, None] * carried + jnp.einsum('shd,she->hde', scaled_keys, value_block, precision=HIGHEST)
        return (carried, local_out + carried_out)
    start_state = jnp.zeros((HEAD_TOTAL, HEAD_DIM, HEAD_DIM), jnp.float32)
    inputs = (queries.reshape(block_dimensions), keys.reshape(block_dimensions), values.reshape(block_dimensions), decays.reshape(N_SEQ, TOK_DEV, HEAD_TOTAL))
    _, raw_out = lax.scan(block_step, start_state, inputs)
    raw_out = raw_out.reshape(SEQUENCE_LENGTH, HEAD_TOTAL * HEAD_DIM)
    row_rms = jnp.sqrt(lax.optimization_barrier(jnp.mean(raw_out * raw_out, axis=1, keepdims=True)) + EPS)
    return raw_out / row_rms

def reference(group_of, soft_query, soft_key, soft_value, soft_grad, lin_query, lin_key, lin_value, log_decay, lin_grad):
    order = jnp.argsort(group_of).astype(jnp.int32)
    soft_inputs = tuple((by_heads(device_to_sequence(matrix, order)) for matrix in (soft_query, soft_key, soft_value, soft_grad)))
    soft_parts = lax.map(softmax_head, soft_inputs)
    soft_out, soft_dq, soft_dk, soft_dv = (sequence_to_device(from_heads(matrix), group_of) for matrix in soft_parts)

    def as_float(matrix):
        return device_to_sequence(matrix, order).astype(jnp.float32).reshape(SEQUENCE_LENGTH, HEAD_TOTAL, HEAD_DIM)
    lin_seq, pullback = jax.vjp(linear_core, as_float(lin_query), as_float(lin_key), as_float(lin_value), device_to_sequence(log_decay, order))
    upstream = device_to_sequence(lin_grad, order).astype(jnp.float32)
    gradients = pullback(upstream)
    lin_dq, lin_dk, lin_dv = (sequence_to_device(matrix.reshape(SEQUENCE_LENGTH, HEAD_TOTAL * HEAD_DIM), group_of) for matrix in gradients[:3])
    lin_out = sequence_to_device(lin_seq, group_of)
    return (soft_out, soft_dq, soft_dk, soft_dv, lin_out, lin_dq, lin_dk, lin_dv)
```

```python
import jax
import jax.numpy as jnp
from jax import lax
from jax.experimental import pallas as pl
from jax.experimental.pallas import tpu as pltpu
from jax.sharding import Mesh
from jax.sharding import PartitionSpec as P

HEAD_TOTAL = 12
HEAD_DIM = 128
HEADS = 3
TOK = 256
NX, NY, NC = 4, 4, 2
EPS = 1e-06
SCALE = HEAD_DIM ** (-0.5)
LOG2E = 1.4426950408889634
NEG = -1e30
F32 = jnp.float32
BF16 = jnp.bfloat16


def send(block, axis, size, offset):
    return lax.ppermute(block, axis, [(i, (i + offset) % size) for i in range(size)])


def fetch(block, axis, size, offset):
    return send(block, axis, size, -offset)


def dot_nt(a, b):
    return lax.dot_general(a, b, (((1,), (1,)), ((), ())), preferred_element_type=F32)


def dot_nn(a, b):
    return lax.dot_general(a, b, (((1,), (0,)), ((), ())), preferred_element_type=F32)


def key_scores(k, q, diagonal):
    s = dot_nt(k, q) * (SCALE * LOG2E)
    if diagonal is not None:
        key_row = lax.broadcasted_iota(jnp.int32, s.shape, 0)
        query_col = lax.broadcasted_iota(jnp.int32, s.shape, 1)
        limit = jnp.where(diagonal > 0, 0, TOK)
        s = jnp.where(key_row <= query_col + limit, s, NEG)
    return s


def forward_kernel(count_ref, diag_ref, slot_ref, qg_ref, kv_ref, out_ref, stat_ref, vt_ref):
    for o in range(NX):
        vt_ref[o] = kv_ref[o, 1].T

    @pl.loop(0, NY)
    def _(i):
        count = count_ref[i]

        @pl.when(count == 0)
        def _():
            out_ref[i, 0] = jnp.zeros((HEAD_DIM, TOK), BF16)
            stat_ref[0, pl.ds(2 * i, 1)] = jnp.full((1, TOK), NEG, F32)
            stat_ref[0, pl.ds(2 * i + 1, 1)] = jnp.zeros((1, TOK), F32)

        for n in range(1, NX + 1):

            @pl.when(count == n)
            def _():
                q = qg_ref[i, 0]
                parts = [
                    key_scores(kv_ref[slot_ref[m], 0], q, diag_ref[i] if m == n - 1 else None)
                    for m in range(n)
                ]
                top = jnp.max(parts[0], axis=0, keepdims=True)
                for s in parts[1:]:
                    top = jnp.maximum(top, jnp.max(s, axis=0, keepdims=True))
                total = jnp.zeros((1, TOK), F32)
                acc = jnp.zeros((HEAD_DIM, TOK), F32)
                for m in range(n):
                    p = jnp.exp2(parts[m] - top)
                    total = total + jnp.sum(p, axis=0, keepdims=True)
                    acc = acc + dot_nn(vt_ref[slot_ref[m]], p.astype(BF16))
                acc = acc / total
                out_ref[i, 0] = acc.astype(BF16)
                grad = qg_ref[i, 1].astype(F32).T
                stat_ref[0, pl.ds(2 * i, 1)] = top + jnp.log(total) * LOG2E
                stat_ref[0, pl.ds(2 * i + 1, 1)] = jnp.sum(acc * grad, axis=0, keepdims=True)


def soft_forward(count, diag, slot, qg, kv):
    tiles = NY * NX * HEADS
    return pl.pallas_call(
        forward_kernel,
        grid_spec=pltpu.PrefetchScalarGridSpec(
            num_scalar_prefetch=3,
            grid=(HEADS,),
            in_specs=[
                pl.BlockSpec((NY, 2, TOK, HEAD_DIM), lambda h, *_: (0, 0, 0, h)),
                pl.BlockSpec((NX, 2, TOK, HEAD_DIM), lambda h, *_: (0, 0, 0, h)),
            ],
            out_specs=[
                pl.BlockSpec((NY, 1, HEAD_DIM, TOK), lambda h, *_: (0, h, 0, 0)),
                pl.BlockSpec((1, 2 * NY, TOK), lambda h, *_: (h, 0, 0)),
            ],
            scratch_shapes=[pltpu.VMEM((NX, HEAD_DIM, TOK), BF16)],
        ),
        out_shape=[
            jax.ShapeDtypeStruct((NY, HEADS, HEAD_DIM, TOK), BF16),
            jax.ShapeDtypeStruct((HEADS, 2 * NY, TOK), F32),
        ],
        cost_estimate=pl.CostEstimate(
            flops=tiles * 4 * TOK * TOK * HEAD_DIM,
            transcendentals=tiles * TOK * TOK,
            bytes_accessed=4 * 2**20,
        ),
        compiler_params=pltpu.CompilerParams(vmem_limit_bytes=32 * 2**20),
        name="soft_forward",
    )(count, diag, slot, qg, kv)


def backward_kernel(
    count_ref, diag_ref, slot_ref, qa_ref, qb_ref, kv_ref, stat_ref,
    dqa_ref, dqb_ref, dkv_ref, kt_ref, acc_ref,
):
    for o in range(NX):
        kt_ref[o] = kv_ref[o, 0].T
    acc_ref[...] = jnp.zeros_like(acc_ref)

    def one_block(qg_ref, dq_ref, b, i):
        count = count_ref[i]

        @pl.when(count == 0)
        def _():
            dq_ref[b] = jnp.zeros((TOK, HEAD_DIM), BF16)

        for n in range(1, NX + 1):

            @pl.when(count == n)
            def _():
                q = qg_ref[b, 0]
                g = qg_ref[b, 1]
                lse = stat_ref[0, pl.ds(2 * i, 1)]
                delta = stat_ref[0, pl.ds(2 * i + 1, 1)]
                dqt = jnp.zeros((HEAD_DIM, TOK), F32)
                for m in range(n):
                    o = slot_ref[m]
                    s = key_scores(kv_ref[o, 0], q, diag_ref[i] if m == n - 1 else None)
                    p = jnp.exp2(s - lse)
                    ds = (p * (dot_nt(kv_ref[o, 1], g) - delta)).astype(BF16)
                    acc_ref[o, 1] += dot_nn(p.astype(BF16), g)
                    acc_ref[o, 0] += dot_nn(ds, q)
                    dqt = dqt + dot_nn(kt_ref[o], ds)
                dq_ref[b] = (dqt * SCALE).T.astype(BF16)

    pl.loop(0, NY)(lambda b: one_block(qa_ref, dqa_ref, b, b))
    pl.loop(0, NY)(lambda b: one_block(qb_ref, dqb_ref, b, b + NY))
    for o in range(NX):
        dkv_ref[o, 0] = (acc_ref[o, 0] * SCALE).astype(BF16)
        dkv_ref[o, 1] = acc_ref[o, 1].astype(BF16)


def soft_backward(count, diag, slot, qa, qb, kv, stats):
    tiles = 2 * NY * NX * HEADS
    rows = pl.BlockSpec((NY, TOK, HEAD_DIM), lambda h, *_: (0, 0, h))
    pair = pl.BlockSpec((NY, 2, TOK, HEAD_DIM), lambda h, *_: (0, 0, 0, h))
    return pl.pallas_call(
        backward_kernel,
        grid_spec=pltpu.PrefetchScalarGridSpec(
            num_scalar_prefetch=3,
            grid=(HEADS,),
            in_specs=[pair, pair, pair, pl.BlockSpec((1, 4 * NY, TOK), lambda h, *_: (h, 0, 0))],
            out_specs=[rows, rows, pair],
            scratch_shapes=[
                pltpu.VMEM((NX, HEAD_DIM, TOK), BF16),
                pltpu.VMEM((NX, 2, TOK, HEAD_DIM), F32),
            ],
        ),
        out_shape=[
            jax.ShapeDtypeStruct((NY, TOK, HEADS * HEAD_DIM), BF16),
            jax.ShapeDtypeStruct((NY, TOK, HEADS * HEAD_DIM), BF16),
            jax.ShapeDtypeStruct((NX, 2, TOK, HEADS * HEAD_DIM), BF16),
        ],
        cost_estimate=pl.CostEstimate(
            flops=tiles * 10 * TOK * TOK * HEAD_DIM,
            transcendentals=tiles * TOK * TOK,
            bytes_accessed=10 * 2**20,
        ),
        compiler_params=pltpu.CompilerParams(vmem_limit_bytes=40 * 2**20),
        name="soft_backward",
    )(count, diag, slot, qa, qb, kv, stats)


def merge(lse_a, delta_a, lse_b, delta_b):
    top = jnp.maximum(lse_a, lse_b)
    weight_a, weight_b = jnp.exp2(lse_a - top), jnp.exp2(lse_b - top)
    total = weight_a + weight_b
    return top + jnp.log2(total), (weight_a * delta_a + weight_b * delta_b) / total


def softmax_core(group_of, soft_query, soft_key, soft_value, soft_grad):
    x, y, c = (lax.axis_index(a) for a in ("x", "y", "c"))
    kv_own = jnp.stack([soft_key, soft_value])
    qg_own = jnp.stack([soft_query, soft_grad])
    kv_from, qg_from = {0: kv_own}, {0: qg_own}
    for o in (1, 3, 2):
        qg_from[o] = fetch(qg_own, "y", NY, o)
        kv_from[o] = fetch(kv_own, "x", NX, o)
    qa = jnp.stack([qg_from[o] for o in range(NY)])
    kv = jnp.stack([kv_from[o] for o in range(NX)])
    qb = fetch(qa, "c", NC, 1)

    def position(xi, yi, ci):
        return group_of[(xi % NX) * (NY * NC) + (yi % NY) * NC + ci % NC]

    offsets = jnp.arange(NX, dtype=jnp.int32)
    key_pos = position(x + offsets, y, c)
    query_pos = jnp.concatenate([position(x, y + offsets, c), position(x, y + offsets, c + 1)])
    count = jnp.sum((key_pos[None] <= query_pos[:, None]).astype(jnp.int32), axis=1)
    diag = jnp.sum((key_pos[None] == query_pos[:, None]).astype(jnp.int32), axis=1)
    rank = jnp.sum((key_pos[None] < key_pos[:, None]).astype(jnp.int32), axis=1)
    slot = jnp.sum(jnp.where(rank[None] == offsets[:, None], offsets[None], 0), axis=1)

    out_a, stat_a = soft_forward(count[:NY], diag[:NY], slot, qa, kv)
    out_b, stat_b = soft_forward(count[NY:], diag[NY:], slot, qb, kv)

    part = jnp.stack([stat_a, stat_b]).reshape(2, HEADS, NY, 2, TOK)
    lse_part, delta_part = part[:, :, :, 0], part[:, :, :, 1]
    other = fetch(jnp.stack([stat_b, stat_a]), "c", NC, 1).reshape(2, HEADS, NY, 2, TOK)
    lse, delta = merge(lse_part, delta_part, other[:, :, :, 0], other[:, :, :, 1])
    chip = jnp.stack([lse, delta])
    received = {o: fetch(chip, "y", NY, o) for o in (1, 3, 2)}
    for o in (1, 3, 2):
        turned = jnp.roll(received[o], o, axis=3)
        lse, delta = merge(lse, delta, turned[0], turned[1])
    stats = jnp.stack([lse, delta], axis=3)
    stats = stats.transpose(1, 0, 2, 3, 4).reshape(HEADS, 4 * NY, TOK)

    weight = jnp.exp2(lse_part - lse).transpose(0, 2, 1, 3)[:, :, :, None, :]
    mine = weight[0] * out_a.astype(F32)
    theirs = (weight[1] * out_b.astype(F32)).astype(BF16)
    chip_out = (mine + fetch(theirs, "c", NC, 1).astype(F32)).astype(BF16)
    out_sum = chip_out[0].astype(F32)
    for o in (1, 3, 2):
        out_sum = out_sum + send(chip_out[o], "y", NY, o).astype(F32)
    soft_out = out_sum.transpose(2, 0, 1).reshape(TOK, HEADS * HEAD_DIM).astype(BF16)

    dq_a, dq_b, dkv = soft_backward(count, diag, slot, qa, qb, kv, stats)
    chip_dq = (dq_a.astype(F32) + fetch(dq_b, "c", NC, 1).astype(F32)).astype(BF16)
    dkv_sum, dq_sum = dkv[0].astype(F32), chip_dq[0].astype(F32)
    for o in (1, 3, 2):
        dkv_sum = dkv_sum + send(dkv[o], "x", NX, o).astype(F32)
    for o in (1, 3, 2):
        dq_sum = dq_sum + send(chip_dq[o], "y", NY, o).astype(F32)
    return soft_out, dq_sum.astype(BF16), dkv_sum[0].astype(BF16), dkv_sum[1].astype(BF16)


SEQ = ("x", "y", "c")


def chain_weights(device_groups, own_group, group_logs, forward):
    if forward:
        source_mask = device_groups < own_group
        between = (device_groups[:, None] < device_groups[None, :]) & (
            device_groups[None, :] < own_group
        )
    else:
        source_mask = device_groups > own_group
        between = (device_groups[:, None] > device_groups[None, :]) & (
            device_groups[None, :] > own_group
        )
    exponent = jnp.sum(jnp.where(between[:, :, None], group_logs[None], 0.0), axis=1)
    return jnp.where(source_mask[:, None], jnp.exp(exponent), 0.0)


def linear_core(group_of, lin_query, lin_key, lin_value, log_decay, lin_grad):
    tok_rows, feat_width = lin_query.shape
    own_group = group_of[lax.axis_index(SEQ)]
    row_index = jnp.arange(tok_rows, dtype=jnp.int32)

    def mm(spec, a, b):
        return jnp.einsum(spec, a.astype(BF16), b.astype(BF16), preferred_element_type=F32)

    def heads_first(matrix):
        return matrix.reshape(tok_rows, HEADS, HEAD_DIM).transpose(1, 0, 2)

    def rows_first(stacked):
        return stacked.transpose(1, 0, 2).reshape(tok_rows, feat_width)

    queries, keys, values = heads_first(lin_query), heads_first(lin_key), heads_first(lin_value)
    cumulative = jnp.cumsum(log_decay, axis=0).T
    group_log = cumulative[:, -1]
    lower_mask = (row_index[:, None] >= row_index[None, :])[None]
    log_gap = cumulative[:, :, None] - cumulative[:, None, :]
    inner_decay = jnp.where(lower_mask, jnp.exp(jnp.where(lower_mask, log_gap, 0.0)), 0.0)
    tail_decay = jnp.exp(group_log[:, None] - cumulative)[:, :, None]
    head_decay = jnp.exp(cumulative)[:, :, None]
    local_state = mm("hsd,hse->hde", keys.astype(F32) * tail_decay, values)
    logs_all = lax.all_gather(group_log[None], SEQ, axis=0, tiled=True)
    states_all = lax.all_gather(
        local_state.astype(BF16).reshape(1, HEADS, HEAD_DIM * HEAD_DIM), SEQ, axis=0, tiled=True
    )
    inner_scores = mm("htd,hsd->hts", queries, keys) * inner_decay
    local_out = mm("hts,hsd->htd", inner_scores, values)
    weight = chain_weights(group_of, own_group, logs_all, True)
    entry = jnp.sum(weight[:, :, None] * states_all.astype(F32), axis=0)
    entry = entry.reshape(HEADS, HEAD_DIM, HEAD_DIM)
    raw = rows_first(local_out + head_decay * mm("htd,hde->hte", queries, entry))
    upstream = lin_grad.astype(F32)
    sums = lax.psum(
        jnp.stack([jnp.sum(raw * raw, axis=1), jnp.sum(upstream * raw, axis=1)]), "head"
    )
    inv_rms = 1.0 / jnp.sqrt(sums[0] / (HEAD_TOTAL * HEAD_DIM) + EPS)
    lin_out = raw * inv_rms[:, None]
    aligned = sums[1] * inv_rms / (HEAD_TOTAL * HEAD_DIM)
    raw_grad = heads_first((upstream - lin_out * aligned[:, None]) * inv_rms[:, None])
    read_grad = mm("htd,hte->hde", queries.astype(F32) * head_decay, raw_grad)
    grads_all = lax.all_gather(
        read_grad.astype(BF16).reshape(1, HEADS, HEAD_DIM * HEAD_DIM), SEQ, axis=0, tiled=True
    )
    value_local = mm("hts,htd->hsd", inner_scores, raw_grad)
    inner_grad = mm("htd,hsd->hts", raw_grad, values) * inner_decay
    lin_dq = mm("hts,hsd->htd", inner_grad, keys)
    lin_dq = lin_dq + head_decay * mm("hte,hde->htd", raw_grad, entry)
    key_local = mm("hts,htd->hsd", inner_grad, queries)
    weight_back = chain_weights(group_of, own_group, logs_all, False)
    leave = jnp.sum(weight_back[:, :, None] * grads_all.astype(F32), axis=0)
    leave = leave.reshape(HEADS, HEAD_DIM, HEAD_DIM)
    lin_dk = key_local + tail_decay * mm("hde,hse->hsd", leave, values)
    lin_dv = value_local + tail_decay * mm("hde,hsd->hse", leave, keys)
    return lin_out, rows_first(lin_dq), rows_first(lin_dk), rows_first(lin_dv)


def on_device(
    group_of, soft_query, soft_key, soft_value, soft_grad,
    lin_query, lin_key, lin_value, log_decay, lin_grad,
):
    soft = softmax_core(group_of, soft_query, soft_key, soft_value, soft_grad)
    lin = linear_core(group_of, lin_query, lin_key, lin_value, log_decay, lin_grad)
    return (*soft, *lin)


def solution(mesh):
    grid = Mesh(mesh.devices.reshape(NX, NY, NC, mesh.shape["head"]), (*SEQ, "head"))
    block = P(SEQ, "head")
    return jax.shard_map(
        on_device,
        mesh=grid,
        in_specs=(P(),) + (block,) * 9,
        out_specs=(block,) * 8,
        check_vma=False,
    )
```

```python
import jax
import jax.numpy as jnp
from jax import lax
from jax.experimental import pallas as pl
from jax.experimental.pallas import tpu as pltpu
from jax.sharding import Mesh
from jax.sharding import PartitionSpec as P

HEAD_TOTAL = 12
HEAD_DIM = 128
HEADS = 3
WIDTH = HEADS * HEAD_DIM
TOK = 256
NX, NY, NC, NZ = 4, 4, 2, 4
LINE = NY * NC
EPS = 1e-06
SCALE = HEAD_DIM ** (-0.5)
LOG2E = 1.4426950408889634
NEG = -1e30
F32 = jnp.float32
BF16 = jnp.bfloat16
HIGHEST = lax.Precision.HIGHEST
SEQ = ("x", "y", "c")
STATE_ROW = 2 * TOK
LOG_ROW = STATE_ROW + HEAD_DIM
PACK_ROWS = LOG_ROW + 16


def send(block, axis, size, offset):
    return lax.ppermute(block, axis, [(i, (i + offset) % size) for i in range(size)])


def fetch(block, axis, size, offset):
    return send(block, axis, size, -offset)


def dot(a, b, dim_a, dim_b, precision=None):
    return lax.dot_general(
        a, b, (((dim_a,), (dim_b,)), ((), ())), precision=precision, preferred_element_type=F32
    )


def head_cols(h):
    return pl.ds(h * HEAD_DIM, HEAD_DIM)


def call(kernel, name, out_shape, flops, args, **kwargs):
    return pl.pallas_call(
        kernel,
        out_shape=out_shape,
        cost_estimate=pl.CostEstimate(
            flops=flops, transcendentals=2**18, bytes_accessed=2 * 2**20
        ),
        compiler_params=pltpu.CompilerParams(vmem_limit_bytes=40 * 2**20),
        name=name,
        **kwargs,
    )(*args)


def key_scores(k, q, diagonal=None):
    s = dot(k, q, 1, 1) * (SCALE * LOG2E)
    if diagonal is not None:
        key_row = lax.broadcasted_iota(jnp.int32, s.shape, 0)
        query_col = lax.broadcasted_iota(jnp.int32, s.shape, 1)
        limit = jnp.where(diagonal > 0, 0, TOK)
        s = jnp.where(key_row <= query_col + limit, s, NEG)
    return s


def forward_kernel(count_ref, diag_ref, slot_ref, qg_ref, kv_ref, out_ref, stat_ref, vt_ref):
    h = pl.program_id(0)
    for o in range(NX):
        vt_ref[o] = kv_ref[o, 1].T

    @pl.when(h == 0)
    def _():
        stat_ref[...] = jnp.zeros_like(stat_ref)

    @pl.loop(0, NY)
    def _(i):
        count = count_ref[i]

        @pl.when(count == 0)
        def _():
            out_ref[i] = jnp.zeros((TOK, HEAD_DIM), BF16)
            stat_ref[i, pl.ds(h, 1)] = jnp.full((1, TOK), NEG, F32)
            stat_ref[i, pl.ds(h + 4, 1)] = jnp.zeros((1, TOK), F32)

        for n in range(1, NX + 1):

            @pl.when(count == n)
            def _():
                q = qg_ref[i, :TOK]
                parts = [
                    key_scores(kv_ref[slot_ref[m], 0], q, diag_ref[i] if m == n - 1 else None)
                    for m in range(n)
                ]
                top = jnp.max(parts[0], axis=0, keepdims=True)
                for s in parts[1:]:
                    top = jnp.maximum(top, jnp.max(s, axis=0, keepdims=True))
                total = jnp.zeros((1, TOK), F32)
                acc = jnp.zeros((HEAD_DIM, TOK), F32)
                for m in range(n):
                    p = jnp.exp2(parts[m] - top)
                    total = total + jnp.sum(p, axis=0, keepdims=True)
                    acc = acc + dot(vt_ref[slot_ref[m]], p.astype(BF16), 1, 0)
                acc = acc / total
                out_ref[i] = acc.T.astype(BF16)
                grad = qg_ref[i, TOK:].astype(F32).T
                stat_ref[i, pl.ds(h, 1)] = top + jnp.log(total) * LOG2E
                stat_ref[i, pl.ds(h + 4, 1)] = jnp.sum(acc * grad, axis=0, keepdims=True)


def soft_forward(count, diag, slot, qg, kv):
    tiles = NY * NX * HEADS
    return call(
        forward_kernel,
        "soft_forward",
        [
            jax.ShapeDtypeStruct((NY, TOK, WIDTH), BF16),
            jax.ShapeDtypeStruct((NY, 8, TOK), F32),
        ],
        tiles * 4 * TOK * TOK * HEAD_DIM,
        (count, diag, slot, qg, kv),
        grid_spec=pltpu.PrefetchScalarGridSpec(
            num_scalar_prefetch=3,
            grid=(HEADS,),
            in_specs=[
                pl.BlockSpec((NY, 2 * TOK, HEAD_DIM), lambda h, *_: (0, 0, h)),
                pl.BlockSpec((NX, 2, TOK, HEAD_DIM), lambda h, *_: (0, 0, 0, h)),
            ],
            out_specs=[
                pl.BlockSpec((NY, TOK, HEAD_DIM), lambda h, *_: (0, 0, h)),
                pl.BlockSpec((NY, 8, TOK), lambda h, *_: (0, 0, 0)),
            ],
            scratch_shapes=[pltpu.VMEM((NX, HEAD_DIM, TOK), BF16)],
        ),
    )


def tile_backward(k, v, kt, q, g, lse, delta, diagonal=None):
    p = jnp.exp2(key_scores(k, q, diagonal) - lse)
    ds = (p * (dot(v, g, 1, 1) - delta)).astype(BF16)
    return dot(ds, q, 1, 0), dot(p.astype(BF16), g, 1, 0), dot(kt, ds, 1, 0)


def far_kernel(
    count_ref, slot_ref, qa_ref, qb_ref, kv_ref, stat_ref,
    dqa_ref, dqb_ref, dkv_ref, kt_ref, acc_ref,
):
    h = pl.program_id(0)
    for o in range(1, NX):
        kt_ref[o] = kv_ref[o, 0].T
    acc_ref[...] = jnp.zeros_like(acc_ref)

    def one_block(qg_ref, dq_ref, side, b):
        count = count_ref[side * NY + b]

        @pl.when(count == 0)
        def _():
            dq_ref[b] = jnp.zeros((TOK, HEAD_DIM), F32)

        for n in range(1, NX):

            @pl.when(count == n)
            def _():
                q = qg_ref[b, :TOK]
                g = qg_ref[b, TOK:]
                lse = stat_ref[side, b, pl.ds(h, 1)]
                delta = stat_ref[side, b, pl.ds(h + 4, 1)]
                dqt = jnp.zeros((HEAD_DIM, TOK), F32)
                for m in range(n):
                    o = slot_ref[m]
                    dk, dv, dq = tile_backward(
                        kv_ref[o, 0], kv_ref[o, 1], kt_ref[o], q, g, lse, delta
                    )
                    acc_ref[o, 0] += dk
                    acc_ref[o, 1] += dv
                    dqt = dqt + dq
                dq_ref[b] = dqt.T

    pl.loop(0, NY)(lambda b: one_block(qa_ref, dqa_ref, 0, b))
    pl.loop(0, NY)(lambda b: one_block(qb_ref, dqb_ref, 1, b))
    for o in range(1, NX):
        dkv_ref[o - 1, 0] = (acc_ref[o, 0] * SCALE).astype(BF16)
        dkv_ref[o - 1, 1] = acc_ref[o, 1].astype(BF16)


def near_kernel(
    count_ref, diag_ref, qa_ref, qb_ref, kv_ref, stat_ref, dqa_in, dqb_in,
    dqa_ref, dqb_ref, dkv_ref, kt_ref,
):
    h = pl.program_id(0)
    kt_ref[...] = kv_ref[0, 0].T
    dkv_ref[...] = jnp.zeros_like(dkv_ref)

    def one_block(qg_ref, dq_in, dq_ref, side, b):
        i = side * NY + b

        @pl.when(count_ref[i] == 0)
        def _():
            dq_ref[b] = (dq_in[b] * SCALE).astype(BF16)

        @pl.when(count_ref[i] > 0)
        def _():
            lse = stat_ref[side, b, pl.ds(h, 1)]
            delta = stat_ref[side, b, pl.ds(h + 4, 1)]
            dk, dv, dq = tile_backward(
                kv_ref[0, 0], kv_ref[0, 1], kt_ref[...], qg_ref[b, :TOK], qg_ref[b, TOK:],
                lse, delta, diag_ref[i],
            )
            dkv_ref[0] += dk * SCALE
            dkv_ref[1] += dv
            dq_ref[b] = ((dq_in[b] + dq.T) * SCALE).astype(BF16)

    pl.loop(0, NY)(lambda b: one_block(qa_ref, dqa_in, dqa_ref, 0, b))
    pl.loop(0, NY)(lambda b: one_block(qb_ref, dqb_in, dqb_ref, 1, b))


ROWS_SPEC = pl.BlockSpec((NY, TOK, HEAD_DIM), lambda h, *_: (0, 0, h))
QG_SPEC = pl.BlockSpec((NY, 2 * TOK, HEAD_DIM), lambda h, *_: (0, 0, h))
STAT_SPEC = pl.BlockSpec((2, NY, 8, TOK), lambda h, *_: (0, 0, 0, 0))


def pair_spec(n):
    return pl.BlockSpec((n, 2, TOK, HEAD_DIM), lambda h, *_: (0, 0, 0, h))


def far_backward(count, slot, qa, qb, kv, stats):
    return call(
        far_kernel,
        "far_backward",
        [
            jax.ShapeDtypeStruct((NY, TOK, WIDTH), F32),
            jax.ShapeDtypeStruct((NY, TOK, WIDTH), F32),
            jax.ShapeDtypeStruct((NX - 1, 2, TOK, WIDTH), BF16),
        ],
        2 * NY * (NX - 1) * HEADS * 10 * TOK * TOK * HEAD_DIM,
        (count, slot, qa, qb, kv, stats),
        grid_spec=pltpu.PrefetchScalarGridSpec(
            num_scalar_prefetch=2,
            grid=(HEADS,),
            in_specs=[QG_SPEC, QG_SPEC, pair_spec(NX), STAT_SPEC],
            out_specs=[ROWS_SPEC, ROWS_SPEC, pair_spec(NX - 1)],
            scratch_shapes=[
                pltpu.VMEM((NX, HEAD_DIM, TOK), BF16),
                pltpu.VMEM((NX, 2, TOK, HEAD_DIM), F32),
            ],
        ),
    )


def near_backward(count, diag, qa, qb, kv, stats, dqa, dqb):
    return call(
        near_kernel,
        "near_backward",
        [
            jax.ShapeDtypeStruct((NY, TOK, WIDTH), BF16),
            jax.ShapeDtypeStruct((NY, TOK, WIDTH), BF16),
            jax.ShapeDtypeStruct((2, TOK, WIDTH), F32),
        ],
        2 * NY * HEADS * 10 * TOK * TOK * HEAD_DIM,
        (count, diag, qa, qb, kv, stats, dqa, dqb),
        grid_spec=pltpu.PrefetchScalarGridSpec(
            num_scalar_prefetch=2,
            grid=(HEADS,),
            in_specs=[QG_SPEC, QG_SPEC, pair_spec(1), STAT_SPEC, ROWS_SPEC, ROWS_SPEC],
            out_specs=[
                ROWS_SPEC,
                ROWS_SPEC,
                pl.BlockSpec((2, TOK, HEAD_DIM), lambda h, *_: (0, 0, h)),
            ],
            scratch_shapes=[pltpu.VMEM((HEAD_DIM, TOK), BF16)],
        ),
    )


def merged(stats_a, stats_b):
    lse_a, lse_b = stats_a[..., :4, :], stats_b[..., :4, :]
    top = jnp.maximum(lse_a, lse_b)
    weight_a, weight_b = jnp.exp2(lse_a - top), jnp.exp2(lse_b - top)
    total = weight_a + weight_b
    delta = (weight_a * stats_a[..., 4:, :] + weight_b * stats_b[..., 4:, :]) / total
    return jnp.concatenate([top + jnp.log(total) * LOG2E, delta], axis=-2)


def chip_kernel(stat_a_ref, stat_b_ref, other_ref, out_ref):
    out_ref[0] = merged(stat_a_ref[...], other_ref[0])
    out_ref[1] = merged(stat_b_ref[...], other_ref[1])


def line_kernel(
    stat_a_ref, stat_b_ref, chip_ref, from_1, from_2, from_3, out_a_ref, out_b_ref, read_ref,
    stat_ref, mine_ref, theirs_ref,
):
    for side in range(2):
        own_ref, o_ref = (stat_a_ref, out_a_ref) if side == 0 else (stat_b_ref, out_b_ref)
        for i in range(NY):
            stats = chip_ref[side, i]
            for o, other in ((1, from_1), (2, from_2), (3, from_3)):
                stats = merged(stats, other[side, (i - o) % NY])
            stat_ref[side, i] = stats
            weight = jnp.exp2(own_ref[i, :4] - stats[:4])
            weight = jnp.concatenate([weight] * (HEAD_DIM // 4), axis=0).T
            for h in range(HEADS):
                scaled = o_ref[i, :, head_cols(h)].astype(F32) * weight[:, h : h + 1]
                if side == 0:
                    mine_ref[i, :, head_cols(h)] = scaled
                else:
                    theirs_ref[pl.ds(i * TOK, TOK), head_cols(h)] = scaled.astype(BF16)
    theirs_ref[pl.ds(NY * TOK, HEAD_DIM)] = read_ref[...]


def triangle(upper):
    row = lax.broadcasted_iota(jnp.int32, (TOK, TOK), 0)
    col = lax.broadcasted_iota(jnp.int32, (TOK, TOK), 1)
    return row <= col if upper else row >= col


def decay_columns(decay_ref):
    return dot(triangle(False).astype(F32), decay_ref[...], 1, 0, HIGHEST)


def pack_kernel(q_ref, g_ref, key_ref, value_ref, decay_ref, out_ref):
    cumulative = decay_columns(decay_ref)
    total = cumulative[TOK - 1 : TOK]
    tail = jnp.exp(total - cumulative)
    out_ref[pl.ds(0, TOK)] = q_ref[...]
    out_ref[pl.ds(TOK, TOK)] = g_ref[...]
    row = lax.broadcasted_iota(jnp.int32, (16, HEAD_DIM), 0)
    for h in range(HEADS):
        keys = key_ref[:, head_cols(h)].astype(F32) * tail[:, h : h + 1]
        state = dot(keys.astype(BF16), value_ref[:, head_cols(h)], 0, 0)
        out_ref[pl.ds(STATE_ROW, HEAD_DIM), head_cols(h)] = state.astype(BF16)
        log = jnp.broadcast_to(total[:, h : h + 1], (16, HEAD_DIM))
        high = log.astype(BF16).astype(F32)
        middle = (log - high).astype(BF16).astype(F32)
        low = log - high - middle
        piece = jnp.where(row == 0, high, jnp.where(row == 1, middle, jnp.where(row == 2, low, 0.0)))
        out_ref[pl.ds(LOG_ROW, 16), head_cols(h)] = piece.astype(BF16)


def inner_terms(q, k, decay_ref, cumulative, h):
    keep = triangle(False)
    rows = dot(decay_ref[...], triangle(True).astype(F32), 0, 0, HIGHEST)
    gap = cumulative[:, h : h + 1] - rows[h : h + 1]
    decay = jnp.where(keep, jnp.exp(jnp.minimum(gap, 0.0)), 0.0)
    return decay, (dot(q, k, 1, 1) * decay).astype(BF16)


def read_kernel(q_ref, k_ref, v_ref, g_ref, decay_ref, entry_ref, raw_ref, sum_ref):
    cumulative = decay_columns(decay_ref)
    squares = jnp.zeros((TOK, 1), F32)
    inner = jnp.zeros((TOK, 1), F32)
    for h in range(HEADS):
        cols = head_cols(h)
        q = q_ref[:, cols]
        scores = inner_terms(q, k_ref[:, cols], decay_ref, cumulative, h)[1]
        carried = dot(q, entry_ref[:, cols].astype(BF16), 1, 0)
        raw = dot(scores, v_ref[:, cols], 1, 0) + jnp.exp(cumulative[:, h : h + 1]) * carried
        raw_ref[:, cols] = raw
        squares = squares + jnp.sum(raw * raw, axis=1, keepdims=True)
        inner = inner + jnp.sum(raw * g_ref[:, cols].astype(F32), axis=1, keepdims=True)
    lane = lax.broadcasted_iota(jnp.int32, (TOK, HEAD_DIM), 1)
    sums = jnp.where(lane == 0, squares, jnp.where(lane == 1, inner, 0.0))
    sum_ref[...] = sums.T[:8]


def grad_kernel(
    q_ref, k_ref, v_ref, g_ref, decay_ref, entry_ref, raw_ref, sum_0, sum_1, sum_2, sum_3,
    out_ref, dq_ref, dk_ref, dv_ref, read_ref,
):
    cumulative = decay_columns(decay_ref)
    sums = (sum_0[...] + sum_1[...]) + (sum_2[...] + sum_3[...])
    sums = jnp.concatenate([sums] * (HEAD_DIM // 8), axis=0).T
    inverse = 1.0 / jnp.sqrt(sums[:, 0:1] * (1.0 / (HEAD_TOTAL * HEAD_DIM)) + EPS)
    aligned = sums[:, 1:2] * inverse * (1.0 / (HEAD_TOTAL * HEAD_DIM))
    for h in range(HEADS):
        cols = head_cols(h)
        q, k = q_ref[:, cols], k_ref[:, cols]
        out = raw_ref[:, cols] * inverse
        out_ref[:, cols] = out
        raw_grad = ((g_ref[:, cols].astype(F32) - out * aligned) * inverse).astype(BF16)
        decay, scores = inner_terms(q, k, decay_ref, cumulative, h)
        head_decay = jnp.exp(cumulative[:, h : h + 1])
        inner_grad = (dot(raw_grad, v_ref[:, cols], 1, 1) * decay).astype(BF16)
        carried = dot(raw_grad, entry_ref[:, cols].astype(BF16), 1, 1)
        dq_ref[:, cols] = dot(inner_grad, k, 1, 0) + head_decay * carried
        dk_ref[:, cols] = dot(inner_grad, q, 0, 0)
        dv_ref[:, cols] = dot(scores, raw_grad, 0, 0)
        scaled = (q.astype(F32) * head_decay).astype(BF16)
        read_ref[:, cols] = dot(scaled, raw_grad, 0, 0).astype(BF16)


def write_kernel(k_ref, v_ref, decay_ref, leave_ref, dk_in, dv_in, dk_ref, dv_ref):
    cumulative = decay_columns(decay_ref)
    tail = jnp.exp(cumulative[TOK - 1 : TOK] - cumulative)
    for h in range(HEADS):
        cols = head_cols(h)
        leave = leave_ref[:, cols].astype(BF16)
        scale = tail[:, h : h + 1]
        dk_ref[:, cols] = dk_in[:, cols] + scale * dot(v_ref[:, cols], leave, 1, 1)
        dv_ref[:, cols] = dv_in[:, cols] + scale * dot(k_ref[:, cols], leave, 1, 0)


def masked_decay(mask, exponents):
    return jnp.where(mask, jnp.exp(jnp.where(mask, exponents, 0.0)), 0.0)


def chain(key, line_key, logs):
    wraps = jnp.max(key) - jnp.min(key) > LINE - 1
    early = key < LINE
    handed = jnp.where(wraps, early, True)
    same = jnp.where(wraps, early == early[0], True)
    before = same & (key < key[0])
    after = key[None, :] > key[:, None]

    def weights(members):
        exponents = jnp.sum(jnp.where((after & members)[:, :, None], logs[None], 0.0), axis=1)
        return masked_decay(members[:, None], exponents)

    own_start = jnp.min(jnp.where(same, key, 32))
    starts = jnp.min(line_key, axis=1)
    prefix = jnp.sum(jnp.where(before[:, None], logs, 0.0), axis=0)

    def line_weights(line_logs):
        earlier = starts < own_start
        between = (starts[None, :] > starts[:, None]) & earlier[None, :]
        exponents = jnp.sum(jnp.where(between[:, :, None], line_logs[None], 0.0), axis=1)
        return masked_decay(earlier[:, None], exponents + prefix[None])

    return weights(before), weights(handed), line_weights


def by_columns(weights):
    return jnp.repeat(weights, HEAD_DIM, axis=-1)[:, None, :]


def weighted(weights, blocks):
    return jnp.sum(by_columns(weights) * blocks.astype(F32), axis=0)


def on_device(
    group_of, soft_query, soft_key, soft_value, soft_grad,
    lin_query, lin_key, lin_value, log_decay, lin_grad,
):
    x, y, c = (lax.axis_index(a) for a in SEQ)
    offsets = (1, 3, 2)

    steps = jnp.arange(NX, dtype=jnp.int32)
    table = group_of.reshape(NX, NY, NC)
    lines = jnp.roll(jnp.roll(jnp.roll(table, -x, 0), -y, 1), -c, 2).transpose(0, 2, 1)
    key_pos, query_pos = lines[:, 0, 0], lines[0].reshape(LINE)
    line_pos = lines.reshape(NX, LINE)
    seen = (key_pos[None] <= query_pos[:, None]).astype(jnp.int32)
    count = jnp.sum(seen, axis=1)
    near_count = seen[:, 0]
    far_count = count - near_count
    diag = (query_pos == key_pos[0]).astype(jnp.int32)

    def sorted_slots(mask):
        ahead = mask[None] & (key_pos[None] < key_pos[:, None])
        rank = jnp.where(mask, jnp.sum(ahead.astype(jnp.int32), axis=1), NX)
        return jnp.sum(jnp.where(rank[None] == steps[:, None], steps[None], 0), axis=1)

    slot, far_slot = sorted_slots(steps >= 0), sorted_slots(steps >= 1)

    kv_own = jnp.stack([soft_key, soft_value])
    kv_from = {0: kv_own, **{o: fetch(kv_own, "x", NX, o) for o in offsets}}
    packed = call(
        pack_kernel,
        "pack",
        jax.ShapeDtypeStruct((PACK_ROWS, WIDTH), BF16),
        2**26,
        (soft_query, soft_grad, lin_key, lin_value, log_decay),
    )
    qg_from = {0: packed, **{o: fetch(packed, "y", NY, o) for o in offsets}}
    qa = jnp.stack([qg_from[o] for o in range(NY)])
    qb = fetch(qa, "c", NC, 1)
    kv = jnp.stack([kv_from[o] for o in range(NX)])

    def line_logs(q):
        return jnp.sum(q[:, LOG_ROW : LOG_ROW + 3, ::HEAD_DIM].astype(F32), axis=1)

    logs = jnp.concatenate([line_logs(qa), line_logs(qb)])
    own_w, handed_w, entry_line_w = chain(query_pos, line_pos, logs)
    back_own_w, back_handed_w, leave_line_w = chain(31 - query_pos, 31 - line_pos, logs)
    states_a, states_b = qa[:, STATE_ROW:LOG_ROW], qb[:, STATE_ROW:LOG_ROW]
    handed = weighted(handed_w[:NY], states_a) + weighted(handed_w[NY:], states_b)
    entry = weighted(own_w[:NY], states_a) + weighted(own_w[NY:], states_b)
    log_row = jnp.repeat(jnp.sum(logs, axis=0), HEAD_DIM)[None]
    handed = jnp.concatenate([handed, jnp.broadcast_to(log_row, (8, WIDTH))])
    totals = jnp.stack([handed, *(fetch(handed, "x", NX, o) for o in (1, 2, 3))])
    all_logs = totals[:, HEAD_DIM, ::HEAD_DIM]
    entry = entry + weighted(entry_line_w(all_logs), totals[:, :HEAD_DIM])

    out_a, stat_a = soft_forward(count[:NY], diag[:NY], slot, qa, kv)
    out_b, stat_b = soft_forward(count[NY:], diag[NY:], slot, qb, kv)

    rows_f32 = jax.ShapeDtypeStruct((TOK, WIDTH), F32)
    raw, sums = call(
        read_kernel,
        "lin_read",
        [rows_f32, jax.ShapeDtypeStruct((8, TOK), F32)],
        2**27,
        (lin_query, lin_key, lin_value, lin_grad, log_decay, entry),
    )
    all_sums = [sums, *(fetch(sums, "head", NZ, o) for o in (1, 2, 3))]
    lin_out, lin_dq, dk_local, dv_local, read_grad = call(
        grad_kernel,
        "lin_grad",
        [rows_f32] * 4 + [jax.ShapeDtypeStruct((HEAD_DIM, WIDTH), BF16)],
        2**28,
        (lin_query, lin_key, lin_value, lin_grad, log_decay, entry, raw, *all_sums),
    )

    stat_shape = jax.ShapeDtypeStruct((2, NY, 8, TOK), F32)
    other = fetch(jnp.stack([stat_b, stat_a]), "c", NC, 1)
    chip_stat = call(chip_kernel, "chip_stats", stat_shape, 2**20, (stat_a, stat_b, other))
    received = {o: fetch(chip_stat, "y", NY, o) for o in offsets}
    stats, mine, theirs = call(
        line_kernel,
        "line_stats",
        [
            stat_shape,
            jax.ShapeDtypeStruct((NY, TOK, WIDTH), F32),
            jax.ShapeDtypeStruct((NY * TOK + HEAD_DIM, WIDTH), BF16),
        ],
        2**22,
        (stat_a, stat_b, chip_stat, received[1], received[2], received[3], out_a, out_b, read_grad),
    )

    from_core = fetch(theirs, "c", NC, 1)
    dq_a, dq_b, far_dkv = far_backward(far_count, far_slot, qa, qb, kv, stats)
    chip_out = mine + from_core[: NY * TOK].reshape(NY, TOK, WIDTH).astype(F32)
    read_pair = jnp.concatenate([read_grad, from_core[NY * TOK :]])
    sent_out = {
        o: send(jnp.concatenate([chip_out[o].astype(BF16), read_pair]), "y", NY, o)
        for o in offsets
    }
    sent_dkv = [send(far_dkv[o - 1], "x", NX, o) for o in offsets]
    dq_a, dq_b, near_dkv = near_backward(near_count, diag, qa, qb, kv, stats, dq_a, dq_b)

    soft_out = chip_out[0]
    for o in offsets:
        soft_out = soft_out + sent_out[o][:TOK].astype(F32)
    reads = [read_pair] + [sent_out[NY - o][TOK:] for o in (1, 2, 3)]
    reads = jnp.stack([r[:HEAD_DIM] for r in reads] + [r[HEAD_DIM:] for r in reads])
    back_handed = weighted(back_handed_w, reads)
    leave = weighted(back_own_w, reads)
    back_totals = jnp.stack([back_handed, *(fetch(back_handed, "x", NX, o) for o in (1, 2, 3))])
    leave = leave + weighted(leave_line_w(all_logs), back_totals)
    lin_dk, lin_dv = call(
        write_kernel,
        "lin_write",
        [rows_f32, rows_f32],
        2**26,
        (lin_key, lin_value, log_decay, leave, dk_local, dv_local),
    )

    chip_dq = dq_a.astype(F32) + fetch(dq_b, "c", NC, 1).astype(F32)
    soft_dq = chip_dq[0]
    for o in offsets:
        soft_dq = soft_dq + send(chip_dq[o].astype(BF16), "y", NY, o).astype(F32)
    dkv = near_dkv
    for part in sent_dkv:
        dkv = dkv + part.astype(F32)
    return (
        soft_out.astype(BF16), soft_dq.astype(BF16), dkv[0].astype(BF16), dkv[1].astype(BF16),
        lin_out, lin_dq, lin_dk, lin_dv,
    )


def solution(mesh):
    grid = Mesh(mesh.devices.reshape(NX, NY, NC, NZ), (*SEQ, "head"))
    block = P(SEQ, "head")
    return jax.shard_map(
        on_device,
        mesh=grid,
        in_specs=(P(),) + (block,) * 9,
        out_specs=(block,) * 8,
        check_vma=False,
    )
```

```python
import functools

import jax
import jax.numpy as jnp
from jax import lax
from jax.experimental import pallas as pl
from jax.experimental.pallas import tpu as pltpu
from jax.sharding import Mesh
from jax.sharding import PartitionSpec as P


HEAD_TOTAL = 12
HEAD_DIM = 128
HEADS = 3
WIDTH = HEADS * HEAD_DIM
TOK = 256
NX, NY, NC, NZ = 4, 4, 2, 4
LINE = NY * NC
EPS = 1e-06
SCALE = HEAD_DIM ** (-0.5)
LOG2E = 1.4426950408889634
NEG = -1e30
F32 = jnp.float32
BF16 = jnp.bfloat16
HIGHEST = lax.Precision.HIGHEST
SEQ = ("x", "y", "c")
OFFSETS = (1, 3, 2)
STATE_ROW = TOK
LOG_ROW = STATE_ROW + HEAD_DIM
PACK_ROWS = LOG_ROW + 16
ANY = pl.BlockSpec(memory_space=pl.ANY)


def send(block, axis, size, offset):
    return lax.ppermute(block, axis, [(i, (i + offset) % size) for i in range(size)])


def fetch(block, axis, size, offset):
    return send(block, axis, size, -offset)


def dot(a, b, dim_a, dim_b, precision=None):
    return lax.dot_general(
        a, b, (((dim_a,), (dim_b,)), ((), ())), precision=precision, preferred_element_type=F32
    )


def head_cols(h):
    return pl.ds(h * HEAD_DIM, HEAD_DIM)


def shaped(*dims, dtype=F32):
    return jax.ShapeDtypeStruct(dims, dtype)


def call(kernel, out_shape, flops, args, vmem=40, **kwargs):
    return pl.pallas_call(
        kernel,
        out_shape=out_shape,
        cost_estimate=pl.CostEstimate(flops=flops, transcendentals=2**18, bytes_accessed=2 * 2**20),
        compiler_params=pltpu.CompilerParams(vmem_limit_bytes=vmem * 2**20),
        **kwargs,
    )(*args)


def placed(in_specs, out_specs, scratch=(), grid=()):
    return {
        "grid_spec": pltpu.PrefetchScalarGridSpec(
            num_scalar_prefetch=2,
            grid=grid,
            in_specs=in_specs,
            out_specs=out_specs,
            scratch_shapes=list(scratch),
        )
    }


def position(group_ref, index_ref, along_x, side, along_y):
    index = index_ref[0]
    x, y, c = (index >> 3) + along_x, ((index >> 1) & 3) + along_y, (index & 1) + side
    return group_ref[(x & 3) * LINE + (y & 3) * NC + (c & 1)]


def flag(condition):
    return jnp.where(condition, 1, 0)


def key_scores(k, q, limit=None):
    s = dot(k, q, 1, 1) * (SCALE * LOG2E)
    if limit is not None:
        key_row = lax.broadcasted_iota(jnp.int32, s.shape, 0)
        query_col = lax.broadcasted_iota(jnp.int32, s.shape, 1)
        s = jnp.where(key_row - query_col <= limit, s, NEG)
    return s


def forward_kernel(
    side, group_ref, index_ref, q_ref, kv_0, kv_1, kv_2, kv_3, out_ref, stat_ref, k_ref, vt_ref
):
    h = pl.program_id(0)
    for o, kv_ref in enumerate((kv_0, kv_1, kv_2, kv_3)):
        k_ref[o] = kv_ref[0]
        vt_ref[o] = kv_ref[1].T
    key_pos = [position(group_ref, index_ref, o, 0, 0) for o in range(NX)]
    first = (4 - (key_pos[0] >> 3)) & 3

    @pl.when(h == 0)
    def _():
        stat_ref[...] = jnp.zeros_like(stat_ref)

    @pl.loop(0, NY)
    def _(i):
        query_pos = position(group_ref, index_ref, 0, side, i)
        count = sum(flag(p <= query_pos) for p in key_pos)
        limit = jnp.where(key_pos[0] == query_pos, 0, TOK)

        @pl.when(count == 0)
        def _():
            out_ref[i] = jnp.zeros((TOK, HEAD_DIM), BF16)
            stat_ref[i, pl.ds(h, 1)] = jnp.full((1, TOK), NEG, F32)

        for n in range(1, NX + 1):

            @pl.when(count == n)
            def _():
                q = q_ref[i]
                slots = [(first + m) & 3 for m in range(n)]
                parts = [
                    key_scores(k_ref[o], q, limit if m == n - 1 else None)
                    for m, o in enumerate(slots)
                ]
                top = jnp.max(parts[0], axis=0, keepdims=True)
                for s in parts[1:]:
                    top = jnp.maximum(top, jnp.max(s, axis=0, keepdims=True))
                total = jnp.zeros((1, TOK), F32)
                acc = jnp.zeros((HEAD_DIM, TOK), F32)
                for m, o in enumerate(slots):
                    p = jnp.exp2(parts[m] - top)
                    total = total + jnp.sum(p, axis=0, keepdims=True)
                    acc = acc + dot(vt_ref[o], p.astype(BF16), 1, 0)
                out_ref[i] = (acc / total).T.astype(BF16)
                stat_ref[i, pl.ds(h, 1)] = top + jnp.log(total) * LOG2E


def rows_spec(first=0):
    return pl.BlockSpec((NY, TOK, HEAD_DIM), lambda h, *_: (0, 0, h + first))


def pair_spec(first=0):
    return pl.BlockSpec((2, TOK, HEAD_DIM), lambda h, *_: (0, 0, h + first))


def soft_forward(place, side, q, kvs):
    return call(
        functools.partial(forward_kernel, side),
        [shaped(NY, TOK, WIDTH, dtype=BF16), shaped(NY, 8, TOK)],
        NY * NX * HEADS * 4 * TOK * TOK * HEAD_DIM,
        (*place, q, *kvs),
        **placed(
            [rows_spec()] + [pair_spec()] * NX,
            [rows_spec(), pl.BlockSpec((NY, 8, TOK), lambda h, *_: (0, 0, 0))],
            [pltpu.VMEM((NX, TOK, HEAD_DIM), BF16), pltpu.VMEM((NX, HEAD_DIM, TOK), BF16)],
            (HEADS,),
        ),
    )


def delta_kernel(g_a, g_b, out_a, out_b, stat_a, stat_b, part_ref):
    h = pl.program_id(0)

    @pl.when(h == 0)
    def _():
        part_ref[0] = stat_a[...]
        part_ref[1] = stat_b[...]

    for side, (g_ref, o_ref) in enumerate(((g_a, out_a), (g_b, out_b))):
        for i in range(NY):
            product = o_ref[i].astype(F32) * g_ref[i].astype(F32)
            part_ref[side, i, pl.ds(h + 4, 1)] = jnp.sum(product.T, axis=0, keepdims=True)


def tile_backward(k, v, kt, q, g, lse, delta, limit=None):
    p = jnp.exp2(key_scores(k, q, limit) - lse)
    ds = (p * (dot(v, g, 1, 1) - delta)).astype(BF16)
    return dot(ds, q, 1, 0), dot(p.astype(BF16), g, 1, 0), dot(kt, ds, 1, 0)


def far_kernel(
    first_head, group_ref, index_ref, qa_ref, qb_ref, ga_ref, gb_ref, kv_1, kv_2, kv_3, stat_ref,
    *refs,
):
    dqa_ref, dqb_ref, dkv_ref, k_ref, v_ref, kt_ref, acc_ref = refs[-7:]
    h = pl.program_id(0) + first_head
    for o, kv_ref in enumerate((kv_1, kv_2, kv_3)):
        k_ref[o] = kv_ref[0]
        v_ref[o] = kv_ref[1]
        kt_ref[o] = kv_ref[0].T
    acc_ref[...] = jnp.zeros_like(acc_ref)
    key_pos = [position(group_ref, index_ref, o, 0, 0) for o in range(NX)]
    first, own_rank = (4 - (key_pos[0] >> 3)) & 3, key_pos[0] >> 3

    def one_block(q_ref, g_ref, dq_ref, side, b):
        query_pos = position(group_ref, index_ref, 0, side, b)
        count = sum(flag(p <= query_pos) for p in key_pos[1:])

        @pl.when(count == 0)
        def _():
            dq_ref[b] = jnp.zeros((TOK, HEAD_DIM), F32)

        for n in range(1, NX):

            @pl.when(count == n)
            def _():
                q, g = q_ref[b], g_ref[b]
                lse = stat_ref[side, b, pl.ds(h, 1)]
                delta = stat_ref[side, b, pl.ds(h + 4, 1)]
                dqt = jnp.zeros((HEAD_DIM, TOK), F32)
                for m in range(n):
                    o = ((first + m + flag(own_rank <= m)) & 3) - 1
                    dk, dv, dq = tile_backward(k_ref[o], v_ref[o], kt_ref[o], q, g, lse, delta)
                    acc_ref[o, 0] += dk
                    acc_ref[o, 1] += dv
                    dqt = dqt + dq
                dq_ref[b] = dqt.T

    pl.loop(0, NY)(lambda b: one_block(qa_ref, ga_ref, dqa_ref, 0, b))
    pl.loop(0, NY)(lambda b: one_block(qb_ref, gb_ref, dqb_ref, 1, b))
    for o in range(NX - 1):
        dkv_ref[o, 0] = (acc_ref[o, 0] * SCALE).astype(BF16)
        dkv_ref[o, 1] = acc_ref[o, 1].astype(BF16)


STAT_SPEC = pl.BlockSpec((2, NY, 8, TOK), lambda h, *_: (0, 0, 0, 0))


def far_backward(place, first, heads, qa, qb, ga, gb, kvs, stats, earlier=()):
    rows, pair = rows_spec(first), pair_spec(first)
    kwargs = placed(
        [rows] * 4 + [pair] * (NX - 1) + [STAT_SPEC] + [ANY] * len(earlier),
        [
            rows,
            rows,
            pl.BlockSpec((NX - 1, 2, TOK, HEAD_DIM), lambda h, *_: (0, 0, 0, h + first)),
        ],
        [
            pltpu.VMEM((NX - 1, TOK, HEAD_DIM), BF16),
            pltpu.VMEM((NX - 1, TOK, HEAD_DIM), BF16),
            pltpu.VMEM((NX - 1, HEAD_DIM, TOK), BF16),
            pltpu.VMEM((NX - 1, 2, TOK, HEAD_DIM), F32),
        ],
        (heads,),
    )
    return call(
        functools.partial(far_kernel, first),
        [shaped(NY, TOK, WIDTH), shaped(NY, TOK, WIDTH), shaped(NX - 1, 2, TOK, WIDTH, dtype=BF16)],
        2 * NY * (NX - 1) * heads * 10 * TOK * TOK * HEAD_DIM,
        (*place, qa, qb, ga, gb, *kvs, stats, *earlier),
        input_output_aliases={10 + i: i for i in range(len(earlier))},
        **kwargs,
    )


def near_kernel(
    group_ref, index_ref, qa_ref, qb_ref, ga_ref, gb_ref, kv_ref, stat_ref, dqa_in, dqb_in,
    dqa_ref, dqb_ref, dkv_ref, kt_ref,
):
    h = pl.program_id(0)
    kt_ref[...] = kv_ref[0].T
    dkv_ref[...] = jnp.zeros_like(dkv_ref)
    own = position(group_ref, index_ref, 0, 0, 0)
    sides = ((qa_ref, ga_ref, dqa_in, dqa_ref), (qb_ref, gb_ref, dqb_in, dqb_ref))
    for side, (q_ref, g_ref, dq_in, dq_ref) in enumerate(sides):
        where = [position(group_ref, index_ref, 0, side, b) for b in range(NY)]
        count = sum(flag(p >= own) for p in where)

        @pl.when(count == 0)
        def _():
            for b in range(NY):
                dq_ref[b] = (dq_in[b] * SCALE).astype(BF16)

        @pl.when(count > 0)
        def _():
            dk_sum = jnp.zeros((TOK, HEAD_DIM), F32)
            dv_sum = jnp.zeros((TOK, HEAD_DIM), F32)
            for b in range(NY):
                limit = jnp.where(where[b] == own, 0, jnp.where(where[b] > own, TOK, -TOK))
                dk, dv, dq = tile_backward(
                    kv_ref[0], kv_ref[1], kt_ref[...], q_ref[b], g_ref[b],
                    stat_ref[side, b, pl.ds(h, 1)], stat_ref[side, b, pl.ds(h + 4, 1)], limit,
                )
                dk_sum = dk_sum + dk
                dv_sum = dv_sum + dv
                dq_ref[b] = ((dq_in[b] + dq.T) * SCALE).astype(BF16)
            dkv_ref[0] += dk_sum * SCALE
            dkv_ref[1] += dv_sum


def near_backward(place, qa, qb, ga, gb, kv, stats, dqa, dqb):
    rows, pair = rows_spec(), pair_spec()
    return call(
        near_kernel,
        [
            shaped(NY, TOK, WIDTH, dtype=BF16),
            shaped(NY, TOK, WIDTH, dtype=BF16),
            shaped(2, TOK, WIDTH),
        ],
        2 * NY * HEADS * 10 * TOK * TOK * HEAD_DIM,
        (*place, qa, qb, ga, gb, kv, stats, dqa, dqb),
        **placed(
            [rows] * 4 + [pair, STAT_SPEC, rows, rows],
            [rows, rows, pair],
            [pltpu.VMEM((HEAD_DIM, TOK), BF16)],
            (HEADS,),
        ),
    )


def merged(stats_a, stats_b):
    lse_a, lse_b = stats_a[..., :4, :], stats_b[..., :4, :]
    top = jnp.maximum(lse_a, lse_b)
    weight_a, weight_b = jnp.exp2(lse_a - top), jnp.exp2(lse_b - top)
    total = weight_a + weight_b
    delta = (weight_a * stats_a[..., 4:, :] + weight_b * stats_b[..., 4:, :]) / total
    return jnp.concatenate([top + jnp.log(total) * LOG2E, delta], axis=-2)


def chip_kernel(part_ref, other_ref, out_ref):
    for side in range(2):
        out_ref[side] = merged(part_ref[side], other_ref[1 - side])


def line_kernel(
    part_ref, chip_ref, from_1, from_2, from_3, out_a_ref, out_b_ref, read_ref,
    stat_ref, mine_ref, theirs_ref,
):
    for side, o_ref in enumerate((out_a_ref, out_b_ref)):
        for i in range(NY):
            stats = chip_ref[side, i]
            for o, other in ((1, from_1), (2, from_2), (3, from_3)):
                stats = merged(stats, other[side, (i - o) % NY])
            stat_ref[side, i] = stats
            weight = jnp.exp2(part_ref[side, i, :4] - stats[:4])
            weight = jnp.concatenate([weight] * (HEAD_DIM // 4), axis=0).T
            for h in range(HEADS):
                scaled = o_ref[i, :, head_cols(h)].astype(F32) * weight[:, h : h + 1]
                if side == 0:
                    mine_ref[i, :, head_cols(h)] = scaled
                else:
                    theirs_ref[pl.ds(i * TOK, TOK), head_cols(h)] = scaled.astype(BF16)
    theirs_ref[pl.ds(NY * TOK, HEAD_DIM)] = read_ref[...]


def join_kernel(mine_ref, core_ref, read_ref, own_ref, pay_1, pay_2, pay_3):
    own_ref[...] = mine_ref[0] + core_ref[pl.ds(0, TOK)].astype(F32)
    for o, pay in ((1, pay_1), (2, pay_2), (3, pay_3)):
        total = mine_ref[o] + core_ref[pl.ds(o * TOK, TOK)].astype(F32)
        pay[pl.ds(0, TOK)] = total.astype(BF16)
        pay[pl.ds(TOK, HEAD_DIM)] = read_ref[...]
        pay[pl.ds(TOK + HEAD_DIM, HEAD_DIM)] = core_ref[pl.ds(NY * TOK, HEAD_DIM)]


def triangle(upper):
    row = lax.broadcasted_iota(jnp.int32, (TOK, TOK), 0)
    col = lax.broadcasted_iota(jnp.int32, (TOK, TOK), 1)
    return row <= col if upper else row >= col


def decay_columns(decay_ref):
    return dot(triangle(False).astype(F32), decay_ref[...], 1, 1, HIGHEST)


def pack_kernel(q_ref, key_ref, value_ref, decay_ref, out_ref):
    cumulative = decay_columns(decay_ref)
    total = cumulative[TOK - 1 : TOK]
    tail = jnp.exp(total - cumulative)
    out_ref[pl.ds(0, TOK)] = q_ref[...]
    row = lax.broadcasted_iota(jnp.int32, (16, HEAD_DIM), 0)
    for h in range(HEADS):
        keys = key_ref[:, head_cols(h)].astype(F32) * tail[:, h : h + 1]
        state = dot(keys.astype(BF16), value_ref[:, head_cols(h)], 0, 0)
        out_ref[pl.ds(STATE_ROW, HEAD_DIM), head_cols(h)] = state.astype(BF16)
        log = jnp.broadcast_to(total[:, h : h + 1], (16, HEAD_DIM))
        high = log.astype(BF16).astype(F32)
        middle = (log - high).astype(BF16).astype(F32)
        low = log - high - middle
        piece = jnp.where(row == 0, high, jnp.where(row == 1, middle, jnp.where(row == 2, low, 0.0)))
        out_ref[pl.ds(LOG_ROW, 16), head_cols(h)] = piece.astype(BF16)


def least(values):
    return functools.reduce(jnp.minimum, values)


def chain_keys(group_ref, index_ref, along_x, forward):
    found = [
        position(group_ref, index_ref, along_x, side, j) for side in range(NC) for j in range(NY)
    ]
    return found if forward else [31 - p for p in found]


def chain_members(keys):
    apart = -least([-k for k in keys]) - least(keys) > LINE - 1
    handed = [flag(jnp.logical_or(k < LINE, jnp.logical_not(apart))) for k in keys]
    whole = flag(jnp.logical_not(apart))
    same = [jnp.maximum(whole, flag(flag(k < LINE) == flag(keys[0] < LINE))) for k in keys]
    return handed, same


def line_sums(keys, logs, states):
    handed, same = chain_members(keys)
    before = [s * flag(k < keys[0]) for s, k in zip(same, keys)]

    def weighted(members):
        total = jnp.zeros((HEAD_DIM, WIDTH), F32)
        for j in range(LINE):
            exponent = jnp.zeros((1, WIDTH), F32)
            for i in range(LINE):
                if i != j:
                    between = members[i] * flag(keys[i] > keys[j])
                    exponent = exponent + logs[i] * between.astype(F32)
            weight = jnp.exp(exponent) * members[j].astype(F32)
            total = total + weight * states[j]()
        return total

    prefix = sum(log * b.astype(F32) for log, b in zip(logs, before))
    return weighted(handed), weighted(before), prefix


def total_sums(group_ref, index_ref, forward, totals, line_logs, prefix):
    lines = [chain_keys(group_ref, index_ref, o, forward) for o in range(NX)]
    starts = [least(keys) for keys in lines]
    same = chain_members(lines[0])[1]
    own_start = least([jnp.where(s > 0, k, 99) for s, k in zip(same, lines[0])])
    earlier = [flag(s < own_start) for s in starts]
    result = jnp.zeros((HEAD_DIM, WIDTH), F32)
    for o in range(NX):
        exponent = prefix
        for i in range(NX):
            if i != o:
                between = earlier[i] * flag(starts[i] > starts[o])
                exponent = exponent + line_logs[i] * between.astype(F32)
        result = result + jnp.exp(exponent) * earlier[o].astype(F32) * totals[o]
    return result


def states_kernel(group_ref, index_ref, qa_ref, qb_ref, handed_ref, entry_ref, log_ref):
    logs, states = [], []
    for ref in (qa_ref, qb_ref):
        for i in range(NY):
            rows = ref[i, pl.ds(LOG_ROW, 16)].astype(F32)
            logs.append(rows[0:1] + rows[1:2] + rows[2:3])
            states.append(
                functools.partial(
                    lambda ref, i: ref[i, pl.ds(STATE_ROW, HEAD_DIM)].astype(F32), ref, i
                )
            )
    keys = chain_keys(group_ref, index_ref, 0, True)
    handed, entry, prefix = line_sums(keys, logs, states)
    handed_ref[pl.ds(0, HEAD_DIM)] = handed
    handed_ref[pl.ds(HEAD_DIM, 8)] = jnp.broadcast_to(sum(logs), (8, WIDTH))
    entry_ref[pl.ds(0, HEAD_DIM)] = entry
    entry_ref[pl.ds(HEAD_DIM, 8)] = jnp.broadcast_to(prefix, (8, WIDTH))
    for j in range(LINE):
        log_ref[pl.ds(j, 1)] = logs[j]


def inner_terms(q, k, decay_ref, cumulative, h):
    rows = dot(decay_ref[...], triangle(True).astype(F32), 1, 0, HIGHEST)
    gap = cumulative[:, h : h + 1] - rows[h : h + 1]
    decay = jnp.where(triangle(False), jnp.exp(jnp.minimum(gap, 0.0)), 0.0)
    return decay, (dot(q, k, 1, 1) * decay).astype(BF16)


def read_kernel(
    group_ref, index_ref, q_ref, k_ref, v_ref, g_ref, decay_ref, part_ref, own, from_1, from_2,
    from_3, raw_ref, sum_ref, entry_ref, log_ref,
):
    all_totals = (own, from_1, from_2, from_3)
    line_logs = [t[pl.ds(HEAD_DIM, 1)] for t in all_totals]
    for o in range(NX):
        log_ref[pl.ds(o, 1)] = line_logs[o]
    log_ref[pl.ds(NX, 4)] = jnp.zeros((4, WIDTH), F32)
    entry = part_ref[pl.ds(0, HEAD_DIM)] + total_sums(
        group_ref, index_ref, True, [t[pl.ds(0, HEAD_DIM)] for t in all_totals], line_logs,
        part_ref[pl.ds(HEAD_DIM, 1)],
    )
    entry_ref[...] = entry.astype(BF16)
    cumulative = decay_columns(decay_ref)
    squares = jnp.zeros((TOK, 1), F32)
    inner = jnp.zeros((TOK, 1), F32)
    for h in range(HEADS):
        cols = head_cols(h)
        q = q_ref[:, cols]
        scores = inner_terms(q, k_ref[:, cols], decay_ref, cumulative, h)[1]
        carried = dot(q, entry_ref[:, cols], 1, 0)
        raw = dot(scores, v_ref[:, cols], 1, 0) + jnp.exp(cumulative[:, h : h + 1]) * carried
        raw_ref[:, cols] = raw
        squares = squares + jnp.sum(raw * raw, axis=1, keepdims=True)
        inner = inner + jnp.sum(raw * g_ref[:, cols].astype(F32), axis=1, keepdims=True)
    lane = lax.broadcasted_iota(jnp.int32, (TOK, HEAD_DIM), 1)
    sums = jnp.where(lane == 0, squares, jnp.where(lane == 1, inner, 0.0))
    sum_ref[...] = sums.T[:8]


def grad_kernel(
    q_ref, k_ref, v_ref, g_ref, decay_ref, entry_ref, raw_ref, sum_0, sum_1, sum_2, sum_3,
    out_ref, dq_ref, dk_ref, dv_ref, read_ref,
):
    cumulative = decay_columns(decay_ref)
    sums = (sum_0[...] + sum_1[...]) + (sum_2[...] + sum_3[...])
    sums = jnp.concatenate([sums] * (HEAD_DIM // 8), axis=0).T
    inverse = 1.0 / jnp.sqrt(sums[:, 0:1] * (1.0 / (HEAD_TOTAL * HEAD_DIM)) + EPS)
    aligned = sums[:, 1:2] * inverse * (1.0 / (HEAD_TOTAL * HEAD_DIM))
    for h in range(HEADS):
        cols = head_cols(h)
        q, k = q_ref[:, cols], k_ref[:, cols]
        out = raw_ref[:, cols] * inverse
        out_ref[:, cols] = out
        raw_grad = ((g_ref[:, cols].astype(F32) - out * aligned) * inverse).astype(BF16)
        decay, scores = inner_terms(q, k, decay_ref, cumulative, h)
        head_decay = jnp.exp(cumulative[:, h : h + 1])
        inner_grad = (dot(raw_grad, v_ref[:, cols], 1, 1) * decay).astype(BF16)
        carried = dot(raw_grad, entry_ref[:, cols], 1, 1)
        dq_ref[:, cols] = dot(inner_grad, k, 1, 0) + head_decay * carried
        dk_ref[:, cols] = dot(inner_grad, q, 0, 0)
        dv_ref[:, cols] = dot(scores, raw_grad, 0, 0)
        scaled = (q.astype(F32) * head_decay).astype(BF16)
        read_ref[:, cols] = dot(scaled, raw_grad, 0, 0).astype(BF16)


def back_kernel(
    group_ref, index_ref, log_ref, read_ref, core_ref, from_1, from_2, from_3, handed_ref, part_ref
):
    logs = [log_ref[pl.ds(j, 1)] for j in range(LINE)]
    sources = [(read_ref, 0), (from_1, TOK), (from_2, TOK), (from_3, TOK)]
    sources += [(core_ref, NY * TOK)]
    sources += [(ref, TOK + HEAD_DIM) for ref in (from_1, from_2, from_3)]
    states = [
        functools.partial(lambda ref, row: ref[pl.ds(row, HEAD_DIM)].astype(F32), ref, row)
        for ref, row in sources
    ]
    keys = chain_keys(group_ref, index_ref, 0, False)
    handed, part, prefix = line_sums(keys, logs, states)
    handed_ref[...] = handed
    part_ref[pl.ds(0, HEAD_DIM)] = part
    part_ref[pl.ds(HEAD_DIM, 8)] = jnp.broadcast_to(prefix, (8, WIDTH))


def write_kernel(
    group_ref, index_ref, k_ref, v_ref, decay_ref, part_ref, log_ref, own, from_1, from_2, from_3,
    dk_in, dv_in, dk_ref, dv_ref,
):
    leave_all = part_ref[pl.ds(0, HEAD_DIM)] + total_sums(
        group_ref, index_ref, False, [t[...] for t in (own, from_1, from_2, from_3)],
        [log_ref[pl.ds(o, 1)] for o in range(NX)], part_ref[pl.ds(HEAD_DIM, 1)],
    )
    cumulative = decay_columns(decay_ref)
    tail = jnp.exp(cumulative[TOK - 1 : TOK] - cumulative)
    for h in range(HEADS):
        cols = head_cols(h)
        leave = leave_all[:, h * HEAD_DIM : (h + 1) * HEAD_DIM].astype(BF16)
        scale = tail[:, h : h + 1]
        dk_ref[:, cols] = dk_in[:, cols] + scale * dot(v_ref[:, cols], leave, 1, 1)
        dv_ref[:, cols] = dv_in[:, cols] + scale * dot(k_ref[:, cols], leave, 1, 0)


def in_vmem(n):
    return [pl.BlockSpec(memory_space=pltpu.VMEM)] * n


def on_device(
    group_of, soft_query, soft_key, soft_value, soft_grad,
    lin_query, lin_key, lin_value, log_decay, lin_grad,
):
    place = (group_of, lax.axis_index(SEQ).reshape(1))
    decay = log_decay.T

    kv_own = jnp.stack([soft_key, soft_value])
    kv = {0: kv_own, **{o: fetch(kv_own, "x", NX, o) for o in OFFSETS}}
    kvs = [kv[o] for o in range(NX)]
    packed = call(
        pack_kernel,
        shaped(PACK_ROWS, WIDTH, dtype=BF16),
        2**26,
        (soft_query, lin_key, lin_value, decay),
        vmem=60,
    )
    q_from = {0: packed, **{o: fetch(packed, "y", NY, o) for o in OFFSETS}}
    g_from = {0: soft_grad, **{o: fetch(soft_grad, "y", NY, o) for o in OFFSETS}}
    qa = jnp.stack([q_from[o] for o in range(NY)])
    qb = fetch(qa, "c", NC, 1)
    ga = jnp.stack([g_from[o] for o in range(NY)])
    gb = fetch(ga, "c", NC, 1)

    out_a, stat_a = soft_forward(place, 0, qa, kvs)
    handed, entry_part, logs = call(
        states_kernel,
        [shaped(HEAD_DIM + 8, WIDTH), shaped(HEAD_DIM + 8, WIDTH), shaped(8, WIDTH)],
        2**24,
        (*place, qa, qb),
        **placed(in_vmem(2), in_vmem(3)),
    )
    totals = [handed, *(fetch(handed, "x", NX, o) for o in (1, 2, 3))]
    out_b, stat_b = soft_forward(place, 1, qb, kvs)
    part = call(
        delta_kernel,
        shaped(2, NY, 8, TOK),
        2**25,
        (ga, gb, out_a, out_b, stat_a, stat_b),
        grid=(HEADS,),
        in_specs=[rows_spec()] * 4 + [pl.BlockSpec((NY, 8, TOK), lambda h: (0, 0, 0))] * 2,
        out_specs=pl.BlockSpec((2, NY, 8, TOK), lambda h: (0, 0, 0, 0)),
    )
    other = fetch(part, "c", NC, 1)

    rows = shaped(TOK, WIDTH)
    raw, sums, entry, line_logs = call(
        read_kernel,
        [rows, shaped(8, TOK), shaped(HEAD_DIM, WIDTH, dtype=BF16), shaped(8, WIDTH)],
        2**27,
        (*place, lin_query, lin_key, lin_value, lin_grad, decay, entry_part, *totals),
        **placed(in_vmem(10), in_vmem(4)),
    )
    all_sums = [sums, *(fetch(sums, "head", NZ, o) for o in (1, 2, 3))]
    chip = call(chip_kernel, shaped(2, NY, 8, TOK), 2**20, (part, other))
    received = {o: fetch(chip, "y", NY, o) for o in OFFSETS}
    lin_out, lin_dq, dk_local, dv_local, read_grad = call(
        grad_kernel,
        [rows] * 4 + [shaped(HEAD_DIM, WIDTH, dtype=BF16)],
        2**28,
        (lin_query, lin_key, lin_value, lin_grad, decay, entry, raw, *all_sums),
    )
    stats, mine, theirs = call(
        line_kernel,
        [
            shaped(2, NY, 8, TOK),
            shaped(NY, TOK, WIDTH),
            shaped(NY * TOK + HEAD_DIM, WIDTH, dtype=BF16),
        ],
        2**22,
        (part, chip, received[1], received[2], received[3], out_a, out_b, read_grad),
    )
    from_core = fetch(theirs, "c", NC, 1)

    grads = far_backward(place, 0, 1, qa, qb, ga, gb, kvs[1:], stats)
    own_out, *pays = call(
        join_kernel,
        [rows] + [shaped(2 * TOK, WIDTH, dtype=BF16)] * 3,
        2**22,
        (mine, from_core, read_grad),
    )
    sent_out = {o: send(pays[o - 1], "y", NY, o) for o in OFFSETS}
    dq_a, dq_b, far_dkv = far_backward(place, 1, 2, qa, qb, ga, gb, kvs[1:], stats, tuple(grads))
    sent_dkv = [send(far_dkv[o - 1], "x", NX, o) for o in OFFSETS]
    dq_a, dq_b, near_dkv = near_backward(place, qa, qb, ga, gb, kvs[0], stats, dq_a, dq_b)
    dq_core = fetch(dq_b, "c", NC, 1)

    back_handed, leave_part = call(
        back_kernel,
        [shaped(HEAD_DIM, WIDTH), shaped(HEAD_DIM + 8, WIDTH)],
        2**24,
        (*place, logs, read_grad, from_core, *(sent_out[NY - o] for o in (1, 2, 3))),
        **placed(in_vmem(6), in_vmem(2)),
    )
    back_totals = [back_handed, *(fetch(back_handed, "x", NX, o) for o in (1, 2, 3))]
    chip_dq = dq_a.astype(F32) + dq_core.astype(F32)
    soft_dq = chip_dq[0]
    for o in OFFSETS:
        soft_dq = soft_dq + send(chip_dq[o].astype(BF16), "y", NY, o).astype(F32)
    lin_dk, lin_dv = call(
        write_kernel,
        [rows, rows],
        2**26,
        (*place, lin_key, lin_value, decay, leave_part, line_logs, *back_totals, dk_local, dv_local),
        **placed(in_vmem(11), in_vmem(2)),
    )
    soft_out = own_out
    for o in OFFSETS:
        soft_out = soft_out + sent_out[o][:TOK].astype(F32)
    dkv = near_dkv
    for sent in sent_dkv:
        dkv = dkv + sent.astype(F32)
    return (
        soft_out.astype(BF16), soft_dq.astype(BF16), dkv[0].astype(BF16), dkv[1].astype(BF16),
        lin_out, lin_dq, lin_dk, lin_dv,
    )


def solution(mesh):
    grid = Mesh(mesh.devices.reshape(NX, NY, NC, NZ), (*SEQ, "head"))
    block = P(SEQ, "head")

    return jax.shard_map(
        on_device,
        mesh=grid,
        in_specs=(P(),) + (block,) * 9,
        out_specs=(block,) * 8,
        check_vma=False,
    )
```

```python
import functools

import jax
import jax.numpy as jnp
from jax import lax
from jax.experimental import pallas as pl
from jax.experimental.pallas import tpu as pltpu
from jax.sharding import Mesh
from jax.sharding import PartitionSpec as P


HEAD_TOTAL = 12
HEAD_DIM = 128
HEADS = 3
WIDTH = HEADS * HEAD_DIM
TOK = 256
NX, NY, NC, NZ = 4, 4, 2, 4
LINE = NY * NC
EPS = 1e-06
SCALE = HEAD_DIM ** (-0.5)
LOG2E = 1.4426950408889634
NEG = -1e30
F32 = jnp.float32
BF16 = jnp.bfloat16
HIGHEST = lax.Precision.HIGHEST
SEQ = ("x", "y", "c")
OFFSETS = (1, 3, 2)
STATE_ROW = TOK
LOG_ROW = STATE_ROW + HEAD_DIM
PACK_ROWS = LOG_ROW + 16
ANY = pl.BlockSpec(memory_space=pl.ANY)


def send(block, axis, size, offset):
    return lax.ppermute(block, axis, [(i, (i + offset) % size) for i in range(size)])


def fetch(block, axis, size, offset):
    return send(block, axis, size, -offset)


def dot(a, b, dim_a, dim_b, precision=None):
    return lax.dot_general(
        a, b, (((dim_a,), (dim_b,)), ((), ())), precision=precision, preferred_element_type=F32
    )


def head_cols(h):
    return pl.ds(h * HEAD_DIM, HEAD_DIM)


def shaped(*dims, dtype=F32):
    return jax.ShapeDtypeStruct(dims, dtype)


def call(kernel, out_shape, flops, args, vmem=40, **kwargs):
    return pl.pallas_call(
        kernel,
        out_shape=out_shape,
        cost_estimate=pl.CostEstimate(flops=flops, transcendentals=2**18, bytes_accessed=2 * 2**20),
        compiler_params=pltpu.CompilerParams(vmem_limit_bytes=vmem * 2**20),
        **kwargs,
    )(*args)


def placed(in_specs, out_specs, scratch=(), grid=()):
    return {
        "grid_spec": pltpu.PrefetchScalarGridSpec(
            num_scalar_prefetch=2,
            grid=grid,
            in_specs=in_specs,
            out_specs=out_specs,
            scratch_shapes=list(scratch),
        )
    }


def position(group_ref, index_ref, along_x, side, along_y):
    index = index_ref[0]
    x, y, c = (index >> 3) + along_x, ((index >> 1) & 3) + along_y, (index & 1) + side
    return group_ref[(x & 3) * LINE + (y & 3) * NC + (c & 1)]


def flag(condition):
    return jnp.where(condition, 1, 0)


def causal(scores):
    row = lax.broadcasted_iota(jnp.int32, scores.shape, 0)
    col = lax.broadcasted_iota(jnp.int32, scores.shape, 1)
    return jnp.where(row <= col, scores, NEG)


def hidden(key_pos, query_pos):
    return jnp.where(key_pos > query_pos, -NEG, 0.0)


def staged(items, first, second):
    current = first(items[0])
    for i, item in enumerate(items):
        following = first(items[i + 1]) if i + 1 < len(items) else None
        second(item, current)
        current = following


def forward_kernel(
    side, group_ref, index_ref, q_ref, kv_0, kv_1, kv_2, kv_3, out_ref, stat_ref, k_ref, vt_ref
):
    h = pl.program_id(0)
    for o, kv_ref in enumerate((kv_0, kv_1, kv_2, kv_3)):
        k_ref[pl.ds(o * TOK, TOK)] = kv_ref[0]
        vt_ref[pl.ds(0, HEAD_DIM), pl.ds(o * TOK, TOK)] = kv_ref[1].T

    @pl.when(h == 0)
    def _():
        stat_ref[...] = jnp.zeros_like(stat_ref)
        vt_ref[pl.ds(HEAD_DIM, 16)] = jnp.ones((16, NX * TOK), BF16)

    key_pos = [position(group_ref, index_ref, o, 0, 0) for o in range(NX)]

    def scores(i):
        return [dot(k_ref[pl.ds(o * TOK, TOK)], q_ref[i], 1, 1) for o in range(NX)]

    def finish(i, parts):
        query_pos = position(group_ref, index_ref, 0, side, i)
        if side == 0 and i == 0:
            parts = [causal(parts[0]), *parts[1:]]
        hide = [hidden(p, query_pos) for p in key_pos]
        tops = [jnp.max(s, axis=0, keepdims=True) - x for s, x in zip(parts, hide)]
        top = functools.reduce(jnp.maximum, tops)
        probs = [
            jnp.exp2((s - (top + x)) * (SCALE * LOG2E)).astype(BF16) for s, x in zip(parts, hide)
        ]
        acc = dot(vt_ref[...], jnp.concatenate(probs), 1, 0)
        total = acc[HEAD_DIM : HEAD_DIM + 1]
        seen = top > 0.5 * NEG
        out_ref[i] = jnp.where(seen, acc[:HEAD_DIM] * (1.0 / total), 0.0).T.astype(BF16)
        log = top * (SCALE * LOG2E) + jnp.log(total) * LOG2E
        stat_ref[i, pl.ds(h, 1)] = jnp.where(seen, log, NEG)

    staged(range(NY), scores, finish)


def rows_spec(first=0):
    return pl.BlockSpec((NY, TOK, HEAD_DIM), lambda h, *_: (0, 0, h + first))


def pair_spec(first=0):
    return pl.BlockSpec((2, TOK, HEAD_DIM), lambda h, *_: (0, 0, h + first))


def soft_forward(place, side, q, kvs):
    return call(
        functools.partial(forward_kernel, side),
        [shaped(NY, TOK, WIDTH, dtype=BF16), shaped(NY, 8, TOK)],
        NY * NX * HEADS * 4 * TOK * TOK * HEAD_DIM,
        (*place, q, *kvs),
        **placed(
            [rows_spec()] + [pair_spec()] * NX,
            [rows_spec(), pl.BlockSpec((NY, 8, TOK), lambda h, *_: (0, 0, 0))],
            [
                pltpu.VMEM((NX * TOK, HEAD_DIM), BF16),
                pltpu.VMEM((HEAD_DIM + 16, NX * TOK), BF16),
            ],
            (HEADS,),
        ),
    )


def delta_kernel(g_a, g_b, out_a, out_b, stat_a, stat_b, part_ref):
    h = pl.program_id(0)

    @pl.when(h == 0)
    def _():
        part_ref[0] = stat_a[...]
        part_ref[1] = stat_b[...]

    for side, (g_ref, o_ref) in enumerate(((g_a, out_a), (g_b, out_b))):
        for i in range(NY):
            product = o_ref[i].astype(F32) * g_ref[i].astype(F32)
            part_ref[side, i, pl.ds(h + 4, 1)] = jnp.sum(product.T, axis=0, keepdims=True)


def far_kernel(
    first_head, group_ref, index_ref, qa_ref, qb_ref, ga_ref, gb_ref, kv_1, kv_2, kv_3, stat_ref,
    *refs,
):
    dqa_ref, dqb_ref, dkv_ref, k_ref, v_ref, kt_ref, acc_ref = refs[-7:]
    h = pl.program_id(0) + first_head
    tiles = [pl.ds(o * TOK, TOK) for o in range(NX - 1)]
    for tile, kv_ref in zip(tiles, (kv_1, kv_2, kv_3)):
        k_ref[tile] = kv_ref[0]
        v_ref[tile] = kv_ref[1]
        kt_ref[:, tile] = kv_ref[0].T
    key_pos = [position(group_ref, index_ref, o, 0, 0) for o in range(1, NX)]
    acc_ref[...] = jnp.zeros_like(acc_ref)

    def products(item):
        q_ref, g_ref, _, _, b = item
        return (
            [dot(k_ref[t], q_ref[b], 1, 1) for t in tiles],
            [dot(v_ref[t], g_ref[b], 1, 1) for t in tiles],
        )

    def finish(item, found):
        q_ref, g_ref, dq_ref, side, b = item
        query_pos = position(group_ref, index_ref, 0, side, b)
        lse = stat_ref[side, b, pl.ds(h, 1)]
        delta = stat_ref[side, b, pl.ds(h + 4, 1)]
        probs, grads = [], []
        for x, s, dprobs in zip(key_pos, *found):
            p = jnp.exp2(s * (SCALE * LOG2E) - (lse + hidden(x, query_pos)))
            probs.append(p.astype(BF16))
            grads.append((p * (dprobs - delta)).astype(BF16))
        probs, grads = jnp.concatenate(probs), jnp.concatenate(grads)
        acc_ref[0] += dot(grads, q_ref[b], 1, 0)
        acc_ref[1] += dot(probs, g_ref[b], 1, 0)
        dq_ref[b, 0] = dot(kt_ref[...], grads, 1, 0)

    items = [(qa_ref, ga_ref, dqa_ref, 0, b) for b in range(NY)]
    items += [(qb_ref, gb_ref, dqb_ref, 1, b) for b in range(NY)]
    staged(items, products, finish)
    for o, tile in enumerate(tiles):
        dkv_ref[o, 0] = (acc_ref[0, tile] * SCALE).astype(BF16)
        dkv_ref[o, 1] = acc_ref[1, tile].astype(BF16)


STAT_SPEC = pl.BlockSpec((2, NY, 8, TOK), lambda h, *_: (0, 0, 0, 0))


def far_backward(place, first, heads, qa, qb, ga, gb, kvs, stats, earlier=()):
    rows, pair = rows_spec(first), pair_spec(first)
    turned = pl.BlockSpec((NY, 1, HEAD_DIM, TOK), lambda h, *_: (0, h + first, 0, 0))
    dq_shape = shaped(NY, HEADS, HEAD_DIM, TOK)
    kwargs = placed(
        [rows] * 4 + [pair] * (NX - 1) + [STAT_SPEC] + [ANY] * len(earlier),
        [
            turned,
            turned,
            pl.BlockSpec((NX - 1, 2, TOK, HEAD_DIM), lambda h, *_: (0, 0, 0, h + first)),
        ],
        [
            pltpu.VMEM(((NX - 1) * TOK, HEAD_DIM), BF16),
            pltpu.VMEM(((NX - 1) * TOK, HEAD_DIM), BF16),
            pltpu.VMEM((HEAD_DIM, (NX - 1) * TOK), BF16),
            pltpu.VMEM((2, (NX - 1) * TOK, HEAD_DIM), F32),
        ],
        (heads,),
    )
    return call(
        functools.partial(far_kernel, first),
        [dq_shape, dq_shape, shaped(NX - 1, 2, TOK, WIDTH, dtype=BF16)],
        2 * NY * (NX - 1) * heads * 10 * TOK * TOK * HEAD_DIM,
        (*place, qa, qb, ga, gb, *kvs, stats, *earlier),
        input_output_aliases={10 + i: i for i in range(len(earlier))},
        **kwargs,
    )


def near_kernel(
    group_ref, index_ref, qa_ref, qb_ref, ga_ref, gb_ref, kv_ref, stat_ref, dqa_in, dqb_in,
    dqa_ref, dqb_ref, dkv_ref, kt_ref,
):
    h = pl.program_id(0)
    kt_ref[...] = kv_ref[0].T
    own = position(group_ref, index_ref, 0, 0, 0)

    def products(item):
        q_ref, g_ref, b = item[0], item[1], item[-1]
        return dot(kv_ref[0], q_ref[b], 1, 1), dot(kv_ref[1], g_ref[b], 1, 1)

    def finish(item, found):
        q_ref, g_ref, dq_in, dq_ref, side, b = item
        s, dprobs = found
        lse = stat_ref[side, b, pl.ds(h, 1)]
        delta = stat_ref[side, b, pl.ds(h + 4, 1)]
        s = s * (SCALE * LOG2E)
        start = side == 0 and b == 0
        if start:
            s = causal(s)
        p = jnp.exp2(s - (lse + hidden(own, position(group_ref, index_ref, 0, side, b))))
        ds = (p * (dprobs - delta)).astype(BF16)
        dq_sum = dq_in[b, 0] + dot(kt_ref[...], ds, 1, 0)
        dq_ref[b] = (dq_sum * SCALE).T.astype(BF16)
        dk, dv = dot(ds, q_ref[b], 1, 0) * SCALE, dot(p.astype(BF16), g_ref[b], 1, 0)
        dkv_ref[0] = dk if start else dkv_ref[0] + dk
        dkv_ref[1] = dv if start else dkv_ref[1] + dv

    sides = ((qa_ref, ga_ref, dqa_in, dqa_ref), (qb_ref, gb_ref, dqb_in, dqb_ref))
    items = [(*refs, side, b) for side, refs in enumerate(sides) for b in range(NY)]
    staged(items, products, finish)


def near_backward(place, qa, qb, ga, gb, kv, stats, dqa, dqb):
    rows, pair = rows_spec(), pair_spec()
    turned = pl.BlockSpec((NY, 1, HEAD_DIM, TOK), lambda h, *_: (0, h, 0, 0))
    return call(
        near_kernel,
        [
            shaped(NY, TOK, WIDTH, dtype=BF16),
            shaped(NY, TOK, WIDTH, dtype=BF16),
            shaped(2, TOK, WIDTH),
        ],
        2 * NY * HEADS * 10 * TOK * TOK * HEAD_DIM,
        (*place, qa, qb, ga, gb, kv, stats, dqa, dqb),
        **placed(
            [rows] * 4 + [pair, STAT_SPEC, turned, turned],
            [rows, rows, pair],
            [pltpu.VMEM((HEAD_DIM, TOK), BF16)],
            (HEADS,),
        ),
    )


def merged(stats_a, stats_b):
    lse_a, lse_b = stats_a[..., :4, :], stats_b[..., :4, :]
    top = jnp.maximum(lse_a, lse_b)
    weight_a, weight_b = jnp.exp2(lse_a - top), jnp.exp2(lse_b - top)
    total = weight_a + weight_b
    delta = (weight_a * stats_a[..., 4:, :] + weight_b * stats_b[..., 4:, :]) / total
    return jnp.concatenate([top + jnp.log(total) * LOG2E, delta], axis=-2)


def chip_kernel(part_ref, other_ref, out_ref):
    for side in range(2):
        out_ref[side] = merged(part_ref[side], other_ref[1 - side])


def line_kernel(
    part_ref, chip_ref, from_1, from_2, from_3, out_a_ref, out_b_ref, read_ref,
    stat_ref, mine_ref, theirs_ref,
):
    for side, o_ref in enumerate((out_a_ref, out_b_ref)):
        for i in range(NY):
            stats = chip_ref[side, i]
            for o, other in ((1, from_1), (2, from_2), (3, from_3)):
                stats = merged(stats, other[side, (i - o) % NY])
            stat_ref[side, i] = stats
            weight = jnp.exp2(part_ref[side, i, :4] - stats[:4])
            weight = jnp.concatenate([weight] * (HEAD_DIM // 4), axis=0).T
            for h in range(HEADS):
                scaled = o_ref[i, :, head_cols(h)].astype(F32) * weight[:, h : h + 1]
                if side == 0:
                    mine_ref[i, :, head_cols(h)] = scaled
                else:
                    theirs_ref[pl.ds(i * TOK, TOK), head_cols(h)] = scaled.astype(BF16)
    theirs_ref[pl.ds(NY * TOK, HEAD_DIM)] = read_ref[...]


def join_kernel(mine_ref, core_ref, read_ref, own_ref, pay_1, pay_2, pay_3):
    own_ref[...] = mine_ref[0] + core_ref[pl.ds(0, TOK)].astype(F32)
    for o, pay in ((1, pay_1), (2, pay_2), (3, pay_3)):
        total = mine_ref[o] + core_ref[pl.ds(o * TOK, TOK)].astype(F32)
        pay[pl.ds(0, TOK)] = total.astype(BF16)
        pay[pl.ds(TOK, HEAD_DIM)] = read_ref[...]
        pay[pl.ds(TOK + HEAD_DIM, HEAD_DIM)] = core_ref[pl.ds(NY * TOK, HEAD_DIM)]


def triangle(upper):
    row = lax.broadcasted_iota(jnp.int32, (TOK, TOK), 0)
    col = lax.broadcasted_iota(jnp.int32, (TOK, TOK), 1)
    return row <= col if upper else row >= col


def decay_columns(decay_ref):
    return dot(triangle(False).astype(F32), decay_ref[...], 1, 1, HIGHEST)


def pack_kernel(g_ref, key_ref, value_ref, decay_ref, out_ref):
    cumulative = decay_columns(decay_ref)
    total = cumulative[TOK - 1 : TOK]
    tail = jnp.exp(total - cumulative)
    out_ref[pl.ds(0, TOK)] = g_ref[...]
    row = lax.broadcasted_iota(jnp.int32, (16, HEAD_DIM), 0)
    for h in range(HEADS):
        keys = key_ref[:, head_cols(h)].astype(F32) * tail[:, h : h + 1]
        state = dot(keys.astype(BF16), value_ref[:, head_cols(h)], 0, 0)
        out_ref[pl.ds(STATE_ROW, HEAD_DIM), head_cols(h)] = state.astype(BF16)
        log = jnp.broadcast_to(total[:, h : h + 1], (16, HEAD_DIM))
        high = log.astype(BF16).astype(F32)
        middle = (log - high).astype(BF16).astype(F32)
        low = log - high - middle
        piece = jnp.where(row == 0, high, jnp.where(row == 1, middle, jnp.where(row == 2, low, 0.0)))
        out_ref[pl.ds(LOG_ROW, 16), head_cols(h)] = piece.astype(BF16)


def least(values):
    return functools.reduce(jnp.minimum, values)


def chain_keys(group_ref, index_ref, along_x, forward):
    found = [
        position(group_ref, index_ref, along_x, side, j) for side in range(NC) for j in range(NY)
    ]
    return found if forward else [31 - p for p in found]


def chain_members(keys):
    apart = -least([-k for k in keys]) - least(keys) > LINE - 1
    handed = [flag(jnp.logical_or(k < LINE, jnp.logical_not(apart))) for k in keys]
    whole = flag(jnp.logical_not(apart))
    same = [jnp.maximum(whole, flag(flag(k < LINE) == flag(keys[0] < LINE))) for k in keys]
    return handed, same


def line_sums(keys, logs, states):
    handed, same = chain_members(keys)
    before = [s * flag(k < keys[0]) for s, k in zip(same, keys)]

    def weighted(members):
        total = jnp.zeros((HEAD_DIM, WIDTH), F32)
        for j in range(LINE):
            exponent = jnp.zeros((1, WIDTH), F32)
            for i in range(LINE):
                if i != j:
                    between = members[i] * flag(keys[i] > keys[j])
                    exponent = exponent + logs[i] * between.astype(F32)
            weight = jnp.exp(exponent) * members[j].astype(F32)
            total = total + weight * states[j]()
        return total

    prefix = sum(log * b.astype(F32) for log, b in zip(logs, before))
    return weighted(handed), weighted(before), prefix


def total_sums(group_ref, index_ref, forward, totals, line_logs, prefix):
    lines = [chain_keys(group_ref, index_ref, o, forward) for o in range(NX)]
    starts = [least(keys) for keys in lines]
    same = chain_members(lines[0])[1]
    own_start = least([jnp.where(s > 0, k, 99) for s, k in zip(same, lines[0])])
    earlier = [flag(s < own_start) for s in starts]
    result = jnp.zeros((HEAD_DIM, WIDTH), F32)
    for o in range(NX):
        exponent = prefix
        for i in range(NX):
            if i != o:
                between = earlier[i] * flag(starts[i] > starts[o])
                exponent = exponent + line_logs[i] * between.astype(F32)
        result = result + jnp.exp(exponent) * earlier[o].astype(F32) * totals[o]
    return result


def states_kernel(group_ref, index_ref, ga_ref, gb_ref, handed_ref, entry_ref, log_ref):
    logs, states = [], []
    for ref in (ga_ref, gb_ref):
        for i in range(NY):
            rows = ref[i, pl.ds(LOG_ROW, 16)].astype(F32)
            logs.append(rows[0:1] + rows[1:2] + rows[2:3])
            states.append(
                functools.partial(
                    lambda ref, i: ref[i, pl.ds(STATE_ROW, HEAD_DIM)].astype(F32), ref, i
                )
            )
    keys = chain_keys(group_ref, index_ref, 0, True)
    handed, entry, prefix = line_sums(keys, logs, states)
    handed_ref[pl.ds(0, HEAD_DIM)] = handed
    handed_ref[pl.ds(HEAD_DIM, 8)] = jnp.broadcast_to(sum(logs), (8, WIDTH))
    entry_ref[pl.ds(0, HEAD_DIM)] = entry
    entry_ref[pl.ds(HEAD_DIM, 8)] = jnp.broadcast_to(prefix, (8, WIDTH))
    for j in range(LINE):
        log_ref[pl.ds(j, 1)] = logs[j]


def inner_terms(q, k, decay_ref, cumulative, h):
    rows = dot(decay_ref[...], triangle(True).astype(F32), 1, 0, HIGHEST)
    gap = cumulative[:, h : h + 1] - rows[h : h + 1]
    decay = jnp.where(triangle(False), jnp.exp(jnp.minimum(gap, 0.0)), 0.0)
    return decay, (dot(q, k, 1, 1) * decay).astype(BF16)


def read_kernel(
    group_ref, index_ref, q_ref, k_ref, v_ref, g_ref, decay_ref, part_ref, own, from_1, from_2,
    from_3, raw_ref, sum_ref, entry_ref, log_ref,
):
    all_totals = (own, from_1, from_2, from_3)
    line_logs = [t[pl.ds(HEAD_DIM, 1)] for t in all_totals]
    for o in range(NX):
        log_ref[pl.ds(o, 1)] = line_logs[o]
    log_ref[pl.ds(NX, 4)] = jnp.zeros((4, WIDTH), F32)
    entry = part_ref[pl.ds(0, HEAD_DIM)] + total_sums(
        group_ref, index_ref, True, [t[pl.ds(0, HEAD_DIM)] for t in all_totals], line_logs,
        part_ref[pl.ds(HEAD_DIM, 1)],
    )
    entry_ref[...] = entry.astype(BF16)
    cumulative = decay_columns(decay_ref)
    squares = jnp.zeros((TOK, 1), F32)
    inner = jnp.zeros((TOK, 1), F32)
    for h in range(HEADS):
        cols = head_cols(h)
        q = q_ref[:, cols]
        scores = inner_terms(q, k_ref[:, cols], decay_ref, cumulative, h)[1]
        carried = dot(q, entry_ref[:, cols], 1, 0)
        raw = dot(scores, v_ref[:, cols], 1, 0) + jnp.exp(cumulative[:, h : h + 1]) * carried
        raw_ref[:, cols] = raw
        squares = squares + jnp.sum(raw * raw, axis=1, keepdims=True)
        inner = inner + jnp.sum(raw * g_ref[:, cols].astype(F32), axis=1, keepdims=True)
    lane = lax.broadcasted_iota(jnp.int32, (TOK, HEAD_DIM), 1)
    sums = jnp.where(lane == 0, squares, jnp.where(lane == 1, inner, 0.0))
    sum_ref[...] = sums.T[:8]


def grad_kernel(
    q_ref, k_ref, v_ref, g_ref, decay_ref, entry_ref, raw_ref, sum_0, sum_1, sum_2, sum_3,
    out_ref, dq_ref, dk_ref, dv_ref, read_ref,
):
    cumulative = decay_columns(decay_ref)
    sums = (sum_0[...] + sum_1[...]) + (sum_2[...] + sum_3[...])
    sums = jnp.concatenate([sums] * (HEAD_DIM // 8), axis=0).T
    inverse = 1.0 / jnp.sqrt(sums[:, 0:1] * (1.0 / (HEAD_TOTAL * HEAD_DIM)) + EPS)
    aligned = sums[:, 1:2] * inverse * (1.0 / (HEAD_TOTAL * HEAD_DIM))
    for h in range(HEADS):
        cols = head_cols(h)
        q, k = q_ref[:, cols], k_ref[:, cols]
        out = raw_ref[:, cols] * inverse
        out_ref[:, cols] = out
        raw_grad = ((g_ref[:, cols].astype(F32) - out * aligned) * inverse).astype(BF16)
        decay, scores = inner_terms(q, k, decay_ref, cumulative, h)
        head_decay = jnp.exp(cumulative[:, h : h + 1])
        inner_grad = (dot(raw_grad, v_ref[:, cols], 1, 1) * decay).astype(BF16)
        carried = dot(raw_grad, entry_ref[:, cols], 1, 1)
        dq_ref[:, cols] = dot(inner_grad, k, 1, 0) + head_decay * carried
        dk_ref[:, cols] = dot(inner_grad, q, 0, 0)
        dv_ref[:, cols] = dot(scores, raw_grad, 0, 0)
        scaled = (q.astype(F32) * head_decay).astype(BF16)
        read_ref[:, cols] = dot(scaled, raw_grad, 0, 0).astype(BF16)


def back_kernel(
    group_ref, index_ref, log_ref, read_ref, core_ref, from_1, from_2, from_3, handed_ref, part_ref
):
    logs = [log_ref[pl.ds(j, 1)] for j in range(LINE)]
    sources = [(read_ref, 0), (from_1, TOK), (from_2, TOK), (from_3, TOK)]
    sources += [(core_ref, NY * TOK)]
    sources += [(ref, TOK + HEAD_DIM) for ref in (from_1, from_2, from_3)]
    states = [
        functools.partial(lambda ref, row: ref[pl.ds(row, HEAD_DIM)].astype(F32), ref, row)
        for ref, row in sources
    ]
    keys = chain_keys(group_ref, index_ref, 0, False)
    handed, part, prefix = line_sums(keys, logs, states)
    handed_ref[...] = handed
    part_ref[pl.ds(0, HEAD_DIM)] = part
    part_ref[pl.ds(HEAD_DIM, 8)] = jnp.broadcast_to(prefix, (8, WIDTH))


def write_kernel(
    group_ref, index_ref, k_ref, v_ref, decay_ref, part_ref, log_ref, own, from_1, from_2, from_3,
    dk_in, dv_in, dk_ref, dv_ref,
):
    leave_all = part_ref[pl.ds(0, HEAD_DIM)] + total_sums(
        group_ref, index_ref, False, [t[...] for t in (own, from_1, from_2, from_3)],
        [log_ref[pl.ds(o, 1)] for o in range(NX)], part_ref[pl.ds(HEAD_DIM, 1)],
    )
    cumulative = decay_columns(decay_ref)
    tail = jnp.exp(cumulative[TOK - 1 : TOK] - cumulative)
    for h in range(HEADS):
        cols = head_cols(h)
        leave = leave_all[:, h * HEAD_DIM : (h + 1) * HEAD_DIM].astype(BF16)
        scale = tail[:, h : h + 1]
        dk_ref[:, cols] = dk_in[:, cols] + scale * dot(v_ref[:, cols], leave, 1, 1)
        dv_ref[:, cols] = dv_in[:, cols] + scale * dot(k_ref[:, cols], leave, 1, 0)


def in_vmem(n):
    return [pl.BlockSpec(memory_space=pltpu.VMEM)] * n


def on_device(
    group_of, soft_query, soft_key, soft_value, soft_grad,
    lin_query, lin_key, lin_value, log_decay, lin_grad,
):
    place = (group_of, lax.axis_index(SEQ).reshape(1))
    decay = log_decay.T

    kv_own = jnp.stack([soft_key, soft_value])
    kv = {0: kv_own, **{o: fetch(kv_own, "x", NX, o) for o in OFFSETS}}
    kvs = [kv[o] for o in range(NX)]
    packed = call(
        pack_kernel,
        shaped(PACK_ROWS, WIDTH, dtype=BF16),
        2**26,
        (soft_grad, lin_key, lin_value, decay),
        vmem=60,
    )
    q_from = {0: soft_query, **{o: fetch(soft_query, "y", NY, o) for o in OFFSETS}}
    g_from = {0: packed, **{o: fetch(packed, "y", NY, o) for o in OFFSETS}}
    qa = jnp.stack([q_from[o] for o in range(NY)])
    qb = fetch(qa, "c", NC, 1)
    ga = jnp.stack([g_from[o] for o in range(NY)])
    gb = fetch(ga, "c", NC, 1)

    out_a, stat_a = soft_forward(place, 0, qa, kvs)
    handed, entry_part, logs = call(
        states_kernel,
        [shaped(HEAD_DIM + 8, WIDTH), shaped(HEAD_DIM + 8, WIDTH), shaped(8, WIDTH)],
        2**24,
        (*place, ga, gb),
        **placed(in_vmem(2), in_vmem(3)),
    )
    totals = [handed, *(fetch(handed, "x", NX, o) for o in (1, 2, 3))]
    out_b, stat_b = soft_forward(place, 1, qb, kvs)
    part = call(
        delta_kernel,
        shaped(2, NY, 8, TOK),
        2**25,
        (ga, gb, out_a, out_b, stat_a, stat_b),
        grid=(HEADS,),
        in_specs=[rows_spec()] * 4 + [pl.BlockSpec((NY, 8, TOK), lambda h: (0, 0, 0))] * 2,
        out_specs=pl.BlockSpec((2, NY, 8, TOK), lambda h: (0, 0, 0, 0)),
    )
    other = fetch(part, "c", NC, 1)

    rows = shaped(TOK, WIDTH)
    raw, sums, entry, line_logs = call(
        read_kernel,
        [rows, shaped(8, TOK), shaped(HEAD_DIM, WIDTH, dtype=BF16), shaped(8, WIDTH)],
        2**27,
        (*place, lin_query, lin_key, lin_value, lin_grad, decay, entry_part, *totals),
        **placed(in_vmem(10), in_vmem(4)),
    )
    all_sums = [sums, *(fetch(sums, "head", NZ, o) for o in (1, 2, 3))]
    chip = call(chip_kernel, shaped(2, NY, 8, TOK), 2**20, (part, other))
    received = {o: fetch(chip, "y", NY, o) for o in OFFSETS}
    lin_out, lin_dq, dk_local, dv_local, read_grad = call(
        grad_kernel,
        [rows] * 4 + [shaped(HEAD_DIM, WIDTH, dtype=BF16)],
        2**28,
        (lin_query, lin_key, lin_value, lin_grad, decay, entry, raw, *all_sums),
    )
    stats, mine, theirs = call(
        line_kernel,
        [
            shaped(2, NY, 8, TOK),
            shaped(NY, TOK, WIDTH),
            shaped(NY * TOK + HEAD_DIM, WIDTH, dtype=BF16),
        ],
        2**22,
        (part, chip, received[1], received[2], received[3], out_a, out_b, read_grad),
    )
    from_core = fetch(theirs, "c", NC, 1)

    grads = far_backward(place, 0, 1, qa, qb, ga, gb, kvs[1:], stats)
    own_out, *pays = call(
        join_kernel,
        [rows] + [shaped(2 * TOK, WIDTH, dtype=BF16)] * 3,
        2**22,
        (mine, from_core, read_grad),
    )
    sent_out = {o: send(pays[o - 1], "y", NY, o) for o in OFFSETS}
    dq_a, dq_b, far_dkv = far_backward(place, 1, 2, qa, qb, ga, gb, kvs[1:], stats, tuple(grads))
    sent_dkv = [send(far_dkv[o - 1], "x", NX, o) for o in OFFSETS]
    dq_a, dq_b, near_dkv = near_backward(place, qa, qb, ga, gb, kvs[0], stats, dq_a, dq_b)
    dq_core = fetch(dq_b, "c", NC, 1)

    back_handed, leave_part = call(
        back_kernel,
        [shaped(HEAD_DIM, WIDTH), shaped(HEAD_DIM + 8, WIDTH)],
        2**24,
        (*place, logs, read_grad, from_core, *(sent_out[NY - o] for o in (1, 2, 3))),
        **placed(in_vmem(6), in_vmem(2)),
    )
    back_totals = [back_handed, *(fetch(back_handed, "x", NX, o) for o in (1, 2, 3))]
    chip_dq = dq_a.astype(F32) + dq_core.astype(F32)
    soft_dq = chip_dq[0]
    for o in OFFSETS:
        soft_dq = soft_dq + send(chip_dq[o].astype(BF16), "y", NY, o).astype(F32)
    lin_dk, lin_dv = call(
        write_kernel,
        [rows, rows],
        2**26,
        (*place, lin_key, lin_value, decay, leave_part, line_logs, *back_totals, dk_local, dv_local),
        **placed(in_vmem(11), in_vmem(2)),
    )
    soft_out = own_out
    for o in OFFSETS:
        soft_out = soft_out + sent_out[o][:TOK].astype(F32)
    dkv = near_dkv
    for sent in sent_dkv:
        dkv = dkv + sent.astype(F32)
    return (
        soft_out.astype(BF16), soft_dq.astype(BF16), dkv[0].astype(BF16), dkv[1].astype(BF16),
        lin_out, lin_dq, lin_dk, lin_dv,
    )


def solution(mesh):
    grid = Mesh(mesh.devices.reshape(NX, NY, NC, NZ), (*SEQ, "head"))
    block = P(SEQ, "head")

    return jax.shard_map(
        on_device,
        mesh=grid,
        in_specs=(P(),) + (block,) * 9,
        out_specs=(block,) * 8,
        check_vma=False,
    )
```

```python
import functools

import jax
import jax.numpy as jnp
from jax import lax
from jax.experimental import pallas as pl
from jax.experimental.pallas import tpu as pltpu
from jax.sharding import Mesh
from jax.sharding import PartitionSpec as P


HEAD_TOTAL = 12
HEAD_DIM = 128
HEADS = 3
WIDTH = HEADS * HEAD_DIM
TOK = 256
NX, NY, NC, NZ = 4, 4, 2, 4
LINE = NY * NC
EPS = 1e-06
SCALE = HEAD_DIM ** (-0.5)
LOG2E = 1.4426950408889634
NEG = -1e30
F32 = jnp.float32
BF16 = jnp.bfloat16
HIGHEST = lax.Precision.HIGHEST
SEQ = ("x", "y", "c")
OFFSETS = (1, 3, 2)
STATE_ROW = TOK
LOG_ROW = STATE_ROW + HEAD_DIM
PACK_ROWS = LOG_ROW + 16
ANY = pl.BlockSpec(memory_space=pl.ANY)


def send(block, axis, size, offset):
    return lax.ppermute(block, axis, [(i, (i + offset) % size) for i in range(size)])


def fetch(block, axis, size, offset):
    return send(block, axis, size, -offset)


def dot(a, b, dim_a, dim_b, precision=None):
    return lax.dot_general(
        a, b, (((dim_a,), (dim_b,)), ((), ())), precision=precision, preferred_element_type=F32
    )


def head_cols(h):
    return pl.ds(h * HEAD_DIM, HEAD_DIM)


def shaped(*dims, dtype=F32):
    return jax.ShapeDtypeStruct(dims, dtype)


def call(kernel, out_shape, flops, args, vmem=40, **kwargs):
    return pl.pallas_call(
        kernel,
        out_shape=out_shape,
        cost_estimate=pl.CostEstimate(flops=flops, transcendentals=2**18, bytes_accessed=2 * 2**20),
        compiler_params=pltpu.CompilerParams(vmem_limit_bytes=vmem * 2**20),
        **kwargs,
    )(*args)


def placed(in_specs, out_specs, scratch=(), grid=()):
    return {
        "grid_spec": pltpu.PrefetchScalarGridSpec(
            num_scalar_prefetch=2,
            grid=grid,
            in_specs=in_specs,
            out_specs=out_specs,
            scratch_shapes=list(scratch),
        )
    }


def position(group_ref, index_ref, along_x, side, along_y):
    index = index_ref[0]
    x, y, c = (index >> 3) + along_x, ((index >> 1) & 3) + along_y, (index & 1) + side
    return group_ref[(x & 3) * LINE + (y & 3) * NC + (c & 1)]


def flag(condition):
    return jnp.where(condition, 1, 0)


def causal(scores):
    row = lax.broadcasted_iota(jnp.int32, scores.shape, 0)
    col = lax.broadcasted_iota(jnp.int32, scores.shape, 1)
    return jnp.where(row <= col, scores, NEG)


def hidden(key_pos, query_pos):
    return jnp.where(key_pos > query_pos, -NEG, 0.0)


def staged(items, first, second):
    current = first(items[0])
    for i, item in enumerate(items):
        following = first(items[i + 1]) if i + 1 < len(items) else None
        second(item, current)
        current = following


def forward_kernel(
    side, group_ref, index_ref, q_ref, kv_0, kv_1, kv_2, kv_3, out_ref, stat_ref, k_ref, vt_ref
):
    h = pl.program_id(0)
    for o, kv_ref in enumerate((kv_0, kv_1, kv_2, kv_3)):
        k_ref[pl.ds(o * TOK, TOK)] = kv_ref[0]
        vt_ref[pl.ds(0, HEAD_DIM), pl.ds(o * TOK, TOK)] = kv_ref[1].T

    @pl.when(h == 0)
    def _():
        stat_ref[...] = jnp.zeros_like(stat_ref)
        vt_ref[pl.ds(HEAD_DIM, 16)] = jnp.ones((16, NX * TOK), BF16)

    key_pos = [position(group_ref, index_ref, o, 0, 0) for o in range(NX)]

    def scores(i):
        return [dot(k_ref[pl.ds(o * TOK, TOK)], q_ref[i], 1, 1) for o in range(NX)]

    def finish(i, parts):
        query_pos = position(group_ref, index_ref, 0, side, i)
        if side == 0 and i == 0:
            parts = [causal(parts[0]), *parts[1:]]
        hide = [hidden(p, query_pos) for p in key_pos]
        tops = [jnp.max(s, axis=0, keepdims=True) - x for s, x in zip(parts, hide)]
        top = functools.reduce(jnp.maximum, tops)
        probs = [
            jnp.exp2((s - (top + x)) * (SCALE * LOG2E)).astype(BF16) for s, x in zip(parts, hide)
        ]
        acc = dot(vt_ref[...], jnp.concatenate(probs), 1, 0)
        total = acc[HEAD_DIM : HEAD_DIM + 1]
        seen = top > 0.5 * NEG
        out_ref[i] = jnp.where(seen, acc[:HEAD_DIM] * (1.0 / total), 0.0).T.astype(BF16)
        log = top * (SCALE * LOG2E) + jnp.log(total) * LOG2E
        stat_ref[i, pl.ds(h, 1)] = jnp.where(seen, log, NEG)

    staged(range(NY), scores, finish)


def rows_spec(first=0):
    return pl.BlockSpec((NY, TOK, HEAD_DIM), lambda h, *_: (0, 0, h + first))


def pair_spec(first=0):
    return pl.BlockSpec((2, TOK, HEAD_DIM), lambda h, *_: (0, 0, h + first))


def soft_forward(place, side, q, kvs):
    return call(
        functools.partial(forward_kernel, side),
        [shaped(NY, TOK, WIDTH, dtype=BF16), shaped(NY, 8, TOK)],
        NY * NX * HEADS * 4 * TOK * TOK * HEAD_DIM,
        (*place, q, *kvs),
        **placed(
            [rows_spec()] + [pair_spec()] * NX,
            [rows_spec(), pl.BlockSpec((NY, 8, TOK), lambda h, *_: (0, 0, 0))],
            [
                pltpu.VMEM((NX * TOK, HEAD_DIM), BF16),
                pltpu.VMEM((HEAD_DIM + 16, NX * TOK), BF16),
            ],
            (HEADS,),
        ),
    )


def delta_kernel(g_a, g_b, out_a, out_b, stat_a, stat_b, part_ref):
    h = pl.program_id(0)

    @pl.when(h == 0)
    def _():
        part_ref[0] = stat_a[...]
        part_ref[1] = stat_b[...]

    for side, (g_ref, o_ref) in enumerate(((g_a, out_a), (g_b, out_b))):
        for i in range(NY):
            product = o_ref[i].astype(F32) * g_ref[i].astype(F32)
            part_ref[side, i, pl.ds(h + 4, 1)] = jnp.sum(product.T, axis=0, keepdims=True)


def far_kernel(
    first_head, group_ref, index_ref, qa_ref, qb_ref, ga_ref, gb_ref, kv_1, kv_2, kv_3, stat_ref,
    *refs,
):
    dqa_ref, dqb_ref, dkv_ref, k_ref, v_ref, kt_ref, acc_ref = refs[-7:]
    h = pl.program_id(0) + first_head
    tiles = [pl.ds(o * TOK, TOK) for o in range(NX - 1)]
    for tile, kv_ref in zip(tiles, (kv_1, kv_2, kv_3)):
        k_ref[tile] = kv_ref[0]
        v_ref[tile] = kv_ref[1]
        kt_ref[:, tile] = kv_ref[0].T
    key_pos = [position(group_ref, index_ref, o, 0, 0) for o in range(1, NX)]
    acc_ref[...] = jnp.zeros_like(acc_ref)

    def products(item):
        q_ref, g_ref, _, _, b = item
        return (
            [dot(k_ref[t], q_ref[b], 1, 1) for t in tiles],
            [dot(v_ref[t], g_ref[b], 1, 1) for t in tiles],
        )

    def finish(item, found):
        q_ref, g_ref, dq_ref, side, b = item
        query_pos = position(group_ref, index_ref, 0, side, b)
        lse = stat_ref[side, b, pl.ds(h, 1)]
        delta = stat_ref[side, b, pl.ds(h + 4, 1)]
        probs, grads = [], []
        for x, s, dprobs in zip(key_pos, *found):
            p = jnp.exp2(s * (SCALE * LOG2E) - (lse + hidden(x, query_pos)))
            probs.append(p.astype(BF16))
            grads.append((p * (dprobs - delta)).astype(BF16))
        probs, grads = jnp.concatenate(probs), jnp.concatenate(grads)
        acc_ref[0] += dot(grads, q_ref[b], 1, 0)
        acc_ref[1] += dot(probs, g_ref[b], 1, 0)
        dq_ref[b, 0] = dot(kt_ref[...], grads, 1, 0)

    items = [(qa_ref, ga_ref, dqa_ref, 0, b) for b in range(NY)]
    items += [(qb_ref, gb_ref, dqb_ref, 1, b) for b in range(NY)]
    staged(items, products, finish)
    for o, tile in enumerate(tiles):
        dkv_ref[o, 0] = (acc_ref[0, tile] * SCALE).astype(BF16)
        dkv_ref[o, 1] = acc_ref[1, tile].astype(BF16)


STAT_SPEC = pl.BlockSpec((2, NY, 8, TOK), lambda h, *_: (0, 0, 0, 0))


def far_backward(place, first, heads, qa, qb, ga, gb, kvs, stats, earlier=()):
    rows, pair = rows_spec(first), pair_spec(first)
    turned = pl.BlockSpec((NY, 1, HEAD_DIM, TOK), lambda h, *_: (0, h + first, 0, 0))
    dq_shape = shaped(NY, HEADS, HEAD_DIM, TOK)
    kwargs = placed(
        [rows] * 4 + [pair] * (NX - 1) + [STAT_SPEC] + [ANY] * len(earlier),
        [
            turned,
            turned,
            pl.BlockSpec((NX - 1, 2, TOK, HEAD_DIM), lambda h, *_: (0, 0, 0, h + first)),
        ],
        [
            pltpu.VMEM(((NX - 1) * TOK, HEAD_DIM), BF16),
            pltpu.VMEM(((NX - 1) * TOK, HEAD_DIM), BF16),
            pltpu.VMEM((HEAD_DIM, (NX - 1) * TOK), BF16),
            pltpu.VMEM((2, (NX - 1) * TOK, HEAD_DIM), F32),
        ],
        (heads,),
    )
    return call(
        functools.partial(far_kernel, first),
        [dq_shape, dq_shape, shaped(NX - 1, 2, TOK, WIDTH, dtype=BF16)],
        2 * NY * (NX - 1) * heads * 10 * TOK * TOK * HEAD_DIM,
        (*place, qa, qb, ga, gb, *kvs, stats, *earlier),
        input_output_aliases={10 + i: i for i in range(len(earlier))},
        **kwargs,
    )


def near_kernel(
    group_ref, index_ref, qa_ref, qb_ref, ga_ref, gb_ref, kv_ref, stat_ref, dqa_in, dqb_in,
    dqa_ref, dqb_ref, dkv_ref, kt_ref,
):
    h = pl.program_id(0)
    kt_ref[...] = kv_ref[0].T
    own = position(group_ref, index_ref, 0, 0, 0)

    def products(item):
        q_ref, g_ref, b = item[0], item[1], item[-1]
        return dot(kv_ref[0], q_ref[b], 1, 1), dot(kv_ref[1], g_ref[b], 1, 1)

    def finish(item, found):
        q_ref, g_ref, dq_in, dq_ref, side, b = item
        s, dprobs = found
        lse = stat_ref[side, b, pl.ds(h, 1)]
        delta = stat_ref[side, b, pl.ds(h + 4, 1)]
        s = s * (SCALE * LOG2E)
        start = side == 0 and b == 0
        if start:
            s = causal(s)
        p = jnp.exp2(s - (lse + hidden(own, position(group_ref, index_ref, 0, side, b))))
        ds = (p * (dprobs - delta)).astype(BF16)
        dq_sum = dq_in[b, 0] + dot(kt_ref[...], ds, 1, 0)
        dq_ref[b] = (dq_sum * SCALE).T.astype(BF16)
        dk, dv = dot(ds, q_ref[b], 1, 0) * SCALE, dot(p.astype(BF16), g_ref[b], 1, 0)
        dkv_ref[0] = dk if start else dkv_ref[0] + dk
        dkv_ref[1] = dv if start else dkv_ref[1] + dv

    sides = ((qa_ref, ga_ref, dqa_in, dqa_ref), (qb_ref, gb_ref, dqb_in, dqb_ref))
    items = [(*refs, side, b) for side, refs in enumerate(sides) for b in range(NY)]
    staged(items, products, finish)


def near_backward(place, qa, qb, ga, gb, kv, stats, dqa, dqb):
    rows, pair = rows_spec(), pair_spec()
    turned = pl.BlockSpec((NY, 1, HEAD_DIM, TOK), lambda h, *_: (0, h, 0, 0))
    return call(
        near_kernel,
        [
            shaped(NY, TOK, WIDTH, dtype=BF16),
            shaped(NY, TOK, WIDTH, dtype=BF16),
            shaped(2, TOK, WIDTH),
        ],
        2 * NY * HEADS * 10 * TOK * TOK * HEAD_DIM,
        (*place, qa, qb, ga, gb, kv, stats, dqa, dqb),
        **placed(
            [rows] * 4 + [pair, STAT_SPEC, turned, turned],
            [rows, rows, pair],
            [pltpu.VMEM((HEAD_DIM, TOK), BF16)],
            (HEADS,),
        ),
    )


def merged(stats_a, stats_b):
    lse_a, lse_b = stats_a[..., :4, :], stats_b[..., :4, :]
    top = jnp.maximum(lse_a, lse_b)
    weight_a, weight_b = jnp.exp2(lse_a - top), jnp.exp2(lse_b - top)
    total = weight_a + weight_b
    delta = (weight_a * stats_a[..., 4:, :] + weight_b * stats_b[..., 4:, :]) / total
    return jnp.concatenate([top + jnp.log(total) * LOG2E, delta], axis=-2)


def chip_kernel(part_ref, other_ref, out_ref):
    for side in range(2):
        out_ref[side] = merged(part_ref[side], other_ref[1 - side])


def line_kernel(
    part_ref, chip_ref, from_1, from_2, from_3, out_a_ref, out_b_ref, read_ref,
    stat_ref, mine_ref, theirs_ref,
):
    for side, o_ref in enumerate((out_a_ref, out_b_ref)):
        for i in range(NY):
            stats = chip_ref[side, i]
            for o, other in ((1, from_1), (2, from_2), (3, from_3)):
                stats = merged(stats, other[side, (i - o) % NY])
            stat_ref[side, i] = stats
            weight = jnp.exp2(part_ref[side, i, :4] - stats[:4])
            weight = jnp.concatenate([weight] * (HEAD_DIM // 4), axis=0).T
            for h in range(HEADS):
                scaled = o_ref[i, :, head_cols(h)].astype(F32) * weight[:, h : h + 1]
                if side == 0:
                    mine_ref[i, :, head_cols(h)] = scaled
                else:
                    theirs_ref[pl.ds(i * TOK, TOK), head_cols(h)] = scaled.astype(BF16)
    theirs_ref[pl.ds(NY * TOK, HEAD_DIM)] = read_ref[...]


def join_kernel(mine_ref, core_ref, read_ref, own_ref, pay_1, pay_2, pay_3):
    own_ref[...] = mine_ref[0] + core_ref[pl.ds(0, TOK)].astype(F32)
    for o, pay in ((1, pay_1), (2, pay_2), (3, pay_3)):
        total = mine_ref[o] + core_ref[pl.ds(o * TOK, TOK)].astype(F32)
        pay[pl.ds(0, TOK)] = total.astype(BF16)
        pay[pl.ds(TOK, HEAD_DIM)] = read_ref[...]
        pay[pl.ds(TOK + HEAD_DIM, HEAD_DIM)] = core_ref[pl.ds(NY * TOK, HEAD_DIM)]


def triangle(upper):
    row = lax.broadcasted_iota(jnp.int32, (TOK, TOK), 0)
    col = lax.broadcasted_iota(jnp.int32, (TOK, TOK), 1)
    return row <= col if upper else row >= col


def decay_columns(decay_ref):
    return dot(triangle(False).astype(F32), decay_ref[...], 1, 1, HIGHEST)


def log_pieces(log):
    log = jnp.broadcast_to(log, (16, log.shape[1]))
    row = lax.broadcasted_iota(jnp.int32, log.shape, 0)
    high = log.astype(BF16).astype(F32)
    middle = (log - high).astype(BF16).astype(F32)
    low = log - high - middle
    piece = jnp.where(row == 0, high, jnp.where(row == 1, middle, jnp.where(row == 2, low, 0.0)))
    return piece.astype(BF16)


def whole_log(pieces):
    pieces = pieces.astype(F32)
    return pieces[0:1] + pieces[1:2] + pieces[2:3]


def pack_kernel(g_ref, key_ref, value_ref, decay_ref, out_ref):
    cumulative = decay_columns(decay_ref)
    total = cumulative[TOK - 1 : TOK]
    tail = jnp.exp(total - cumulative)
    out_ref[pl.ds(0, TOK)] = g_ref[...]
    for h in range(HEADS):
        keys = key_ref[:, head_cols(h)].astype(F32) * tail[:, h : h + 1]
        state = dot(keys.astype(BF16), value_ref[:, head_cols(h)], 0, 0)
        out_ref[pl.ds(STATE_ROW, HEAD_DIM), head_cols(h)] = state.astype(BF16)
        log = jnp.broadcast_to(total[:, h : h + 1], (1, HEAD_DIM))
        out_ref[pl.ds(LOG_ROW, 16), head_cols(h)] = log_pieces(log)


def least(values):
    return functools.reduce(jnp.minimum, values)


def chain_keys(group_ref, index_ref, along_x, forward):
    found = [
        position(group_ref, index_ref, along_x, side, j) for side in range(NC) for j in range(NY)
    ]
    return found if forward else [31 - p for p in found]


def chain_members(keys):
    apart = -least([-k for k in keys]) - least(keys) > LINE - 1
    handed = [flag(jnp.logical_or(k < LINE, jnp.logical_not(apart))) for k in keys]
    whole = flag(jnp.logical_not(apart))
    same = [jnp.maximum(whole, flag(flag(k < LINE) == flag(keys[0] < LINE))) for k in keys]
    return handed, same


def line_sums(keys, logs, states):
    handed, same = chain_members(keys)
    before = [s * flag(k < keys[0]) for s, k in zip(same, keys)]

    def weighted(members):
        total = jnp.zeros((HEAD_DIM, WIDTH), F32)
        for j in range(LINE):
            exponent = jnp.zeros((1, WIDTH), F32)
            for i in range(LINE):
                if i != j:
                    between = members[i] * flag(keys[i] > keys[j])
                    exponent = exponent + logs[i] * between.astype(F32)
            weight = jnp.exp(exponent) * members[j].astype(F32)
            total = total + weight * states[j]()
        return total

    prefix = sum(log * b.astype(F32) for log, b in zip(logs, before))
    return weighted(handed), weighted(before), prefix


def total_sums(group_ref, index_ref, forward, totals, line_logs, prefix):
    lines = [chain_keys(group_ref, index_ref, o, forward) for o in range(NX)]
    starts = [least(keys) for keys in lines]
    same = chain_members(lines[0])[1]
    own_start = least([jnp.where(s > 0, k, 99) for s, k in zip(same, lines[0])])
    earlier = [flag(s < own_start) for s in starts]
    result = jnp.zeros((HEAD_DIM, WIDTH), F32)
    for o in range(NX):
        exponent = prefix
        for i in range(NX):
            if i != o:
                between = earlier[i] * flag(starts[i] > starts[o])
                exponent = exponent + line_logs[i] * between.astype(F32)
        result = result + jnp.exp(exponent) * earlier[o].astype(F32) * totals[o].astype(F32)
    return result


def states_kernel(group_ref, index_ref, ga_ref, gb_ref, handed_ref, entry_ref, log_ref):
    logs, states = [], []
    for ref in (ga_ref, gb_ref):
        for i in range(NY):
            logs.append(whole_log(ref[i, pl.ds(LOG_ROW, 16)]))
            states.append(
                functools.partial(
                    lambda ref, i: ref[i, pl.ds(STATE_ROW, HEAD_DIM)].astype(F32), ref, i
                )
            )
    keys = chain_keys(group_ref, index_ref, 0, True)
    handed, entry, prefix = line_sums(keys, logs, states)
    handed_ref[pl.ds(0, HEAD_DIM)] = handed.astype(BF16)
    handed_ref[pl.ds(HEAD_DIM, 16)] = log_pieces(sum(logs))
    entry_ref[pl.ds(0, HEAD_DIM)] = entry
    entry_ref[pl.ds(HEAD_DIM, 8)] = jnp.broadcast_to(prefix, (8, WIDTH))
    for j in range(LINE):
        log_ref[pl.ds(j, 1)] = logs[j]


def decay_rows(decay_ref):
    return dot(decay_ref[...], triangle(True).astype(F32), 1, 0, HIGHEST)


def inner_terms(q, k, rows, cumulative, h):
    gap = cumulative[:, h : h + 1] - rows[h : h + 1]
    decay = jnp.where(triangle(False), jnp.exp(jnp.minimum(gap, 0.0)), 0.0)
    return decay, (dot(q, k, 1, 1) * decay).astype(BF16)


def read_kernel(
    group_ref, index_ref, q_ref, k_ref, v_ref, g_ref, decay_ref, part_ref, own, from_1, from_2,
    from_3, raw_ref, sum_ref, entry_ref, log_ref,
):
    all_totals = (own, from_1, from_2, from_3)
    line_logs = [whole_log(t[pl.ds(HEAD_DIM, 16)]) for t in all_totals]
    for o in range(NX):
        log_ref[pl.ds(o, 1)] = line_logs[o]
    log_ref[pl.ds(NX, 4)] = jnp.zeros((4, WIDTH), F32)
    entry = part_ref[pl.ds(0, HEAD_DIM)] + total_sums(
        group_ref, index_ref, True, [t[pl.ds(0, HEAD_DIM)] for t in all_totals], line_logs,
        part_ref[pl.ds(HEAD_DIM, 1)],
    )
    entry_ref[...] = entry.astype(BF16)
    cumulative, decay_in_rows = decay_columns(decay_ref), decay_rows(decay_ref)
    squares = jnp.zeros((TOK, 1), F32)
    inner = jnp.zeros((TOK, 1), F32)
    for h in range(HEADS):
        cols = head_cols(h)
        q = q_ref[:, cols]
        scores = inner_terms(q, k_ref[:, cols], decay_in_rows, cumulative, h)[1]
        carried = dot(q, entry_ref[:, cols], 1, 0)
        raw = dot(scores, v_ref[:, cols], 1, 0) + jnp.exp(cumulative[:, h : h + 1]) * carried
        raw_ref[:, cols] = raw
        squares = squares + jnp.sum(raw * raw, axis=1, keepdims=True)
        inner = inner + jnp.sum(raw * g_ref[:, cols].astype(F32), axis=1, keepdims=True)
    lane = lax.broadcasted_iota(jnp.int32, (TOK, HEAD_DIM), 1)
    sums = jnp.where(lane == 0, squares, jnp.where(lane == 1, inner, 0.0))
    sum_ref[...] = sums.T[:8]


def grad_kernel(
    q_ref, k_ref, v_ref, g_ref, decay_ref, entry_ref, raw_ref, sum_0, sum_1, sum_2, sum_3,
    out_ref, dq_ref, dk_ref, dv_ref, read_ref,
):
    cumulative, decay_in_rows = decay_columns(decay_ref), decay_rows(decay_ref)
    sums = (sum_0[...] + sum_1[...]) + (sum_2[...] + sum_3[...])
    sums = jnp.concatenate([sums] * (HEAD_DIM // 8), axis=0).T
    inverse = 1.0 / jnp.sqrt(sums[:, 0:1] * (1.0 / (HEAD_TOTAL * HEAD_DIM)) + EPS)
    aligned = sums[:, 1:2] * inverse * (1.0 / (HEAD_TOTAL * HEAD_DIM))
    for h in range(HEADS):
        cols = head_cols(h)
        q, k = q_ref[:, cols], k_ref[:, cols]
        out = raw_ref[:, cols] * inverse
        out_ref[:, cols] = out
        raw_grad = ((g_ref[:, cols].astype(F32) - out * aligned) * inverse).astype(BF16)
        decay, scores = inner_terms(q, k, decay_in_rows, cumulative, h)
        head_decay = jnp.exp(cumulative[:, h : h + 1])
        inner_grad = (dot(raw_grad, v_ref[:, cols], 1, 1) * decay).astype(BF16)
        carried = dot(raw_grad, entry_ref[:, cols], 1, 1)
        dq_ref[:, cols] = dot(inner_grad, k, 1, 0) + head_decay * carried
        dk_ref[:, cols] = dot(inner_grad, q, 0, 0)
        dv_ref[:, cols] = dot(scores, raw_grad, 0, 0)
        scaled = (q.astype(F32) * head_decay).astype(BF16)
        read_ref[:, cols] = dot(scaled, raw_grad, 0, 0).astype(BF16)


def back_kernel(
    group_ref, index_ref, log_ref, read_ref, core_ref, from_1, from_2, from_3, handed_ref, part_ref
):
    logs = [log_ref[pl.ds(j, 1)] for j in range(LINE)]
    sources = [(read_ref, 0), (from_1, TOK), (from_2, TOK), (from_3, TOK)]
    sources += [(core_ref, NY * TOK)]
    sources += [(ref, TOK + HEAD_DIM) for ref in (from_1, from_2, from_3)]
    states = [
        functools.partial(lambda ref, row: ref[pl.ds(row, HEAD_DIM)].astype(F32), ref, row)
        for ref, row in sources
    ]
    keys = chain_keys(group_ref, index_ref, 0, False)
    handed, part, prefix = line_sums(keys, logs, states)
    handed_ref[...] = handed.astype(BF16)
    part_ref[pl.ds(0, HEAD_DIM)] = part
    part_ref[pl.ds(HEAD_DIM, 8)] = jnp.broadcast_to(prefix, (8, WIDTH))


def write_kernel(
    group_ref, index_ref, k_ref, v_ref, decay_ref, part_ref, log_ref, own, from_1, from_2, from_3,
    dk_in, dv_in, dk_ref, dv_ref,
):
    leave_all = part_ref[pl.ds(0, HEAD_DIM)] + total_sums(
        group_ref, index_ref, False, [t[...] for t in (own, from_1, from_2, from_3)],
        [log_ref[pl.ds(o, 1)] for o in range(NX)], part_ref[pl.ds(HEAD_DIM, 1)],
    )
    cumulative = decay_columns(decay_ref)
    tail = jnp.exp(cumulative[TOK - 1 : TOK] - cumulative)
    for h in range(HEADS):
        cols = head_cols(h)
        leave = leave_all[:, h * HEAD_DIM : (h + 1) * HEAD_DIM].astype(BF16)
        scale = tail[:, h : h + 1]
        dk_ref[:, cols] = dk_in[:, cols] + scale * dot(v_ref[:, cols], leave, 1, 1)
        dv_ref[:, cols] = dv_in[:, cols] + scale * dot(k_ref[:, cols], leave, 1, 0)


def in_vmem(n):
    return [pl.BlockSpec(memory_space=pltpu.VMEM)] * n


def on_device(
    group_of, soft_query, soft_key, soft_value, soft_grad,
    lin_query, lin_key, lin_value, log_decay, lin_grad,
):
    place = (group_of, lax.axis_index(SEQ).reshape(1))
    decay = log_decay.T

    kv_own = jnp.stack([soft_key, soft_value])
    kv = {0: kv_own, **{o: fetch(kv_own, "x", NX, o) for o in OFFSETS}}
    kvs = [kv[o] for o in range(NX)]
    packed = call(
        pack_kernel,
        shaped(PACK_ROWS, WIDTH, dtype=BF16),
        2**26,
        (soft_grad, lin_key, lin_value, decay),
    )
    q_from = {0: soft_query, **{o: fetch(soft_query, "y", NY, o) for o in OFFSETS}}
    g_from = {0: packed, **{o: fetch(packed, "y", NY, o) for o in OFFSETS}}
    qa = jnp.stack([q_from[o] for o in range(NY)])
    qb = fetch(qa, "c", NC, 1)
    ga = jnp.stack([g_from[o] for o in range(NY)])
    gb = fetch(ga, "c", NC, 1)

    out_a, stat_a = soft_forward(place, 0, qa, kvs)
    handed, entry_part, logs = call(
        states_kernel,
        [
            shaped(HEAD_DIM + 16, WIDTH, dtype=BF16),
            shaped(HEAD_DIM + 8, WIDTH),
            shaped(8, WIDTH),
        ],
        2**24,
        (*place, ga, gb),
        **placed(in_vmem(2), in_vmem(3)),
    )
    totals = [handed, *(fetch(handed, "x", NX, o) for o in (1, 2, 3))]
    out_b, stat_b = soft_forward(place, 1, qb, kvs)
    part = call(
        delta_kernel,
        shaped(2, NY, 8, TOK),
        2**25,
        (ga, gb, out_a, out_b, stat_a, stat_b),
        grid=(HEADS,),
        in_specs=[rows_spec()] * 4 + [pl.BlockSpec((NY, 8, TOK), lambda h: (0, 0, 0))] * 2,
        out_specs=pl.BlockSpec((2, NY, 8, TOK), lambda h: (0, 0, 0, 0)),
    )
    other = fetch(part, "c", NC, 1)

    rows = shaped(TOK, WIDTH)
    raw, sums, entry, line_logs = call(
        read_kernel,
        [rows, shaped(8, TOK), shaped(HEAD_DIM, WIDTH, dtype=BF16), shaped(8, WIDTH)],
        2**27,
        (*place, lin_query, lin_key, lin_value, lin_grad, decay, entry_part, *totals),
        **placed(in_vmem(10), in_vmem(4)),
    )
    all_sums = [sums, *(fetch(sums, "head", NZ, o) for o in (1, 2, 3))]
    chip = call(chip_kernel, shaped(2, NY, 8, TOK), 2**20, (part, other))
    received = {o: fetch(chip, "y", NY, o) for o in OFFSETS}
    lin_out, lin_dq, dk_local, dv_local, read_grad = call(
        grad_kernel,
        [rows] * 4 + [shaped(HEAD_DIM, WIDTH, dtype=BF16)],
        2**28,
        (lin_query, lin_key, lin_value, lin_grad, decay, entry, raw, *all_sums),
    )
    stats, mine, theirs = call(
        line_kernel,
        [
            shaped(2, NY, 8, TOK),
            shaped(NY, TOK, WIDTH),
            shaped(NY * TOK + HEAD_DIM, WIDTH, dtype=BF16),
        ],
        2**22,
        (part, chip, received[1], received[2], received[3], out_a, out_b, read_grad),
    )
    from_core = fetch(theirs, "c", NC, 1)

    grads = far_backward(place, 0, 1, qa, qb, ga, gb, kvs[1:], stats)
    own_out, *pays = call(
        join_kernel,
        [rows] + [shaped(2 * TOK, WIDTH, dtype=BF16)] * 3,
        2**22,
        (mine, from_core, read_grad),
    )
    sent_out = {o: send(pays[o - 1], "y", NY, o) for o in OFFSETS}
    dq_a, dq_b, far_dkv = far_backward(place, 1, 2, qa, qb, ga, gb, kvs[1:], stats, tuple(grads))
    sent_dkv = [send(far_dkv[o - 1], "x", NX, o) for o in OFFSETS]
    dq_a, dq_b, near_dkv = near_backward(place, qa, qb, ga, gb, kvs[0], stats, dq_a, dq_b)
    dq_core = fetch(dq_b, "c", NC, 1)

    back_handed, leave_part = call(
        back_kernel,
        [shaped(HEAD_DIM, WIDTH, dtype=BF16), shaped(HEAD_DIM + 8, WIDTH)],
        2**24,
        (*place, logs, read_grad, from_core, *(sent_out[NY - o] for o in (1, 2, 3))),
        **placed(in_vmem(6), in_vmem(2)),
    )
    back_totals = [back_handed, *(fetch(back_handed, "x", NX, o) for o in (1, 2, 3))]
    chip_dq = dq_a.astype(F32) + dq_core.astype(F32)
    soft_dq = chip_dq[0]
    for o in OFFSETS:
        soft_dq = soft_dq + send(chip_dq[o].astype(BF16), "y", NY, o).astype(F32)
    lin_dk, lin_dv = call(
        write_kernel,
        [rows, rows],
        2**26,
        (*place, lin_key, lin_value, decay, leave_part, line_logs, *back_totals, dk_local, dv_local),
        **placed(in_vmem(11), in_vmem(2)),
    )
    soft_out = own_out
    for o in OFFSETS:
        soft_out = soft_out + sent_out[o][:TOK].astype(F32)
    dkv = near_dkv
    for sent in sent_dkv:
        dkv = dkv + sent.astype(F32)
    return (
        soft_out.astype(BF16), soft_dq.astype(BF16), dkv[0].astype(BF16), dkv[1].astype(BF16),
        lin_out, lin_dq, lin_dk, lin_dv,
    )


def solution(mesh):
    grid = Mesh(mesh.devices.reshape(NX, NY, NC, NZ), (*SEQ, "head"))
    block = P(SEQ, "head")

    return jax.shard_map(
        on_device,
        mesh=grid,
        in_specs=(P(),) + (block,) * 9,
        out_specs=(block,) * 8,
        check_vma=False,
    )
```

```python
import functools

import jax
import jax.numpy as jnp
from jax import lax
from jax.experimental import pallas as pl
from jax.experimental.pallas import tpu as pltpu
from jax.sharding import Mesh
from jax.sharding import PartitionSpec as P


HEAD_TOTAL = 12
HEAD_DIM = 128
HEADS = 3
WIDTH = HEADS * HEAD_DIM
TOK = 256
NX, NY, NC, NZ = 4, 4, 2, 4
LINE = NY * NC
EPS = 1e-06
SCALE = HEAD_DIM ** (-0.5)
LOG2E = 1.4426950408889634
NEG = -1e30
F32 = jnp.float32
BF16 = jnp.bfloat16
HIGHEST = lax.Precision.HIGHEST
SEQ = ("x", "y", "c")
OFFSETS = (1, 3, 2)
STATE_ROW = TOK
LOG_ROW = STATE_ROW + HEAD_DIM
PACK_ROWS = LOG_ROW + 16
ANY = pl.BlockSpec(memory_space=pl.ANY)


def send(block, axis, size, offset):
    return lax.ppermute(block, axis, [(i, (i + offset) % size) for i in range(size)])


def fetch(block, axis, size, offset):
    return send(block, axis, size, -offset)


def dot(a, b, dim_a, dim_b, precision=None):
    return lax.dot_general(
        a, b, (((dim_a,), (dim_b,)), ((), ())), precision=precision, preferred_element_type=F32
    )


def head_cols(h):
    return pl.ds(h * HEAD_DIM, HEAD_DIM)


def shaped(*dims, dtype=F32):
    return jax.ShapeDtypeStruct(dims, dtype)


def call(kernel, out_shape, flops, args, vmem=40, **kwargs):
    return pl.pallas_call(
        kernel,
        out_shape=out_shape,
        cost_estimate=pl.CostEstimate(flops=flops, transcendentals=2**18, bytes_accessed=2 * 2**20),
        compiler_params=pltpu.CompilerParams(vmem_limit_bytes=vmem * 2**20),
        **kwargs,
    )(*args)


def placed(in_specs, out_specs, scratch=(), grid=()):
    return {
        "grid_spec": pltpu.PrefetchScalarGridSpec(
            num_scalar_prefetch=2,
            grid=grid,
            in_specs=in_specs,
            out_specs=out_specs,
            scratch_shapes=list(scratch),
        )
    }


def position(group_ref, index_ref, along_x, side, along_y):
    index = index_ref[0]
    x, y, c = (index >> 3) + along_x, ((index >> 1) & 3) + along_y, (index & 1) + side
    return group_ref[(x & 3) * LINE + (y & 3) * NC + (c & 1)]


def flag(condition):
    return jnp.where(condition, 1, 0)


def causal(scores):
    row = lax.broadcasted_iota(jnp.int32, scores.shape, 0)
    col = lax.broadcasted_iota(jnp.int32, scores.shape, 1)
    return jnp.where(row <= col, scores, NEG)


def hidden(key_pos, query_pos):
    return jnp.where(key_pos > query_pos, -NEG, 0.0)


def staged(items, first, second):
    current = first(items[0])
    for i, item in enumerate(items):
        following = first(items[i + 1]) if i + 1 < len(items) else None
        second(item, current)
        current = following


def forward_kernel(
    side, group_ref, index_ref, q_ref, kv_0, kv_1, kv_2, kv_3, out_ref, stat_ref, k_ref, vt_ref
):
    h = pl.program_id(0)
    for o, kv_ref in enumerate((kv_0, kv_1, kv_2, kv_3)):
        k_ref[pl.ds(o * TOK, TOK)] = kv_ref[0]
        vt_ref[pl.ds(0, HEAD_DIM), pl.ds(o * TOK, TOK)] = kv_ref[1].T

    @pl.when(h == 0)
    def _():
        stat_ref[...] = jnp.zeros_like(stat_ref)
        vt_ref[pl.ds(HEAD_DIM, 16)] = jnp.ones((16, NX * TOK), BF16)

    key_pos = [position(group_ref, index_ref, o, 0, 0) for o in range(NX)]

    def scores(i):
        return [dot(k_ref[pl.ds(o * TOK, TOK)], q_ref[i], 1, 1) for o in range(NX)]

    def finish(i, parts):
        query_pos = position(group_ref, index_ref, 0, side, i)
        if side == 0 and i == 0:
            parts = [causal(parts[0]), *parts[1:]]
        hide = [hidden(p, query_pos) for p in key_pos]
        tops = [jnp.max(s, axis=0, keepdims=True) - x for s, x in zip(parts, hide)]
        top = functools.reduce(jnp.maximum, tops)
        probs = [
            jnp.exp2((s - (top + x)) * (SCALE * LOG2E)).astype(BF16) for s, x in zip(parts, hide)
        ]
        acc = dot(vt_ref[...], jnp.concatenate(probs), 1, 0)
        total = acc[HEAD_DIM : HEAD_DIM + 1]
        seen = top > 0.5 * NEG
        out_ref[i] = jnp.where(seen, acc[:HEAD_DIM] * (1.0 / total), 0.0).T.astype(BF16)
        log = top * (SCALE * LOG2E) + jnp.log(total) * LOG2E
        stat_ref[i, pl.ds(h, 1)] = jnp.where(seen, log, NEG)

    staged(range(NY), scores, finish)


def rows_spec(first=0):
    return pl.BlockSpec((NY, TOK, HEAD_DIM), lambda h, *_: (0, 0, h + first))


def pair_spec(first=0):
    return pl.BlockSpec((2, TOK, HEAD_DIM), lambda h, *_: (0, 0, h + first))


def soft_forward(place, side, q, kvs):
    return call(
        functools.partial(forward_kernel, side),
        [shaped(NY, TOK, WIDTH, dtype=BF16), shaped(NY, 8, TOK)],
        NY * NX * HEADS * 4 * TOK * TOK * HEAD_DIM,
        (*place, q, *kvs),
        **placed(
            [rows_spec()] + [pair_spec()] * NX,
            [rows_spec(), pl.BlockSpec((NY, 8, TOK), lambda h, *_: (0, 0, 0))],
            [
                pltpu.VMEM((NX * TOK, HEAD_DIM), BF16),
                pltpu.VMEM((HEAD_DIM + 16, NX * TOK), BF16),
            ],
            (HEADS,),
        ),
    )


def delta_kernel(g_a, g_b, out_a, out_b, stat_a, stat_b, part_ref):
    h = pl.program_id(0)

    @pl.when(h == 0)
    def _():
        part_ref[0] = stat_a[...]
        part_ref[1] = stat_b[...]

    for side, (g_ref, o_ref) in enumerate(((g_a, out_a), (g_b, out_b))):
        for i in range(NY):
            product = o_ref[i].astype(F32) * g_ref[i].astype(F32)
            part_ref[side, i, pl.ds(h + 4, 1)] = jnp.sum(product.T, axis=0, keepdims=True)


def far_kernel(
    first_head, group_ref, index_ref, qa_ref, qb_ref, ga_ref, gb_ref, kv_1, kv_2, kv_3, stat_ref,
    *refs,
):
    dqa_ref, dqb_ref, dkv_ref, k_ref, v_ref, kt_ref, acc_ref = refs[-7:]
    h = pl.program_id(0) + first_head
    tiles = [pl.ds(o * TOK, TOK) for o in range(NX - 1)]
    for tile, kv_ref in zip(tiles, (kv_1, kv_2, kv_3)):
        k_ref[tile] = kv_ref[0]
        v_ref[tile] = kv_ref[1]
        kt_ref[:, tile] = kv_ref[0].T
    key_pos = [position(group_ref, index_ref, o, 0, 0) for o in range(1, NX)]
    acc_ref[...] = jnp.zeros_like(acc_ref)

    def products(item):
        q_ref, g_ref, _, _, b = item
        return (
            [dot(k_ref[t], q_ref[b], 1, 1) for t in tiles],
            [dot(v_ref[t], g_ref[b], 1, 1) for t in tiles],
        )

    def finish(item, found):
        q_ref, g_ref, dq_ref, side, b = item
        query_pos = position(group_ref, index_ref, 0, side, b)
        lse = stat_ref[side, b, pl.ds(h, 1)]
        delta = stat_ref[side, b, pl.ds(h + 4, 1)]
        probs, grads = [], []
        for x, s, dprobs in zip(key_pos, *found):
            p = jnp.exp2(s * (SCALE * LOG2E) - (lse + hidden(x, query_pos)))
            probs.append(p.astype(BF16))
            grads.append((p * (dprobs - delta)).astype(BF16))
        probs, grads = jnp.concatenate(probs), jnp.concatenate(grads)
        acc_ref[0] += dot(grads, q_ref[b], 1, 0)
        acc_ref[1] += dot(probs, g_ref[b], 1, 0)
        dq_ref[b, 0] = dot(kt_ref[...], grads, 1, 0)

    items = [(qa_ref, ga_ref, dqa_ref, 0, b) for b in range(NY)]
    items += [(qb_ref, gb_ref, dqb_ref, 1, b) for b in range(NY)]
    staged(items, products, finish)
    for o, tile in enumerate(tiles):
        dkv_ref[o, 0] = (acc_ref[0, tile] * SCALE).astype(BF16)
        dkv_ref[o, 1] = acc_ref[1, tile].astype(BF16)


STAT_SPEC = pl.BlockSpec((2, NY, 8, TOK), lambda h, *_: (0, 0, 0, 0))


def far_backward(place, first, heads, qa, qb, ga, gb, kvs, stats, earlier=()):
    rows, pair = rows_spec(first), pair_spec(first)
    turned = pl.BlockSpec((NY, 1, HEAD_DIM, TOK), lambda h, *_: (0, h + first, 0, 0))
    dq_shape = shaped(NY, HEADS, HEAD_DIM, TOK)
    kwargs = placed(
        [rows] * 4 + [pair] * (NX - 1) + [STAT_SPEC] + [ANY] * len(earlier),
        [
            turned,
            turned,
            pl.BlockSpec((NX - 1, 2, TOK, HEAD_DIM), lambda h, *_: (0, 0, 0, h + first)),
        ],
        [
            pltpu.VMEM(((NX - 1) * TOK, HEAD_DIM), BF16),
            pltpu.VMEM(((NX - 1) * TOK, HEAD_DIM), BF16),
            pltpu.VMEM((HEAD_DIM, (NX - 1) * TOK), BF16),
            pltpu.VMEM((2, (NX - 1) * TOK, HEAD_DIM), F32),
        ],
        (heads,),
    )
    return call(
        functools.partial(far_kernel, first),
        [dq_shape, dq_shape, shaped(NX - 1, 2, TOK, WIDTH, dtype=BF16)],
        2 * NY * (NX - 1) * heads * 10 * TOK * TOK * HEAD_DIM,
        (*place, qa, qb, ga, gb, *kvs, stats, *earlier),
        input_output_aliases={10 + i: i for i in range(len(earlier))},
        **kwargs,
    )


def near_kernel(
    group_ref, index_ref, qa_ref, qb_ref, ga_ref, gb_ref, kv_ref, stat_ref, dqa_in, dqb_in,
    dqa_ref, dqb_ref, dkv_ref, kt_ref,
):
    h = pl.program_id(0)
    kt_ref[...] = kv_ref[0].T
    own = position(group_ref, index_ref, 0, 0, 0)

    def products(item):
        q_ref, g_ref, b = item[0], item[1], item[-1]
        return dot(kv_ref[0], q_ref[b], 1, 1), dot(kv_ref[1], g_ref[b], 1, 1)

    def finish(item, found):
        q_ref, g_ref, dq_in, dq_ref, side, b = item
        s, dprobs = found
        lse = stat_ref[side, b, pl.ds(h, 1)]
        delta = stat_ref[side, b, pl.ds(h + 4, 1)]
        s = s * (SCALE * LOG2E)
        start = side == 0 and b == 0
        if start:
            s = causal(s)
        p = jnp.exp2(s - (lse + hidden(own, position(group_ref, index_ref, 0, side, b))))
        ds = (p * (dprobs - delta)).astype(BF16)
        dq_sum = dq_in[b, 0] + dot(kt_ref[...], ds, 1, 0)
        dq_ref[b] = (dq_sum * SCALE).T.astype(BF16)
        dk, dv = dot(ds, q_ref[b], 1, 0) * SCALE, dot(p.astype(BF16), g_ref[b], 1, 0)
        dkv_ref[0] = dk if start else dkv_ref[0] + dk
        dkv_ref[1] = dv if start else dkv_ref[1] + dv

    sides = ((qa_ref, ga_ref, dqa_in, dqa_ref), (qb_ref, gb_ref, dqb_in, dqb_ref))
    items = [(*refs, side, b) for side, refs in enumerate(sides) for b in range(NY)]
    staged(items, products, finish)


def near_backward(place, qa, qb, ga, gb, kv, stats, dqa, dqb):
    rows, pair = rows_spec(), pair_spec()
    turned = pl.BlockSpec((NY, 1, HEAD_DIM, TOK), lambda h, *_: (0, h, 0, 0))
    return call(
        near_kernel,
        [
            shaped(NY, TOK, WIDTH, dtype=BF16),
            shaped(NY, TOK, WIDTH, dtype=BF16),
            shaped(2, TOK, WIDTH),
        ],
        2 * NY * HEADS * 10 * TOK * TOK * HEAD_DIM,
        (*place, qa, qb, ga, gb, kv, stats, dqa, dqb),
        **placed(
            [rows] * 4 + [pair, STAT_SPEC, turned, turned],
            [rows, rows, pair],
            [pltpu.VMEM((HEAD_DIM, TOK), BF16)],
            (HEADS,),
        ),
    )


def merged(stats_a, stats_b):
    lse_a, lse_b = stats_a[..., :4, :], stats_b[..., :4, :]
    top = jnp.maximum(lse_a, lse_b)
    weight_a, weight_b = jnp.exp2(lse_a - top), jnp.exp2(lse_b - top)
    total = weight_a + weight_b
    delta = (weight_a * stats_a[..., 4:, :] + weight_b * stats_b[..., 4:, :]) / total
    return jnp.concatenate([top + jnp.log(total) * LOG2E, delta], axis=-2)


def chip_kernel(part_ref, other_ref, out_ref):
    for side in range(2):
        out_ref[side] = merged(part_ref[side], other_ref[1 - side])


def line_kernel(
    part_ref, chip_ref, from_1, from_2, from_3, out_a_ref, out_b_ref,
    stat_ref, mine_ref, theirs_ref,
):
    for side, o_ref in enumerate((out_a_ref, out_b_ref)):
        for i in range(NY):
            stats = chip_ref[side, i]
            for o, other in ((1, from_1), (2, from_2), (3, from_3)):
                stats = merged(stats, other[side, (i - o) % NY])
            stat_ref[side, i] = stats
            weight = jnp.exp2(part_ref[side, i, :4] - stats[:4])
            weight = jnp.concatenate([weight] * (HEAD_DIM // 4), axis=0).T
            for h in range(HEADS):
                scaled = o_ref[i, :, head_cols(h)].astype(F32) * weight[:, h : h + 1]
                if side == 0:
                    mine_ref[i, :, head_cols(h)] = scaled
                else:
                    theirs_ref[pl.ds(i * TOK, TOK), head_cols(h)] = scaled.astype(BF16)


def join_kernel(mine_ref, core_ref, read_ref, pair_ref, own_ref, pay_1, pay_2, pay_3):
    own_ref[...] = mine_ref[0] + core_ref[pl.ds(0, TOK)].astype(F32)
    for o, pay in ((1, pay_1), (2, pay_2), (3, pay_3)):
        total = mine_ref[o] + core_ref[pl.ds(o * TOK, TOK)].astype(F32)
        pay[pl.ds(0, TOK)] = total.astype(BF16)
        pay[pl.ds(TOK, HEAD_DIM)] = read_ref[...]
        pay[pl.ds(TOK + HEAD_DIM, HEAD_DIM)] = pair_ref[...]


def triangle(upper):
    row = lax.broadcasted_iota(jnp.int32, (TOK, TOK), 0)
    col = lax.broadcasted_iota(jnp.int32, (TOK, TOK), 1)
    return row <= col if upper else row >= col


def decay_columns(decay):
    return dot(triangle(False).astype(F32), decay[...], 1, 1, HIGHEST)


def log_pieces(log):
    log = jnp.broadcast_to(log, (16, log.shape[1]))
    row = lax.broadcasted_iota(jnp.int32, log.shape, 0)
    high = log.astype(BF16).astype(F32)
    middle = (log - high).astype(BF16).astype(F32)
    low = log - high - middle
    piece = jnp.where(row == 0, high, jnp.where(row == 1, middle, jnp.where(row == 2, low, 0.0)))
    return piece.astype(BF16)


def whole_log(pieces):
    pieces = pieces.astype(F32)
    return pieces[0:1] + pieces[1:2] + pieces[2:3]


def pack_kernel(g_ref, key_ref, value_ref, decay_ref, out_ref):
    cumulative = decay_columns(decay_ref)
    total = cumulative[TOK - 1 : TOK]
    tail = jnp.exp(total - cumulative)
    out_ref[pl.ds(0, TOK)] = g_ref[...]
    for h in range(HEADS):
        keys = key_ref[:, head_cols(h)].astype(F32) * tail[:, h : h + 1]
        state = dot(keys.astype(BF16), value_ref[:, head_cols(h)], 0, 0)
        out_ref[pl.ds(STATE_ROW, HEAD_DIM), head_cols(h)] = state.astype(BF16)
        log = jnp.broadcast_to(total[:, h : h + 1], (1, HEAD_DIM))
        out_ref[pl.ds(LOG_ROW, 16), head_cols(h)] = log_pieces(log)


def least(values):
    return functools.reduce(jnp.minimum, values)


def chain_keys(group_ref, index_ref, along_x, forward):
    found = [
        position(group_ref, index_ref, along_x, side, j) for side in range(NC) for j in range(NY)
    ]
    return found if forward else [31 - p for p in found]


def chain_members(keys):
    apart = -least([-k for k in keys]) - least(keys) > LINE - 1
    handed = [flag(jnp.logical_or(k < LINE, jnp.logical_not(apart))) for k in keys]
    whole = flag(jnp.logical_not(apart))
    same = [jnp.maximum(whole, flag(flag(k < LINE) == flag(keys[0] < LINE))) for k in keys]
    return handed, same


def line_sums(keys, logs, states):
    handed, same = chain_members(keys)
    before = [s * flag(k < keys[0]) for s, k in zip(same, keys)]

    def weighted(members):
        total = jnp.zeros((HEAD_DIM, WIDTH), F32)
        for j in range(LINE):
            exponent = jnp.zeros((1, WIDTH), F32)
            for i in range(LINE):
                if i != j:
                    between = members[i] * flag(keys[i] > keys[j])
                    exponent = exponent + logs[i] * between.astype(F32)
            weight = jnp.exp(exponent) * members[j].astype(F32)
            total = total + weight * states[j]()
        return total

    prefix = sum(log * b.astype(F32) for log, b in zip(logs, before))
    return weighted(handed), weighted(before), prefix


def total_sums(group_ref, index_ref, forward, totals, line_logs, prefix):
    lines = [chain_keys(group_ref, index_ref, o, forward) for o in range(NX)]
    starts = [least(keys) for keys in lines]
    same = chain_members(lines[0])[1]
    own_start = least([jnp.where(s > 0, k, 99) for s, k in zip(same, lines[0])])
    earlier = [flag(s < own_start) for s in starts]
    result = 0.0
    for o in range(NX):
        exponent = prefix
        for i in range(NX):
            if i != o:
                between = earlier[i] * flag(starts[i] > starts[o])
                exponent = exponent + line_logs[i] * between.astype(F32)
        result = result + jnp.exp(exponent) * earlier[o].astype(F32) * totals[o].astype(F32)
    return result


def states_kernel(group_ref, index_ref, ga_ref, gb_ref, handed_ref, entry_ref, log_ref):
    logs, states = [], []
    for ref in (ga_ref, gb_ref):
        for i in range(NY):
            logs.append(whole_log(ref[i, pl.ds(LOG_ROW, 16)]))
            states.append(
                functools.partial(
                    lambda ref, i: ref[i, pl.ds(STATE_ROW, HEAD_DIM)].astype(F32), ref, i
                )
            )
    keys = chain_keys(group_ref, index_ref, 0, True)
    handed, entry, prefix = line_sums(keys, logs, states)
    handed_ref[pl.ds(0, HEAD_DIM)] = handed.astype(BF16)
    handed_ref[pl.ds(HEAD_DIM, 16)] = log_pieces(sum(logs))
    entry_ref[pl.ds(0, HEAD_DIM)] = entry
    entry_ref[pl.ds(HEAD_DIM, 8)] = jnp.broadcast_to(prefix, (8, WIDTH))
    for j in range(LINE):
        log_ref[pl.ds(j, 1)] = logs[j]


def decay_rows(decay_ref):
    return dot(decay_ref[...], triangle(True).astype(F32), 1, 0, HIGHEST)


def inner_terms(q, k, rows, cumulative, h):
    gap = cumulative[:, h : h + 1] - rows[h : h + 1]
    decay = jnp.where(triangle(False), jnp.exp(jnp.minimum(gap, 0.0)), 0.0)
    return decay, (dot(q, k, 1, 1) * decay).astype(BF16)


def read_kernel(
    group_ref, index_ref, q_ref, k_ref, v_ref, g_ref, decay_ref, part_ref, own, from_1, from_2,
    from_3, raw_ref, sum_ref, entry_ref, log_ref,
):
    all_totals = (own, from_1, from_2, from_3)
    line_logs = [whole_log(t[pl.ds(HEAD_DIM, 16)]) for t in all_totals]
    for o in range(NX):
        log_ref[pl.ds(o, 1)] = line_logs[o]
    log_ref[pl.ds(NX, 4)] = jnp.zeros((4, WIDTH), F32)
    entry = part_ref[pl.ds(0, HEAD_DIM)] + total_sums(
        group_ref, index_ref, True, [t[pl.ds(0, HEAD_DIM)] for t in all_totals], line_logs,
        part_ref[pl.ds(HEAD_DIM, 1)],
    )
    entry_ref[...] = entry.astype(BF16)
    cumulative, decay_in_rows = decay_columns(decay_ref), decay_rows(decay_ref)
    squares = jnp.zeros((TOK, 1), F32)
    inner = jnp.zeros((TOK, 1), F32)
    for h in range(HEADS):
        cols = head_cols(h)
        q = q_ref[:, cols]
        scores = inner_terms(q, k_ref[:, cols], decay_in_rows, cumulative, h)[1]
        carried = dot(q, entry_ref[:, cols], 1, 0)
        raw = dot(scores, v_ref[:, cols], 1, 0) + jnp.exp(cumulative[:, h : h + 1]) * carried
        raw_ref[:, cols] = raw
        squares = squares + jnp.sum(raw * raw, axis=1, keepdims=True)
        inner = inner + jnp.sum(raw * g_ref[:, cols].astype(F32), axis=1, keepdims=True)
    lane = lax.broadcasted_iota(jnp.int32, (TOK, HEAD_DIM), 1)
    sums = jnp.where(lane == 0, squares, jnp.where(lane == 1, inner, 0.0))
    sum_ref[...] = sums.T[:8]


def grad_kernel(
    q_ref, k_ref, v_ref, g_ref, decay_ref, entry_ref, raw_ref, sum_0, sum_1, sum_2, sum_3,
    out_ref, dq_ref, dk_ref, dv_ref, read_ref,
):
    cumulative, decay_in_rows = decay_columns(decay_ref), decay_rows(decay_ref)
    sums = (sum_0[...] + sum_1[...]) + (sum_2[...] + sum_3[...])
    sums = jnp.concatenate([sums] * (HEAD_DIM // 8), axis=0).T
    inverse = 1.0 / jnp.sqrt(sums[:, 0:1] * (1.0 / (HEAD_TOTAL * HEAD_DIM)) + EPS)
    aligned = sums[:, 1:2] * inverse * (1.0 / (HEAD_TOTAL * HEAD_DIM))
    for h in range(HEADS):
        cols = head_cols(h)
        q, k = q_ref[:, cols], k_ref[:, cols]
        out = raw_ref[:, cols] * inverse
        out_ref[:, cols] = out
        raw_grad = ((g_ref[:, cols].astype(F32) - out * aligned) * inverse).astype(BF16)
        decay, scores = inner_terms(q, k, decay_in_rows, cumulative, h)
        head_decay = jnp.exp(cumulative[:, h : h + 1])
        inner_grad = (dot(raw_grad, v_ref[:, cols], 1, 1) * decay).astype(BF16)
        carried = dot(raw_grad, entry_ref[:, cols], 1, 1)
        dq_ref[:, cols] = dot(inner_grad, k, 1, 0) + head_decay * carried
        dk_ref[:, cols] = dot(inner_grad, q, 0, 0)
        dv_ref[:, cols] = dot(scores, raw_grad, 0, 0)
        scaled = (q.astype(F32) * head_decay).astype(BF16)
        read_ref[:, cols] = dot(scaled, raw_grad, 0, 0).astype(BF16)


def back_kernel(
    group_ref, index_ref, log_ref, read_ref, pair_ref, from_1, from_2, from_3, handed_ref, part_ref
):
    logs = [log_ref[pl.ds(j, 1)] for j in range(LINE)]
    sources = [(read_ref, 0), (from_1, TOK), (from_2, TOK), (from_3, TOK)]
    sources += [(pair_ref, 0)]
    sources += [(ref, TOK + HEAD_DIM) for ref in (from_1, from_2, from_3)]
    states = [
        functools.partial(lambda ref, row: ref[pl.ds(row, HEAD_DIM)].astype(F32), ref, row)
        for ref, row in sources
    ]
    keys = chain_keys(group_ref, index_ref, 0, False)
    handed, part, prefix = line_sums(keys, logs, states)
    handed_ref[...] = handed.astype(BF16)
    part_ref[pl.ds(0, HEAD_DIM)] = part
    part_ref[pl.ds(HEAD_DIM, 8)] = jnp.broadcast_to(prefix, (8, WIDTH))


def write_kernel(
    group_ref, index_ref, k_ref, v_ref, decay_ref, part_ref, log_ref, own, from_1, from_2, from_3,
    dk_in, dv_in, out_own, out_1, out_2, out_3, dkv_own, dkv_1, dkv_2, dkv_3,
    dk_ref, dv_ref, soft_out_ref, soft_dk_ref, soft_dv_ref,
):
    leave = part_ref[pl.ds(0, HEAD_DIM)] + total_sums(
        group_ref, index_ref, False, [t[...] for t in (own, from_1, from_2, from_3)],
        [log_ref[pl.ds(o, 1)] for o in range(NX)], part_ref[pl.ds(HEAD_DIM, 1)],
    )
    leave = leave.astype(BF16)
    cumulative = decay_columns(decay_ref[pl.ds(pl.program_id(0), 1)])
    tail = jnp.exp(cumulative[TOK - 1 : TOK] - cumulative)
    dk_ref[...] = dk_in[...] + tail * dot(v_ref[...], leave, 1, 1)
    dv_ref[...] = dv_in[...] + tail * dot(k_ref[...], leave, 1, 0)
    soft_out_ref[...] = sum(
        (r[...].astype(F32) for r in (out_1, out_2, out_3)), out_own[...]
    ).astype(BF16)
    for i, ref in enumerate((soft_dk_ref, soft_dv_ref)):
        ref[...] = sum(
            (r[i].astype(F32) for r in (dkv_1, dkv_2, dkv_3)), dkv_own[i]
        ).astype(BF16)


def in_vmem(n):
    return [pl.BlockSpec(memory_space=pltpu.VMEM)] * n


def on_device(
    group_of, soft_query, soft_key, soft_value, soft_grad,
    lin_query, lin_key, lin_value, log_decay, lin_grad,
):
    place = (group_of, lax.axis_index(SEQ).reshape(1))
    decay = log_decay.T

    kv_own = jnp.stack([soft_key, soft_value])
    kv = {0: kv_own, **{o: fetch(kv_own, "x", NX, o) for o in OFFSETS}}
    kvs = [kv[o] for o in range(NX)]
    packed = call(
        pack_kernel,
        shaped(PACK_ROWS, WIDTH, dtype=BF16),
        2**26,
        (soft_grad, lin_key, lin_value, decay),
        vmem=60,
    )
    q_from = {0: soft_query, **{o: fetch(soft_query, "y", NY, o) for o in OFFSETS}}
    g_from = {0: packed, **{o: fetch(packed, "y", NY, o) for o in OFFSETS}}
    qa = jnp.stack([q_from[o] for o in range(NY)])
    qb = fetch(qa, "c", NC, 1)
    ga = jnp.stack([g_from[o] for o in range(NY)])
    gb = fetch(ga, "c", NC, 1)

    out_a, stat_a = soft_forward(place, 0, qa, kvs)
    handed, entry_part, logs = call(
        states_kernel,
        [
            shaped(HEAD_DIM + 16, WIDTH, dtype=BF16),
            shaped(HEAD_DIM + 8, WIDTH),
            shaped(8, WIDTH),
        ],
        2**24,
        (*place, ga, gb),
        **placed(in_vmem(2), in_vmem(3)),
    )
    totals = [handed, *(fetch(handed, "x", NX, o) for o in (1, 2, 3))]
    out_b, stat_b = soft_forward(place, 1, qb, kvs)
    part = call(
        delta_kernel,
        shaped(2, NY, 8, TOK),
        2**25,
        (ga, gb, out_a, out_b, stat_a, stat_b),
        grid=(HEADS,),
        in_specs=[rows_spec()] * 4 + [pl.BlockSpec((NY, 8, TOK), lambda h: (0, 0, 0))] * 2,
        out_specs=pl.BlockSpec((2, NY, 8, TOK), lambda h: (0, 0, 0, 0)),
    )
    other = fetch(part, "c", NC, 1)

    rows = shaped(TOK, WIDTH)
    raw, sums, entry, line_logs = call(
        read_kernel,
        [rows, shaped(8, TOK), shaped(HEAD_DIM, WIDTH, dtype=BF16), shaped(8, WIDTH)],
        2**27,
        (*place, lin_query, lin_key, lin_value, lin_grad, decay, entry_part, *totals),
        **placed(in_vmem(10), in_vmem(4)),
    )
    all_sums = [sums, *(fetch(sums, "head", NZ, o) for o in (1, 2, 3))]
    chip = call(chip_kernel, shaped(2, NY, 8, TOK), 2**20, (part, other))
    received = {o: fetch(chip, "y", NY, o) for o in OFFSETS}
    lin_out, lin_dq, dk_local, dv_local, read_grad = call(
        grad_kernel,
        [rows] * 4 + [shaped(HEAD_DIM, WIDTH, dtype=BF16)],
        2**28,
        (lin_query, lin_key, lin_value, lin_grad, decay, entry, raw, *all_sums),
    )
    stats, mine, theirs = call(
        line_kernel,
        [
            shaped(2, NY, 8, TOK),
            shaped(NY, TOK, WIDTH),
            shaped(NY * TOK, WIDTH, dtype=BF16),
        ],
        2**22,
        (part, chip, received[1], received[2], received[3], out_a, out_b),
    )
    from_core = fetch(theirs, "c", NC, 1)
    pair_read = fetch(read_grad, "c", NC, 1)

    grads = far_backward(place, 0, 1, qa, qb, ga, gb, kvs[1:], stats)
    own_out, *pays = call(
        join_kernel,
        [rows] + [shaped(2 * TOK, WIDTH, dtype=BF16)] * 3,
        2**22,
        (mine, from_core, read_grad, pair_read),
    )
    sent_out = {o: send(pays[o - 1], "y", NY, o) for o in OFFSETS}
    dq_a, dq_b, far_dkv = far_backward(place, 1, 2, qa, qb, ga, gb, kvs[1:], stats, tuple(grads))
    sent_dkv = [send(far_dkv[o - 1], "x", NX, o) for o in OFFSETS]
    dq_a, dq_b, near_dkv = near_backward(place, qa, qb, ga, gb, kvs[0], stats, dq_a, dq_b)
    dq_core = fetch(dq_b, "c", NC, 1)

    back_handed, leave_part = call(
        back_kernel,
        [shaped(HEAD_DIM, WIDTH, dtype=BF16), shaped(HEAD_DIM + 8, WIDTH)],
        2**24,
        (*place, logs, read_grad, pair_read, *(sent_out[NY - o] for o in (1, 2, 3))),
        **placed(in_vmem(6), in_vmem(2)),
    )
    back_totals = [back_handed, *(fetch(back_handed, "x", NX, o) for o in (1, 2, 3))]
    chip_dq = dq_a.astype(F32) + dq_core.astype(F32)
    soft_dq = chip_dq[0]
    for o in OFFSETS:
        soft_dq = soft_dq + send(chip_dq[o].astype(BF16), "y", NY, o).astype(F32)
    head_block = pl.BlockSpec((TOK, HEAD_DIM), lambda h, *_: (0, h))
    lin_dk, lin_dv, soft_out, soft_dk, soft_dv = call(
        write_kernel,
        [rows, rows] + [shaped(TOK, WIDTH, dtype=BF16)] * 3,
        2**26,
        (
            *place, lin_key, lin_value, decay, leave_part, line_logs, *back_totals,
            dk_local, dv_local, own_out, *(sent_out[o] for o in OFFSETS), near_dkv, *sent_dkv,
        ),
        **placed(
            [
                head_block,
                head_block,
                pl.BlockSpec((HEADS, TOK), lambda h, *_: (0, 0)),
                pl.BlockSpec((HEAD_DIM + 8, HEAD_DIM), lambda h, *_: (0, h)),
                pl.BlockSpec((8, HEAD_DIM), lambda h, *_: (0, h)),
            ]
            + [pl.BlockSpec((HEAD_DIM, HEAD_DIM), lambda h, *_: (0, h))] * NX
            + [head_block] * 6
            + [pair_spec()] * NX,
            [head_block] * 5,
            grid=(HEADS,),
        ),
    )
    return (
        soft_out, soft_dq.astype(BF16), soft_dk, soft_dv, lin_out, lin_dq, lin_dk, lin_dv,
    )


def solution(mesh):
    grid = Mesh(mesh.devices.reshape(NX, NY, NC, NZ), (*SEQ, "head"))
    block = P(SEQ, "head")

    return jax.shard_map(
        on_device,
        mesh=grid,
        in_specs=(P(),) + (block,) * 9,
        out_specs=(block,) * 8,
        check_vma=False,
    )
```

```python
import functools

import jax
import jax.numpy as jnp
from jax import lax
from jax.experimental import pallas as pl
from jax.experimental.pallas import tpu as pltpu
from jax.sharding import Mesh
from jax.sharding import PartitionSpec as P


HEAD_TOTAL = 12
HEAD_DIM = 128
HEADS = 3
WIDTH = HEADS * HEAD_DIM
TOK = 256
NX, NY, NC, NZ = 4, 4, 2, 4
LINE = NY * NC
EPS = 1e-06
SCALE = HEAD_DIM ** (-0.5)
LOG2E = 1.4426950408889634
NEG = -1e30
F32 = jnp.float32
BF16 = jnp.bfloat16
HIGHEST = lax.Precision.HIGHEST
SEQ = ("x", "y", "c")
OFFSETS = (1, 3, 2)
STATE_ROW = TOK
LOG_ROW = STATE_ROW + HEAD_DIM
PACK_ROWS = LOG_ROW + 16
ANY = pl.BlockSpec(memory_space=pl.ANY)


def send(block, axis, size, offset):
    return lax.ppermute(block, axis, [(i, (i + offset) % size) for i in range(size)])


def fetch(block, axis, size, offset):
    return send(block, axis, size, -offset)


def dot(a, b, dim_a, dim_b, precision=None):
    return lax.dot_general(
        a, b, (((dim_a,), (dim_b,)), ((), ())), precision=precision, preferred_element_type=F32
    )


def head_cols(h):
    return pl.ds(h * HEAD_DIM, HEAD_DIM)


def shaped(*dims, dtype=F32):
    return jax.ShapeDtypeStruct(dims, dtype)


def call(kernel, out_shape, flops, args, vmem=40, **kwargs):
    return pl.pallas_call(
        kernel,
        out_shape=out_shape,
        cost_estimate=pl.CostEstimate(flops=flops, transcendentals=2**18, bytes_accessed=2 * 2**20),
        compiler_params=pltpu.CompilerParams(vmem_limit_bytes=vmem * 2**20),
        **kwargs,
    )(*args)


def placed(in_specs, out_specs, scratch=(), grid=()):
    return {
        "grid_spec": pltpu.PrefetchScalarGridSpec(
            num_scalar_prefetch=2,
            grid=grid,
            in_specs=in_specs,
            out_specs=out_specs,
            scratch_shapes=list(scratch),
        )
    }


def position(group_ref, index_ref, along_x, side, along_y):
    index = index_ref[0]
    x, y, c = (index >> 3) + along_x, ((index >> 1) & 3) + along_y, (index & 1) + side
    return group_ref[(x & 3) * LINE + (y & 3) * NC + (c & 1)]


def flag(condition):
    return jnp.where(condition, 1, 0)


def causal(scores):
    row = lax.broadcasted_iota(jnp.int32, scores.shape, 0)
    col = lax.broadcasted_iota(jnp.int32, scores.shape, 1)
    return jnp.where(row <= col, scores, NEG)


def hidden(key_pos, query_pos):
    return jnp.where(key_pos > query_pos, -NEG, 0.0)


def staged(items, first, second):
    current = first(items[0])
    for i, item in enumerate(items):
        following = first(items[i + 1]) if i + 1 < len(items) else None
        second(item, current)
        current = following


def forward_kernel(
    side, group_ref, index_ref, q_ref, kv_0, kv_1, kv_2, kv_3, out_ref, stat_ref, k_ref, vt_ref
):
    h = pl.program_id(0)
    for o, kv_ref in enumerate((kv_0, kv_1, kv_2, kv_3)):
        k_ref[pl.ds(o * TOK, TOK)] = kv_ref[0]
        vt_ref[pl.ds(0, HEAD_DIM), pl.ds(o * TOK, TOK)] = kv_ref[1].T

    @pl.when(h == 0)
    def _():
        stat_ref[...] = jnp.zeros_like(stat_ref)
        vt_ref[pl.ds(HEAD_DIM, 16)] = jnp.ones((16, NX * TOK), BF16)

    key_pos = [position(group_ref, index_ref, o, 0, 0) for o in range(NX)]

    def scores(i):
        return [dot(k_ref[pl.ds(o * TOK, TOK)], q_ref[i], 1, 1) for o in range(NX)]

    def finish(i, parts):
        query_pos = position(group_ref, index_ref, 0, side, i)
        if side == 0 and i == 0:
            parts = [causal(parts[0]), *parts[1:]]
        hide = [hidden(p, query_pos) for p in key_pos]
        tops = [jnp.max(s, axis=0, keepdims=True) - x for s, x in zip(parts, hide)]
        top = functools.reduce(jnp.maximum, tops)
        probs = [
            jnp.exp2((s - (top + x)) * (SCALE * LOG2E)).astype(BF16) for s, x in zip(parts, hide)
        ]
        acc = dot(vt_ref[...], jnp.concatenate(probs), 1, 0)
        total = acc[HEAD_DIM : HEAD_DIM + 1]
        seen = top > 0.5 * NEG
        out_ref[i] = jnp.where(seen, acc[:HEAD_DIM] * (1.0 / total), 0.0).T.astype(BF16)
        log = top * (SCALE * LOG2E) + jnp.log(total) * LOG2E
        stat_ref[i, pl.ds(h, 1)] = jnp.where(seen, log, NEG)

    staged(range(NY), scores, finish)


def rows_spec(first=0):
    return pl.BlockSpec((NY, TOK, HEAD_DIM), lambda h, *_: (0, 0, h + first))


def pair_spec(first=0):
    return pl.BlockSpec((2, TOK, HEAD_DIM), lambda h, *_: (0, 0, h + first))


def soft_forward(place, side, q, kvs):
    return call(
        functools.partial(forward_kernel, side),
        [shaped(NY, TOK, WIDTH, dtype=BF16), shaped(NY, 8, TOK)],
        NY * NX * HEADS * 4 * TOK * TOK * HEAD_DIM,
        (*place, q, *kvs),
        **placed(
            [rows_spec()] + [pair_spec()] * NX,
            [rows_spec(), pl.BlockSpec((NY, 8, TOK), lambda h, *_: (0, 0, 0))],
            [
                pltpu.VMEM((NX * TOK, HEAD_DIM), BF16),
                pltpu.VMEM((HEAD_DIM + 16, NX * TOK), BF16),
            ],
            (HEADS,),
        ),
    )


def delta_kernel(g_a, g_b, out_a, out_b, stat_a, stat_b, part_ref):
    h = pl.program_id(0)

    @pl.when(h == 0)
    def _():
        part_ref[0] = stat_a[...]
        part_ref[1] = stat_b[...]

    for side, (g_ref, o_ref) in enumerate(((g_a, out_a), (g_b, out_b))):
        for i in range(NY):
            product = o_ref[i].astype(F32) * g_ref[i].astype(F32)
            part_ref[side, i, pl.ds(h + 4, 1)] = jnp.sum(product.T, axis=0, keepdims=True)


def far_kernel(
    first_head, group_ref, index_ref, qa_ref, qb_ref, ga_ref, gb_ref, kv_1, kv_2, kv_3, stat_ref,
    *refs,
):
    dqa_ref, dqb_ref, dkv_ref, k_ref, v_ref, kt_ref, acc_ref = refs[-7:]
    h = pl.program_id(0) + first_head
    tiles = [pl.ds(o * TOK, TOK) for o in range(NX - 1)]
    for tile, kv_ref in zip(tiles, (kv_1, kv_2, kv_3)):
        k_ref[tile] = kv_ref[0]
        v_ref[tile] = kv_ref[1]
        kt_ref[:, tile] = kv_ref[0].T
    key_pos = [position(group_ref, index_ref, o, 0, 0) for o in range(1, NX)]
    acc_ref[...] = jnp.zeros_like(acc_ref)

    def products(item):
        q_ref, g_ref, _, _, b = item
        return (
            [dot(k_ref[t], q_ref[b], 1, 1) for t in tiles],
            [dot(v_ref[t], g_ref[b], 1, 1) for t in tiles],
        )

    def finish(item, found):
        q_ref, g_ref, dq_ref, side, b = item
        query_pos = position(group_ref, index_ref, 0, side, b)
        lse = stat_ref[side, b, pl.ds(h, 1)]
        delta = stat_ref[side, b, pl.ds(h + 4, 1)]
        probs, grads = [], []
        for x, s, dprobs in zip(key_pos, *found):
            p = jnp.exp2(s * (SCALE * LOG2E) - (lse + hidden(x, query_pos)))
            probs.append(p.astype(BF16))
            grads.append((p * (dprobs - delta)).astype(BF16))
        probs, grads = jnp.concatenate(probs), jnp.concatenate(grads)
        acc_ref[0] += dot(grads, q_ref[b], 1, 0)
        acc_ref[1] += dot(probs, g_ref[b], 1, 0)
        dq_ref[b, 0] = dot(kt_ref[...], grads, 1, 0)

    items = [(qa_ref, ga_ref, dqa_ref, 0, b) for b in range(NY)]
    items += [(qb_ref, gb_ref, dqb_ref, 1, b) for b in range(NY)]
    staged(items, products, finish)
    for o, tile in enumerate(tiles):
        dkv_ref[o, 0] = (acc_ref[0, tile] * SCALE).astype(BF16)
        dkv_ref[o, 1] = acc_ref[1, tile].astype(BF16)


STAT_SPEC = pl.BlockSpec((2, NY, 8, TOK), lambda h, *_: (0, 0, 0, 0))


def far_backward(place, first, heads, qa, qb, ga, gb, kvs, stats, earlier=()):
    rows, pair = rows_spec(first), pair_spec(first)
    turned = pl.BlockSpec((NY, 1, HEAD_DIM, TOK), lambda h, *_: (0, h + first, 0, 0))
    dq_shape = shaped(NY, HEADS, HEAD_DIM, TOK)
    kwargs = placed(
        [rows] * 4 + [pair] * (NX - 1) + [STAT_SPEC] + [ANY] * len(earlier),
        [
            turned,
            turned,
            pl.BlockSpec((NX - 1, 2, TOK, HEAD_DIM), lambda h, *_: (0, 0, 0, h + first)),
        ],
        [
            pltpu.VMEM(((NX - 1) * TOK, HEAD_DIM), BF16),
            pltpu.VMEM(((NX - 1) * TOK, HEAD_DIM), BF16),
            pltpu.VMEM((HEAD_DIM, (NX - 1) * TOK), BF16),
            pltpu.VMEM((2, (NX - 1) * TOK, HEAD_DIM), F32),
        ],
        (heads,),
    )
    return call(
        functools.partial(far_kernel, first),
        [dq_shape, dq_shape, shaped(NX - 1, 2, TOK, WIDTH, dtype=BF16)],
        2 * NY * (NX - 1) * heads * 10 * TOK * TOK * HEAD_DIM,
        (*place, qa, qb, ga, gb, *kvs, stats, *earlier),
        input_output_aliases={10 + i: i for i in range(len(earlier))},
        **kwargs,
    )


def near_kernel(
    group_ref, index_ref, qa_ref, qb_ref, ga_ref, gb_ref, kv_ref, stat_ref, dqa_in, dqb_in,
    dqa_ref, dqb_ref, dkv_ref, kt_ref,
):
    h = pl.program_id(0)
    kt_ref[...] = kv_ref[0].T
    own = position(group_ref, index_ref, 0, 0, 0)

    def products(item):
        q_ref, g_ref, b = item[0], item[1], item[-1]
        return dot(kv_ref[0], q_ref[b], 1, 1), dot(kv_ref[1], g_ref[b], 1, 1)

    def finish(item, found):
        q_ref, g_ref, dq_in, dq_ref, side, b = item
        s, dprobs = found
        lse = stat_ref[side, b, pl.ds(h, 1)]
        delta = stat_ref[side, b, pl.ds(h + 4, 1)]
        s = s * (SCALE * LOG2E)
        start = side == 0 and b == 0
        if start:
            s = causal(s)
        p = jnp.exp2(s - (lse + hidden(own, position(group_ref, index_ref, 0, side, b))))
        ds = (p * (dprobs - delta)).astype(BF16)
        dq_sum = dq_in[b, 0] + dot(kt_ref[...], ds, 1, 0)
        dq_ref[b] = (dq_sum * SCALE).T.astype(BF16)
        dk, dv = dot(ds, q_ref[b], 1, 0) * SCALE, dot(p.astype(BF16), g_ref[b], 1, 0)
        dkv_ref[0] = dk if start else dkv_ref[0] + dk
        dkv_ref[1] = dv if start else dkv_ref[1] + dv

    sides = ((qa_ref, ga_ref, dqa_in, dqa_ref), (qb_ref, gb_ref, dqb_in, dqb_ref))
    items = [(*refs, side, b) for side, refs in enumerate(sides) for b in range(NY)]
    staged(items, products, finish)


def near_backward(place, qa, qb, ga, gb, kv, stats, dqa, dqb):
    rows, pair = rows_spec(), pair_spec()
    turned = pl.BlockSpec((NY, 1, HEAD_DIM, TOK), lambda h, *_: (0, h, 0, 0))
    return call(
        near_kernel,
        [
            shaped(NY, TOK, WIDTH, dtype=BF16),
            shaped(NY, TOK, WIDTH, dtype=BF16),
            shaped(2, TOK, WIDTH),
        ],
        2 * NY * HEADS * 10 * TOK * TOK * HEAD_DIM,
        (*place, qa, qb, ga, gb, kv, stats, dqa, dqb),
        **placed(
            [rows] * 4 + [pair, STAT_SPEC, turned, turned],
            [rows, rows, pair],
            [pltpu.VMEM((HEAD_DIM, TOK), BF16)],
            (HEADS,),
        ),
    )


def merged(stats_a, stats_b):
    lse_a, lse_b = stats_a[..., :4, :], stats_b[..., :4, :]
    top = jnp.maximum(lse_a, lse_b)
    weight_a, weight_b = jnp.exp2(lse_a - top), jnp.exp2(lse_b - top)
    total = weight_a + weight_b
    delta = (weight_a * stats_a[..., 4:, :] + weight_b * stats_b[..., 4:, :]) / total
    return jnp.concatenate([top + jnp.log(total) * LOG2E, delta], axis=-2)


def chip_kernel(part_ref, other_ref, out_ref):
    for side in range(2):
        out_ref[side] = merged(part_ref[side], other_ref[1 - side])


def line_kernel(
    part_ref, chip_ref, from_1, from_2, from_3, out_a_ref, out_b_ref,
    stat_ref, mine_ref, theirs_ref,
):
    for side, o_ref in enumerate((out_a_ref, out_b_ref)):
        for i in range(NY):
            stats = chip_ref[side, i]
            for o, other in ((1, from_1), (2, from_2), (3, from_3)):
                stats = merged(stats, other[side, (i - o) % NY])
            stat_ref[side, i] = stats
            weight = jnp.exp2(part_ref[side, i, :4] - stats[:4])
            weight = jnp.concatenate([weight] * (HEAD_DIM // 4), axis=0).T
            for h in range(HEADS):
                scaled = o_ref[i, :, head_cols(h)].astype(F32) * weight[:, h : h + 1]
                if side == 0:
                    mine_ref[i, :, head_cols(h)] = scaled
                else:
                    theirs_ref[pl.ds(i * TOK, TOK), head_cols(h)] = scaled.astype(BF16)


def join_kernel(mine_ref, core_ref, read_ref, pair_ref, own_ref, pay_1, pay_2, pay_3):
    own_ref[...] = mine_ref[0] + core_ref[pl.ds(0, TOK)].astype(F32)
    for o, pay in ((1, pay_1), (2, pay_2), (3, pay_3)):
        total = mine_ref[o] + core_ref[pl.ds(o * TOK, TOK)].astype(F32)
        pay[pl.ds(0, TOK)] = total.astype(BF16)
        pay[pl.ds(TOK, HEAD_DIM)] = read_ref[...]
        pay[pl.ds(TOK + HEAD_DIM, HEAD_DIM)] = pair_ref[...]


def triangle(upper):
    row = lax.broadcasted_iota(jnp.int32, (TOK, TOK), 0)
    col = lax.broadcasted_iota(jnp.int32, (TOK, TOK), 1)
    return row <= col if upper else row >= col


def decay_columns(decay):
    return dot(triangle(False).astype(F32), decay[...], 1, 1, HIGHEST)


def log_pieces(log):
    log = jnp.broadcast_to(log, (16, log.shape[1]))
    row = lax.broadcasted_iota(jnp.int32, log.shape, 0)
    high = log.astype(BF16).astype(F32)
    middle = (log - high).astype(BF16).astype(F32)
    low = log - high - middle
    piece = jnp.where(row == 0, high, jnp.where(row == 1, middle, jnp.where(row == 2, low, 0.0)))
    return piece.astype(BF16)


def whole_log(pieces):
    pieces = pieces.astype(F32)
    return pieces[0:1] + pieces[1:2] + pieces[2:3]


def pack_kernel(g_ref, key_ref, value_ref, decay_ref, out_ref):
    cumulative = decay_columns(decay_ref)
    total = cumulative[TOK - 1 : TOK]
    tail = jnp.exp(total - cumulative)
    out_ref[pl.ds(0, TOK)] = g_ref[...]
    for h in range(HEADS):
        keys = key_ref[:, head_cols(h)].astype(F32) * tail[:, h : h + 1]
        state = dot(keys.astype(BF16), value_ref[:, head_cols(h)], 0, 0)
        out_ref[pl.ds(STATE_ROW, HEAD_DIM), head_cols(h)] = state.astype(BF16)
        log = jnp.broadcast_to(total[:, h : h + 1], (1, HEAD_DIM))
        out_ref[pl.ds(LOG_ROW, 16), head_cols(h)] = log_pieces(log)


def least(values):
    return functools.reduce(jnp.minimum, values)


def chain_keys(group_ref, index_ref, along_x, forward):
    found = [
        position(group_ref, index_ref, along_x, side, j) for side in range(NC) for j in range(NY)
    ]
    return found if forward else [31 - p for p in found]


def chain_members(keys):
    apart = -least([-k for k in keys]) - least(keys) > LINE - 1
    handed = [flag(jnp.logical_or(k < LINE, jnp.logical_not(apart))) for k in keys]
    whole = flag(jnp.logical_not(apart))
    same = [jnp.maximum(whole, flag(flag(k < LINE) == flag(keys[0] < LINE))) for k in keys]
    return handed, same


def line_sums(keys, logs, states):
    handed, same = chain_members(keys)
    before = [s * flag(k < keys[0]) for s, k in zip(same, keys)]

    def weighted(members):
        total = jnp.zeros((HEAD_DIM, WIDTH), F32)
        for j in range(LINE):
            exponent = jnp.zeros((1, WIDTH), F32)
            for i in range(LINE):
                if i != j:
                    between = members[i] * flag(keys[i] > keys[j])
                    exponent = exponent + logs[i] * between.astype(F32)
            weight = jnp.exp(exponent) * members[j].astype(F32)
            total = total + weight * states[j]()
        return total

    prefix = sum(log * b.astype(F32) for log, b in zip(logs, before))
    return weighted(handed), weighted(before), prefix


def total_sums(group_ref, index_ref, forward, totals, line_logs, prefix):
    lines = [chain_keys(group_ref, index_ref, o, forward) for o in range(NX)]
    starts = [least(keys) for keys in lines]
    same = chain_members(lines[0])[1]
    own_start = least([jnp.where(s > 0, k, 99) for s, k in zip(same, lines[0])])
    earlier = [flag(s < own_start) for s in starts]
    result = 0.0
    for o in range(NX):
        exponent = prefix
        for i in range(NX):
            if i != o:
                between = earlier[i] * flag(starts[i] > starts[o])
                exponent = exponent + line_logs[i] * between.astype(F32)
        result = result + jnp.exp(exponent) * earlier[o].astype(F32) * totals[o].astype(F32)
    return result


def states_kernel(group_ref, index_ref, ga_ref, gb_ref, handed_ref, entry_ref, log_ref):
    logs, states = [], []
    for ref in (ga_ref, gb_ref):
        for i in range(NY):
            logs.append(whole_log(ref[i, pl.ds(LOG_ROW, 16)]))
            states.append(
                functools.partial(
                    lambda ref, i: ref[i, pl.ds(STATE_ROW, HEAD_DIM)].astype(F32), ref, i
                )
            )
    keys = chain_keys(group_ref, index_ref, 0, True)
    handed, entry, prefix = line_sums(keys, logs, states)
    handed_ref[pl.ds(0, HEAD_DIM)] = handed.astype(BF16)
    handed_ref[pl.ds(HEAD_DIM, 16)] = log_pieces(sum(logs))
    entry_ref[pl.ds(0, HEAD_DIM)] = entry
    entry_ref[pl.ds(HEAD_DIM, 8)] = jnp.broadcast_to(prefix, (8, WIDTH))
    for j in range(LINE):
        log_ref[pl.ds(j, 1)] = logs[j]


def decay_rows(decay_ref):
    return dot(decay_ref[...], triangle(True).astype(F32), 1, 0, HIGHEST)


def inner_terms(q, k, rows, cumulative, h):
    gap = cumulative[:, h : h + 1] - rows[h : h + 1]
    decay = jnp.where(triangle(False), jnp.exp(jnp.minimum(gap, 0.0)), 0.0)
    return decay, (dot(q, k, 1, 1) * decay).astype(BF16)


def read_kernel(
    group_ref, index_ref, q_ref, k_ref, v_ref, g_ref, decay_ref, part_ref, own, from_1, from_2,
    from_3, raw_ref, sum_ref, entry_ref, log_ref,
):
    all_totals = (own, from_1, from_2, from_3)
    line_logs = [whole_log(t[pl.ds(HEAD_DIM, 16)]) for t in all_totals]
    for o in range(NX):
        log_ref[pl.ds(o, 1)] = line_logs[o]
    log_ref[pl.ds(NX, 4)] = jnp.zeros((4, WIDTH), F32)
    entry = part_ref[pl.ds(0, HEAD_DIM)] + total_sums(
        group_ref, index_ref, True, [t[pl.ds(0, HEAD_DIM)] for t in all_totals], line_logs,
        part_ref[pl.ds(HEAD_DIM, 1)],
    )
    entry_ref[...] = entry.astype(BF16)
    cumulative, decay_in_rows = decay_columns(decay_ref), decay_rows(decay_ref)
    squares = jnp.zeros((TOK, 1), F32)
    inner = jnp.zeros((TOK, 1), F32)
    for h in range(HEADS):
        cols = head_cols(h)
        q = q_ref[:, cols]
        scores = inner_terms(q, k_ref[:, cols], decay_in_rows, cumulative, h)[1]
        carried = dot(q, entry_ref[:, cols], 1, 0)
        raw = dot(scores, v_ref[:, cols], 1, 0) + jnp.exp(cumulative[:, h : h + 1]) * carried
        raw_ref[:, cols] = raw
        squares = squares + jnp.sum(raw * raw, axis=1, keepdims=True)
        inner = inner + jnp.sum(raw * g_ref[:, cols].astype(F32), axis=1, keepdims=True)
    lane = lax.broadcasted_iota(jnp.int32, (TOK, HEAD_DIM), 1)
    sums = jnp.where(lane == 0, squares, jnp.where(lane == 1, inner, 0.0))
    sum_ref[...] = sums.T[:8]


def grad_kernel(
    q_ref, k_ref, v_ref, g_ref, decay_ref, entry_ref, raw_ref, sum_0, sum_1, sum_2, sum_3,
    out_ref, dq_ref, dk_ref, dv_ref, read_ref,
):
    cumulative, decay_in_rows = decay_columns(decay_ref), decay_rows(decay_ref)
    sums = (sum_0[...] + sum_1[...]) + (sum_2[...] + sum_3[...])
    sums = jnp.concatenate([sums] * (HEAD_DIM // 8), axis=0).T
    inverse = 1.0 / jnp.sqrt(sums[:, 0:1] * (1.0 / (HEAD_TOTAL * HEAD_DIM)) + EPS)
    aligned = sums[:, 1:2] * inverse * (1.0 / (HEAD_TOTAL * HEAD_DIM))
    for h in range(HEADS):
        cols = head_cols(h)
        q, k = q_ref[:, cols], k_ref[:, cols]
        out = raw_ref[:, cols] * inverse
        out_ref[:, cols] = out
        raw_grad = ((g_ref[:, cols].astype(F32) - out * aligned) * inverse).astype(BF16)
        decay, scores = inner_terms(q, k, decay_in_rows, cumulative, h)
        head_decay = jnp.exp(cumulative[:, h : h + 1])
        inner_grad = (dot(raw_grad, v_ref[:, cols], 1, 1) * decay).astype(BF16)
        carried = dot(raw_grad, entry_ref[:, cols], 1, 1)
        dq_ref[:, cols] = dot(inner_grad, k, 1, 0) + head_decay * carried
        dk_ref[:, cols] = dot(inner_grad, q, 0, 0)
        dv_ref[:, cols] = dot(scores, raw_grad, 0, 0)
        scaled = (q.astype(F32) * head_decay).astype(BF16)
        read_ref[:, cols] = dot(scaled, raw_grad, 0, 0).astype(BF16)


def back_kernel(
    group_ref, index_ref, log_ref, read_ref, pair_ref, from_1, from_2, from_3, handed_ref, part_ref
):
    logs = [log_ref[pl.ds(j, 1)] for j in range(LINE)]
    sources = [(read_ref, 0), (from_1, TOK), (from_2, TOK), (from_3, TOK)]
    sources += [(pair_ref, 0)]
    sources += [(ref, TOK + HEAD_DIM) for ref in (from_1, from_2, from_3)]
    states = [
        functools.partial(lambda ref, row: ref[pl.ds(row, HEAD_DIM)].astype(F32), ref, row)
        for ref, row in sources
    ]
    keys = chain_keys(group_ref, index_ref, 0, False)
    handed, part, prefix = line_sums(keys, logs, states)
    handed_ref[...] = handed.astype(BF16)
    part_ref[pl.ds(0, HEAD_DIM)] = part
    part_ref[pl.ds(HEAD_DIM, 8)] = jnp.broadcast_to(prefix, (8, WIDTH))


def write_kernel(
    group_ref, index_ref, k_ref, v_ref, decay_ref, part_ref, log_ref, own, from_1, from_2, from_3,
    dk_in, dv_in, dk_ref, dv_ref,
):
    leave_all = part_ref[pl.ds(0, HEAD_DIM)] + total_sums(
        group_ref, index_ref, False, [t[...] for t in (own, from_1, from_2, from_3)],
        [log_ref[pl.ds(o, 1)] for o in range(NX)], part_ref[pl.ds(HEAD_DIM, 1)],
    )
    cumulative = decay_columns(decay_ref)
    tail = jnp.exp(cumulative[TOK - 1 : TOK] - cumulative)
    for h in range(HEADS):
        cols = head_cols(h)
        leave = leave_all[:, h * HEAD_DIM : (h + 1) * HEAD_DIM].astype(BF16)
        scale = tail[:, h : h + 1]
        dk_ref[:, cols] = dk_in[:, cols] + scale * dot(v_ref[:, cols], leave, 1, 1)
        dv_ref[:, cols] = dv_in[:, cols] + scale * dot(k_ref[:, cols], leave, 1, 0)


def in_vmem(n):
    return [pl.BlockSpec(memory_space=pltpu.VMEM)] * n


def on_device(
    group_of, soft_query, soft_key, soft_value, soft_grad,
    lin_query, lin_key, lin_value, log_decay, lin_grad,
):
    place = (group_of, lax.axis_index(SEQ).reshape(1))
    decay = log_decay.T

    kv_own = jnp.stack([soft_key, soft_value])
    kv = {0: kv_own, **{o: fetch(kv_own, "x", NX, o) for o in OFFSETS}}
    kvs = [kv[o] for o in range(NX)]
    packed = call(
        pack_kernel,
        shaped(PACK_ROWS, WIDTH, dtype=BF16),
        2**26,
        (soft_grad, lin_key, lin_value, decay),
    )
    q_from = {0: soft_query, **{o: fetch(soft_query, "y", NY, o) for o in OFFSETS}}
    g_from = {0: packed, **{o: fetch(packed, "y", NY, o) for o in OFFSETS}}
    qa = jnp.stack([q_from[o] for o in range(NY)])
    qb = fetch(qa, "c", NC, 1)
    ga = jnp.stack([g_from[o] for o in range(NY)])
    gb = fetch(ga, "c", NC, 1)

    out_a, stat_a = soft_forward(place, 0, qa, kvs)
    handed, entry_part, logs = call(
        states_kernel,
        [
            shaped(HEAD_DIM + 16, WIDTH, dtype=BF16),
            shaped(HEAD_DIM + 8, WIDTH),
            shaped(8, WIDTH),
        ],
        2**24,
        (*place, ga, gb),
        **placed(in_vmem(2), in_vmem(3)),
    )
    totals = [handed, *(fetch(handed, "x", NX, o) for o in (1, 2, 3))]
    out_b, stat_b = soft_forward(place, 1, qb, kvs)
    part = call(
        delta_kernel,
        shaped(2, NY, 8, TOK),
        2**25,
        (ga, gb, out_a, out_b, stat_a, stat_b),
        grid=(HEADS,),
        in_specs=[rows_spec()] * 4 + [pl.BlockSpec((NY, 8, TOK), lambda h: (0, 0, 0))] * 2,
        out_specs=pl.BlockSpec((2, NY, 8, TOK), lambda h: (0, 0, 0, 0)),
    )
    other = fetch(part, "c", NC, 1)

    rows = shaped(TOK, WIDTH)
    raw, sums, entry, line_logs = call(
        read_kernel,
        [rows, shaped(8, TOK), shaped(HEAD_DIM, WIDTH, dtype=BF16), shaped(8, WIDTH)],
        2**27,
        (*place, lin_query, lin_key, lin_value, lin_grad, decay, entry_part, *totals),
        **placed(in_vmem(10), in_vmem(4)),
    )
    all_sums = [sums, *(fetch(sums, "head", NZ, o) for o in (1, 2, 3))]
    chip = call(chip_kernel, shaped(2, NY, 8, TOK), 2**20, (part, other))
    received = {o: fetch(chip, "y", NY, o) for o in OFFSETS}
    lin_out, lin_dq, dk_local, dv_local, read_grad = call(
        grad_kernel,
        [rows] * 4 + [shaped(HEAD_DIM, WIDTH, dtype=BF16)],
        2**28,
        (lin_query, lin_key, lin_value, lin_grad, decay, entry, raw, *all_sums),
    )
    stats, mine, theirs = call(
        line_kernel,
        [
            shaped(2, NY, 8, TOK),
            shaped(NY, TOK, WIDTH),
            shaped(NY * TOK, WIDTH, dtype=BF16),
        ],
        2**22,
        (part, chip, received[1], received[2], received[3], out_a, out_b),
    )
    from_core = fetch(theirs, "c", NC, 1)
    pair_read = fetch(read_grad, "c", NC, 1)

    grads = far_backward(place, 0, 1, qa, qb, ga, gb, kvs[1:], stats)
    own_out, *pays = call(
        join_kernel,
        [rows] + [shaped(2 * TOK, WIDTH, dtype=BF16)] * 3,
        2**22,
        (mine, from_core, read_grad, pair_read),
    )
    sent_out = {o: send(pays[o - 1], "y", NY, o) for o in OFFSETS}
    dq_a, dq_b, far_dkv = far_backward(place, 1, 2, qa, qb, ga, gb, kvs[1:], stats, tuple(grads))
    sent_dkv = [send(far_dkv[o - 1], "x", NX, o) for o in OFFSETS]
    dq_a, dq_b, near_dkv = near_backward(place, qa, qb, ga, gb, kvs[0], stats, dq_a, dq_b)
    dq_core = fetch(dq_b, "c", NC, 1)

    back_handed, leave_part = call(
        back_kernel,
        [shaped(HEAD_DIM, WIDTH, dtype=BF16), shaped(HEAD_DIM + 8, WIDTH)],
        2**24,
        (*place, logs, read_grad, pair_read, *(sent_out[NY - o] for o in (1, 2, 3))),
        **placed(in_vmem(6), in_vmem(2)),
    )
    back_totals = [back_handed, *(fetch(back_handed, "x", NX, o) for o in (1, 2, 3))]
    chip_dq = dq_a.astype(F32) + dq_core.astype(F32)
    soft_dq = chip_dq[0]
    for o in OFFSETS:
        soft_dq = soft_dq + send(chip_dq[o].astype(BF16), "y", NY, o).astype(F32)
    lin_dk, lin_dv = call(
        write_kernel,
        [rows, rows],
        2**26,
        (*place, lin_key, lin_value, decay, leave_part, line_logs, *back_totals, dk_local, dv_local),
        **placed(in_vmem(11), in_vmem(2)),
    )
    soft_out = own_out
    for o in OFFSETS:
        soft_out = soft_out + sent_out[o][:TOK].astype(F32)
    soft_out = soft_out.astype(BF16)
    dkv = near_dkv
    for sent in sent_dkv:
        dkv = dkv + sent.astype(F32)
    soft_dk, soft_dv = dkv[0].astype(BF16), dkv[1].astype(BF16)
    return (
        soft_out, soft_dq.astype(BF16), soft_dk, soft_dv, lin_out, lin_dq, lin_dk, lin_dv,
    )


def solution(mesh):
    grid = Mesh(mesh.devices.reshape(NX, NY, NC, NZ), (*SEQ, "head"))
    block = P(SEQ, "head")

    return jax.shard_map(
        on_device,
        mesh=grid,
        in_specs=(P(),) + (block,) * 9,
        out_specs=(block,) * 8,
        check_vma=False,
    )
```

```python
import functools

import jax
import jax.numpy as jnp
from jax import lax
from jax.experimental import pallas as pl
from jax.experimental.pallas import tpu as pltpu
from jax.sharding import Mesh
from jax.sharding import PartitionSpec as P


HEAD_TOTAL = 12
HEAD_DIM = 128
HEADS = 3
WIDTH = HEADS * HEAD_DIM
TOK = 256
NX, NY, NC, NZ = 4, 4, 2, 4
LINE = NY * NC
EPS = 1e-06
SCALE = HEAD_DIM ** (-0.5)
LOG2E = 1.4426950408889634
NEG = -1e30
F32 = jnp.float32
BF16 = jnp.bfloat16
HIGHEST = lax.Precision.HIGHEST
SEQ = ("x", "y", "c")
OFFSETS = (1, 3, 2)
STATE_ROW = TOK
LOG_ROW = STATE_ROW + HEAD_DIM
PACK_ROWS = LOG_ROW + 16
ANY = pl.BlockSpec(memory_space=pl.ANY)


def send(block, axis, size, offset):
    return lax.ppermute(block, axis, [(i, (i + offset) % size) for i in range(size)])


def fetch(block, axis, size, offset):
    return send(block, axis, size, -offset)


def dot(a, b, dim_a, dim_b, precision=None):
    return lax.dot_general(
        a, b, (((dim_a,), (dim_b,)), ((), ())), precision=precision, preferred_element_type=F32
    )


def head_cols(h):
    return pl.ds(h * HEAD_DIM, HEAD_DIM)


def shaped(*dims, dtype=F32):
    return jax.ShapeDtypeStruct(dims, dtype)


def call(kernel, out_shape, flops, args, vmem=40, **kwargs):
    return pl.pallas_call(
        kernel,
        out_shape=out_shape,
        cost_estimate=pl.CostEstimate(flops=flops, transcendentals=2**18, bytes_accessed=2 * 2**20),
        compiler_params=pltpu.CompilerParams(vmem_limit_bytes=vmem * 2**20),
        **kwargs,
    )(*args)


def placed(in_specs, out_specs, scratch=(), grid=()):
    return {
        "grid_spec": pltpu.PrefetchScalarGridSpec(
            num_scalar_prefetch=2,
            grid=grid,
            in_specs=in_specs,
            out_specs=out_specs,
            scratch_shapes=list(scratch),
        )
    }


def position(group_ref, index_ref, along_x, side, along_y):
    index = index_ref[0]
    x, y, c = (index >> 3) + along_x, ((index >> 1) & 3) + along_y, (index & 1) + side
    return group_ref[(x & 3) * LINE + (y & 3) * NC + (c & 1)]


def flag(condition):
    return jnp.where(condition, 1, 0)


def causal(scores):
    row = lax.broadcasted_iota(jnp.int32, scores.shape, 0)
    col = lax.broadcasted_iota(jnp.int32, scores.shape, 1)
    return jnp.where(row <= col, scores, NEG)


def hidden(key_pos, query_pos):
    return jnp.where(key_pos > query_pos, -NEG, 0.0)


def staged(items, first, second):
    current = first(items[0])
    for i, item in enumerate(items):
        following = first(items[i + 1]) if i + 1 < len(items) else None
        second(item, current)
        current = following


def forward_a_kernel(
    group_ref, index_ref, q_ref, kv_0, kv_1, kv_2, kv_3, out_ref, stat_ref, k_ref, vt_ref
):
    for o, kv_ref in enumerate((kv_0, kv_1, kv_2, kv_3)):
        k_ref[pl.ds(o * TOK, TOK)] = kv_ref[0]
        vt_ref[0, pl.ds(0, HEAD_DIM), pl.ds(o * TOK, TOK)] = kv_ref[1].T
    vt_ref[0, pl.ds(HEAD_DIM, 16)] = jnp.ones((16, NX * TOK), BF16)
    forward_blocks(0, group_ref, index_ref, q_ref, k_ref, vt_ref, out_ref, stat_ref)


def forward_b_kernel(group_ref, index_ref, q_ref, k_ref, vt_ref, out_ref, stat_ref):
    forward_blocks(1, group_ref, index_ref, q_ref, k_ref, vt_ref, out_ref, stat_ref)


def forward_blocks(side, group_ref, index_ref, q_ref, k_ref, vt_ref, out_ref, stat_ref):
    h = pl.program_id(0)

    @pl.when(h == 0)
    def _():
        stat_ref[...] = jnp.zeros_like(stat_ref)

    key_pos = [position(group_ref, index_ref, o, 0, 0) for o in range(NX)]

    def scores(i):
        return [dot(k_ref[pl.ds(o * TOK, TOK)], q_ref[i], 1, 1) for o in range(NX)]

    def finish(i, parts):
        query_pos = position(group_ref, index_ref, 0, side, i)
        if side == 0 and i == 0:
            parts = [causal(parts[0]), *parts[1:]]
        hide = [hidden(p, query_pos) for p in key_pos]
        tops = [jnp.max(s, axis=0, keepdims=True) - x for s, x in zip(parts, hide)]
        top = functools.reduce(jnp.maximum, tops)
        probs = [
            jnp.exp2((s - (top + x)) * (SCALE * LOG2E)).astype(BF16) for s, x in zip(parts, hide)
        ]
        acc = dot(vt_ref[0], jnp.concatenate(probs), 1, 0)
        total = acc[HEAD_DIM : HEAD_DIM + 1]
        seen = top > 0.5 * NEG
        out_ref[i] = jnp.where(seen, acc[:HEAD_DIM] * (1.0 / total), 0.0).T.astype(BF16)
        log = top * (SCALE * LOG2E) + jnp.log(total) * LOG2E
        stat_ref[i, pl.ds(h, 1)] = jnp.where(seen, log, NEG)

    staged(range(NY), scores, finish)


def rows_spec(first=0):
    return pl.BlockSpec((NY, TOK, HEAD_DIM), lambda h, *_: (0, 0, h + first))


def pair_spec(first=0):
    return pl.BlockSpec((2, TOK, HEAD_DIM), lambda h, *_: (0, 0, h + first))


KEYS_SPEC = pl.BlockSpec((NX * TOK, HEAD_DIM), lambda h, *_: (0, h))
TURNED_SPEC = pl.BlockSpec((1, HEAD_DIM + 16, NX * TOK), lambda h, *_: (h, 0, 0))


def soft_forward(place, kernel, q, keys, key_specs, extra_shapes=(), extra_specs=()):
    return call(
        kernel,
        [shaped(NY, TOK, WIDTH, dtype=BF16), shaped(NY, 8, TOK), *extra_shapes],
        NY * NX * HEADS * 4 * TOK * TOK * HEAD_DIM,
        (*place, q, *keys),
        **placed(
            [rows_spec(), *key_specs],
            [rows_spec(), pl.BlockSpec((NY, 8, TOK), lambda h, *_: (0, 0, 0)), *extra_specs],
            grid=(HEADS,),
        ),
    )


def delta_kernel(g_a, g_b, out_a, out_b, stat_a, stat_b, part_ref):
    h = pl.program_id(0)

    @pl.when(h == 0)
    def _():
        part_ref[0] = stat_a[...]
        part_ref[1] = stat_b[...]

    for side, (g_ref, o_ref) in enumerate(((g_a, out_a), (g_b, out_b))):
        for i in range(NY):
            product = o_ref[i].astype(F32) * g_ref[i].astype(F32)
            part_ref[side, i, pl.ds(h + 4, 1)] = jnp.sum(product.T, axis=0, keepdims=True)


def far_kernel(
    first_head, group_ref, index_ref, qa_ref, qb_ref, ga_ref, gb_ref, kv_1, kv_2, kv_3, stat_ref,
    *refs,
):
    dqa_ref, dqb_ref, dkv_ref, k_ref, v_ref, kt_ref, acc_ref = refs[-7:]
    h = pl.program_id(0) + first_head
    tiles = [pl.ds(o * TOK, TOK) for o in range(NX - 1)]
    for tile, kv_ref in zip(tiles, (kv_1, kv_2, kv_3)):
        k_ref[tile] = kv_ref[0]
        v_ref[tile] = kv_ref[1]
        kt_ref[:, tile] = kv_ref[0].T
    key_pos = [position(group_ref, index_ref, o, 0, 0) for o in range(1, NX)]
    acc_ref[...] = jnp.zeros_like(acc_ref)

    def products(item):
        q_ref, g_ref, _, _, b = item
        return (
            [dot(k_ref[t], q_ref[b], 1, 1) for t in tiles],
            [dot(v_ref[t], g_ref[b], 1, 1) for t in tiles],
        )

    def finish(item, found):
        q_ref, g_ref, dq_ref, side, b = item
        query_pos = position(group_ref, index_ref, 0, side, b)
        lse = stat_ref[side, b, pl.ds(h, 1)]
        delta = stat_ref[side, b, pl.ds(h + 4, 1)]
        probs, grads = [], []
        for x, s, dprobs in zip(key_pos, *found):
            p = jnp.exp2(s * (SCALE * LOG2E) - (lse + hidden(x, query_pos)))
            probs.append(p.astype(BF16))
            grads.append((p * (dprobs - delta)).astype(BF16))
        probs, grads = jnp.concatenate(probs), jnp.concatenate(grads)
        acc_ref[0] += dot(grads, q_ref[b], 1, 0)
        acc_ref[1] += dot(probs, g_ref[b], 1, 0)
        dq_ref[b, 0] = dot(kt_ref[...], grads, 1, 0)

    items = [(qa_ref, ga_ref, dqa_ref, 0, b) for b in range(NY)]
    items += [(qb_ref, gb_ref, dqb_ref, 1, b) for b in range(NY)]
    staged(items, products, finish)
    for o, tile in enumerate(tiles):
        dkv_ref[o, 0] = (acc_ref[0, tile] * SCALE).astype(BF16)
        dkv_ref[o, 1] = acc_ref[1, tile].astype(BF16)


STAT_SPEC = pl.BlockSpec((2, NY, 8, TOK), lambda h, *_: (0, 0, 0, 0))


def far_backward(place, first, heads, qa, qb, ga, gb, kvs, stats, earlier=()):
    rows, pair = rows_spec(first), pair_spec(first)
    turned = pl.BlockSpec((NY, 1, HEAD_DIM, TOK), lambda h, *_: (0, h + first, 0, 0))
    dq_shape = shaped(NY, HEADS, HEAD_DIM, TOK)
    kwargs = placed(
        [rows] * 4 + [pair] * (NX - 1) + [STAT_SPEC] + [ANY] * len(earlier),
        [
            turned,
            turned,
            pl.BlockSpec((NX - 1, 2, TOK, HEAD_DIM), lambda h, *_: (0, 0, 0, h + first)),
        ],
        [
            pltpu.VMEM(((NX - 1) * TOK, HEAD_DIM), BF16),
            pltpu.VMEM(((NX - 1) * TOK, HEAD_DIM), BF16),
            pltpu.VMEM((HEAD_DIM, (NX - 1) * TOK), BF16),
            pltpu.VMEM((2, (NX - 1) * TOK, HEAD_DIM), F32),
        ],
        (heads,),
    )
    return call(
        functools.partial(far_kernel, first),
        [dq_shape, dq_shape, shaped(NX - 1, 2, TOK, WIDTH, dtype=BF16)],
        2 * NY * (NX - 1) * heads * 10 * TOK * TOK * HEAD_DIM,
        (*place, qa, qb, ga, gb, *kvs, stats, *earlier),
        input_output_aliases={10 + i: i for i in range(len(earlier))},
        **kwargs,
    )


def near_kernel(
    group_ref, index_ref, qa_ref, qb_ref, ga_ref, gb_ref, kv_ref, stat_ref, dqa_in, dqb_in,
    dqa_ref, dqb_ref, dkv_ref, kt_ref,
):
    h = pl.program_id(0)
    kt_ref[...] = kv_ref[0].T
    own = position(group_ref, index_ref, 0, 0, 0)

    def products(item):
        q_ref, g_ref, b = item[0], item[1], item[-1]
        return dot(kv_ref[0], q_ref[b], 1, 1), dot(kv_ref[1], g_ref[b], 1, 1)

    def finish(item, found):
        q_ref, g_ref, dq_in, dq_ref, side, b = item
        s, dprobs = found
        lse = stat_ref[side, b, pl.ds(h, 1)]
        delta = stat_ref[side, b, pl.ds(h + 4, 1)]
        s = s * (SCALE * LOG2E)
        start = side == 0 and b == 0
        if start:
            s = causal(s)
        p = jnp.exp2(s - (lse + hidden(own, position(group_ref, index_ref, 0, side, b))))
        ds = (p * (dprobs - delta)).astype(BF16)
        dq_sum = dq_in[b, 0] + dot(kt_ref[...], ds, 1, 0)
        dq_ref[b] = (dq_sum * SCALE).T.astype(BF16)
        dk, dv = dot(ds, q_ref[b], 1, 0) * SCALE, dot(p.astype(BF16), g_ref[b], 1, 0)
        dkv_ref[0] = dk if start else dkv_ref[0] + dk
        dkv_ref[1] = dv if start else dkv_ref[1] + dv

    sides = ((qa_ref, ga_ref, dqa_in, dqa_ref), (qb_ref, gb_ref, dqb_in, dqb_ref))
    items = [(*refs, side, b) for side, refs in enumerate(sides) for b in range(NY)]
    staged(items, products, finish)


def near_backward(place, qa, qb, ga, gb, kv, stats, dqa, dqb):
    rows, pair = rows_spec(), pair_spec()
    turned = pl.BlockSpec((NY, 1, HEAD_DIM, TOK), lambda h, *_: (0, h, 0, 0))
    return call(
        near_kernel,
        [
            shaped(NY, TOK, WIDTH, dtype=BF16),
            shaped(NY, TOK, WIDTH, dtype=BF16),
            shaped(2, TOK, WIDTH),
        ],
        2 * NY * HEADS * 10 * TOK * TOK * HEAD_DIM,
        (*place, qa, qb, ga, gb, kv, stats, dqa, dqb),
        **placed(
            [rows] * 4 + [pair, STAT_SPEC, turned, turned],
            [rows, rows, pair],
            [pltpu.VMEM((HEAD_DIM, TOK), BF16)],
            (HEADS,),
        ),
    )


def merged(stats_a, stats_b):
    lse_a, lse_b = stats_a[..., :4, :], stats_b[..., :4, :]
    top = jnp.maximum(lse_a, lse_b)
    weight_a, weight_b = jnp.exp2(lse_a - top), jnp.exp2(lse_b - top)
    total = weight_a + weight_b
    delta = (weight_a * stats_a[..., 4:, :] + weight_b * stats_b[..., 4:, :]) / total
    return jnp.concatenate([top + jnp.log(total) * LOG2E, delta], axis=-2)


def chip_kernel(part_ref, other_ref, out_ref):
    for side in range(2):
        out_ref[side] = merged(part_ref[side], other_ref[1 - side])


def line_kernel(
    part_ref, chip_ref, from_1, from_2, from_3, out_a_ref, out_b_ref,
    stat_ref, mine_ref, theirs_ref,
):
    for side, o_ref in enumerate((out_a_ref, out_b_ref)):
        for i in range(NY):
            stats = chip_ref[side, i]
            for o, other in ((1, from_1), (2, from_2), (3, from_3)):
                stats = merged(stats, other[side, (i - o) % NY])
            stat_ref[side, i] = stats
            weight = jnp.exp2(part_ref[side, i, :4] - stats[:4])
            weight = jnp.concatenate([weight] * (HEAD_DIM // 4), axis=0).T
            for h in range(HEADS):
                scaled = o_ref[i, :, head_cols(h)].astype(F32) * weight[:, h : h + 1]
                if side == 0:
                    mine_ref[i, :, head_cols(h)] = scaled
                else:
                    theirs_ref[pl.ds(i * TOK, TOK), head_cols(h)] = scaled.astype(BF16)


def join_kernel(mine_ref, core_ref, read_ref, pair_ref, own_ref, pay_1, pay_2, pay_3):
    own_ref[...] = mine_ref[0] + core_ref[pl.ds(0, TOK)].astype(F32)
    for o, pay in ((1, pay_1), (2, pay_2), (3, pay_3)):
        total = mine_ref[o] + core_ref[pl.ds(o * TOK, TOK)].astype(F32)
        pay[pl.ds(0, TOK)] = total.astype(BF16)
        pay[pl.ds(TOK, HEAD_DIM)] = read_ref[...]
        pay[pl.ds(TOK + HEAD_DIM, HEAD_DIM)] = pair_ref[...]


def triangle(upper):
    row = lax.broadcasted_iota(jnp.int32, (TOK, TOK), 0)
    col = lax.broadcasted_iota(jnp.int32, (TOK, TOK), 1)
    return row <= col if upper else row >= col


def decay_columns(decay):
    return dot(triangle(False).astype(F32), decay[...], 1, 1, HIGHEST)


def log_pieces(log):
    log = jnp.broadcast_to(log, (16, log.shape[1]))
    row = lax.broadcasted_iota(jnp.int32, log.shape, 0)
    high = log.astype(BF16).astype(F32)
    middle = (log - high).astype(BF16).astype(F32)
    low = log - high - middle
    piece = jnp.where(row == 0, high, jnp.where(row == 1, middle, jnp.where(row == 2, low, 0.0)))
    return piece.astype(BF16)


def whole_log(pieces):
    pieces = pieces.astype(F32)
    return pieces[0:1] + pieces[1:2] + pieces[2:3]


def pack_kernel(g_ref, key_ref, value_ref, decay_ref, out_ref):
    cumulative = decay_columns(decay_ref)
    total = cumulative[TOK - 1 : TOK]
    tail = jnp.exp(total - cumulative)
    out_ref[pl.ds(0, TOK)] = g_ref[...]
    for h in range(HEADS):
        keys = key_ref[:, head_cols(h)].astype(F32) * tail[:, h : h + 1]
        state = dot(keys.astype(BF16), value_ref[:, head_cols(h)], 0, 0)
        out_ref[pl.ds(STATE_ROW, HEAD_DIM), head_cols(h)] = state.astype(BF16)
        log = jnp.broadcast_to(total[:, h : h + 1], (1, HEAD_DIM))
        out_ref[pl.ds(LOG_ROW, 16), head_cols(h)] = log_pieces(log)


def least(values):
    return functools.reduce(jnp.minimum, values)


def chain_keys(group_ref, index_ref, along_x, forward):
    found = [
        position(group_ref, index_ref, along_x, side, j) for side in range(NC) for j in range(NY)
    ]
    return found if forward else [31 - p for p in found]


def chain_members(keys):
    apart = -least([-k for k in keys]) - least(keys) > LINE - 1
    handed = [flag(jnp.logical_or(k < LINE, jnp.logical_not(apart))) for k in keys]
    whole = flag(jnp.logical_not(apart))
    same = [jnp.maximum(whole, flag(flag(k < LINE) == flag(keys[0] < LINE))) for k in keys]
    return handed, same


def line_sums(keys, logs, states):
    handed, same = chain_members(keys)
    before = [s * flag(k < keys[0]) for s, k in zip(same, keys)]

    def weighted(members):
        total = jnp.zeros((HEAD_DIM, WIDTH), F32)
        for j in range(LINE):
            exponent = jnp.zeros((1, WIDTH), F32)
            for i in range(LINE):
                if i != j:
                    between = members[i] * flag(keys[i] > keys[j])
                    exponent = exponent + logs[i] * between.astype(F32)
            weight = jnp.exp(exponent) * members[j].astype(F32)
            total = total + weight * states[j]()
        return total

    prefix = sum(log * b.astype(F32) for log, b in zip(logs, before))
    return weighted(handed), weighted(before), prefix


def total_sums(group_ref, index_ref, forward, totals, line_logs, prefix):
    lines = [chain_keys(group_ref, index_ref, o, forward) for o in range(NX)]
    starts = [least(keys) for keys in lines]
    same = chain_members(lines[0])[1]
    own_start = least([jnp.where(s > 0, k, 99) for s, k in zip(same, lines[0])])
    earlier = [flag(s < own_start) for s in starts]
    result = 0.0
    for o in range(NX):
        exponent = prefix
        for i in range(NX):
            if i != o:
                between = earlier[i] * flag(starts[i] > starts[o])
                exponent = exponent + line_logs[i] * between.astype(F32)
        result = result + jnp.exp(exponent) * earlier[o].astype(F32) * totals[o].astype(F32)
    return result


def states_kernel(group_ref, index_ref, ga_ref, gb_ref, handed_ref, entry_ref, log_ref):
    logs, states = [], []
    for ref in (ga_ref, gb_ref):
        for i in range(NY):
            logs.append(whole_log(ref[i, pl.ds(LOG_ROW, 16)]))
            states.append(
                functools.partial(
                    lambda ref, i: ref[i, pl.ds(STATE_ROW, HEAD_DIM)].astype(F32), ref, i
                )
            )
    keys = chain_keys(group_ref, index_ref, 0, True)
    handed, entry, prefix = line_sums(keys, logs, states)
    handed_ref[pl.ds(0, HEAD_DIM)] = handed.astype(BF16)
    handed_ref[pl.ds(HEAD_DIM, 16)] = log_pieces(sum(logs))
    entry_ref[pl.ds(0, HEAD_DIM)] = entry
    entry_ref[pl.ds(HEAD_DIM, 8)] = jnp.broadcast_to(prefix, (8, WIDTH))
    for j in range(LINE):
        log_ref[pl.ds(j, 1)] = logs[j]


def decay_rows(decay_ref):
    return dot(decay_ref[...], triangle(True).astype(F32), 1, 0, HIGHEST)


def inner_decay(rows, cumulative, h):
    gap = cumulative[:, h : h + 1] - rows[h : h + 1]
    return jnp.where(triangle(False), jnp.exp(jnp.minimum(gap, 0.0)), 0.0)


def local_kernel(q_ref, k_ref, v_ref, decay_ref, local_ref, score_ref):
    cumulative, decay_in_rows = decay_columns(decay_ref), decay_rows(decay_ref)
    for h in range(HEADS):
        cols = head_cols(h)
        decay = inner_decay(decay_in_rows, cumulative, h)
        scores = (dot(q_ref[:, cols], k_ref[:, cols], 1, 1) * decay).astype(BF16)
        score_ref[h] = scores
        local_ref[:, cols] = dot(scores, v_ref[:, cols], 1, 0)


def read_kernel(
    group_ref, index_ref, q_ref, local_ref, g_ref, decay_ref, part_ref, own, from_1, from_2,
    from_3, raw_ref, sum_ref, entry_ref, log_ref,
):
    all_totals = (own, from_1, from_2, from_3)
    line_logs = [whole_log(t[pl.ds(HEAD_DIM, 16)]) for t in all_totals]
    for o in range(NX):
        log_ref[pl.ds(o, 1)] = line_logs[o]
    log_ref[pl.ds(NX, 4)] = jnp.zeros((4, WIDTH), F32)
    entry = part_ref[pl.ds(0, HEAD_DIM)] + total_sums(
        group_ref, index_ref, True, [t[pl.ds(0, HEAD_DIM)] for t in all_totals], line_logs,
        part_ref[pl.ds(HEAD_DIM, 1)],
    )
    entry_ref[...] = entry.astype(BF16)
    cumulative = decay_columns(decay_ref)
    squares = jnp.zeros((TOK, 1), F32)
    inner = jnp.zeros((TOK, 1), F32)
    for h in range(HEADS):
        cols = head_cols(h)
        carried = dot(q_ref[:, cols], entry_ref[:, cols], 1, 0)
        raw = local_ref[:, cols] + jnp.exp(cumulative[:, h : h + 1]) * carried
        raw_ref[:, cols] = raw
        squares = squares + jnp.sum(raw * raw, axis=1, keepdims=True)
        inner = inner + jnp.sum(raw * g_ref[:, cols].astype(F32), axis=1, keepdims=True)
    lane = lax.broadcasted_iota(jnp.int32, (TOK, HEAD_DIM), 1)
    sums = jnp.where(lane == 0, squares, jnp.where(lane == 1, inner, 0.0))
    sum_ref[...] = sums.T[:8]


def grad_kernel(
    q_ref, k_ref, v_ref, g_ref, decay_ref, score_ref, entry_ref, raw_ref, sum_0, sum_1, sum_2, sum_3,
    out_ref, dq_ref, dk_ref, dv_ref, read_ref,
):
    cumulative, decay_in_rows = decay_columns(decay_ref), decay_rows(decay_ref)
    sums = (sum_0[...] + sum_1[...]) + (sum_2[...] + sum_3[...])
    sums = jnp.concatenate([sums] * (HEAD_DIM // 8), axis=0).T
    inverse = 1.0 / jnp.sqrt(sums[:, 0:1] * (1.0 / (HEAD_TOTAL * HEAD_DIM)) + EPS)
    aligned = sums[:, 1:2] * inverse * (1.0 / (HEAD_TOTAL * HEAD_DIM))
    for h in range(HEADS):
        cols = head_cols(h)
        q, k = q_ref[:, cols], k_ref[:, cols]
        out = raw_ref[:, cols] * inverse
        out_ref[:, cols] = out
        raw_grad = ((g_ref[:, cols].astype(F32) - out * aligned) * inverse).astype(BF16)
        decay = inner_decay(decay_in_rows, cumulative, h)
        head_decay = jnp.exp(cumulative[:, h : h + 1])
        inner_grad = (dot(raw_grad, v_ref[:, cols], 1, 1) * decay).astype(BF16)
        carried = dot(raw_grad, entry_ref[:, cols], 1, 1)
        dq_ref[:, cols] = dot(inner_grad, k, 1, 0) + head_decay * carried
        dk_ref[:, cols] = dot(inner_grad, q, 0, 0)
        dv_ref[:, cols] = dot(score_ref[h], raw_grad, 0, 0)
        scaled = (q.astype(F32) * head_decay).astype(BF16)
        read_ref[:, cols] = dot(scaled, raw_grad, 0, 0).astype(BF16)


def back_kernel(
    group_ref, index_ref, log_ref, read_ref, pair_ref, from_1, from_2, from_3, handed_ref, part_ref
):
    logs = [log_ref[pl.ds(j, 1)] for j in range(LINE)]
    sources = [(read_ref, 0), (from_1, TOK), (from_2, TOK), (from_3, TOK)]
    sources += [(pair_ref, 0)]
    sources += [(ref, TOK + HEAD_DIM) for ref in (from_1, from_2, from_3)]
    states = [
        functools.partial(lambda ref, row: ref[pl.ds(row, HEAD_DIM)].astype(F32), ref, row)
        for ref, row in sources
    ]
    keys = chain_keys(group_ref, index_ref, 0, False)
    handed, part, prefix = line_sums(keys, logs, states)
    handed_ref[...] = handed.astype(BF16)
    part_ref[pl.ds(0, HEAD_DIM)] = part
    part_ref[pl.ds(HEAD_DIM, 8)] = jnp.broadcast_to(prefix, (8, WIDTH))


def write_kernel(
    group_ref, index_ref, k_ref, v_ref, decay_ref, part_ref, log_ref, own, from_1, from_2, from_3,
    dk_in, dv_in, dk_ref, dv_ref,
):
    leave_all = part_ref[pl.ds(0, HEAD_DIM)] + total_sums(
        group_ref, index_ref, False, [t[...] for t in (own, from_1, from_2, from_3)],
        [log_ref[pl.ds(o, 1)] for o in range(NX)], part_ref[pl.ds(HEAD_DIM, 1)],
    )
    cumulative = decay_columns(decay_ref)
    tail = jnp.exp(cumulative[TOK - 1 : TOK] - cumulative)
    for h in range(HEADS):
        cols = head_cols(h)
        leave = leave_all[:, h * HEAD_DIM : (h + 1) * HEAD_DIM].astype(BF16)
        scale = tail[:, h : h + 1]
        dk_ref[:, cols] = dk_in[:, cols] + scale * dot(v_ref[:, cols], leave, 1, 1)
        dv_ref[:, cols] = dv_in[:, cols] + scale * dot(k_ref[:, cols], leave, 1, 0)


def in_vmem(n):
    return [pl.BlockSpec(memory_space=pltpu.VMEM)] * n


def on_device(
    group_of, soft_query, soft_key, soft_value, soft_grad,
    lin_query, lin_key, lin_value, log_decay, lin_grad,
):
    place = (group_of, lax.axis_index(SEQ).reshape(1))
    decay = log_decay.T

    kv_own = jnp.stack([soft_key, soft_value])
    kv = {0: kv_own, **{o: fetch(kv_own, "x", NX, o) for o in OFFSETS}}
    kvs = [kv[o] for o in range(NX)]
    packed = call(
        pack_kernel,
        shaped(PACK_ROWS, WIDTH, dtype=BF16),
        2**26,
        (soft_grad, lin_key, lin_value, decay),
    )
    q_from = {0: soft_query, **{o: fetch(soft_query, "y", NY, o) for o in OFFSETS}}
    g_from = {0: packed, **{o: fetch(packed, "y", NY, o) for o in OFFSETS}}
    qa = jnp.stack([q_from[o] for o in range(NY)])
    qb = fetch(qa, "c", NC, 1)
    ga = jnp.stack([g_from[o] for o in range(NY)])
    gb = fetch(ga, "c", NC, 1)

    out_a, stat_a, keys, values_turned = soft_forward(
        place, forward_a_kernel, qa, kvs, [pair_spec()] * NX,
        [
            shaped(NX * TOK, WIDTH, dtype=BF16),
            shaped(HEADS, HEAD_DIM + 16, NX * TOK, dtype=BF16),
        ],
        [KEYS_SPEC, TURNED_SPEC],
    )
    handed, entry_part, logs = call(
        states_kernel,
        [
            shaped(HEAD_DIM + 16, WIDTH, dtype=BF16),
            shaped(HEAD_DIM + 8, WIDTH),
            shaped(8, WIDTH),
        ],
        2**24,
        (*place, ga, gb),
        **placed(in_vmem(2), in_vmem(3)),
    )
    totals = [handed, *(fetch(handed, "x", NX, o) for o in (1, 2, 3))]
    out_b, stat_b = soft_forward(
        place, forward_b_kernel, qb, (keys, values_turned), [KEYS_SPEC, TURNED_SPEC]
    )
    part = call(
        delta_kernel,
        shaped(2, NY, 8, TOK),
        2**25,
        (ga, gb, out_a, out_b, stat_a, stat_b),
        grid=(HEADS,),
        in_specs=[rows_spec()] * 4 + [pl.BlockSpec((NY, 8, TOK), lambda h: (0, 0, 0))] * 2,
        out_specs=pl.BlockSpec((2, NY, 8, TOK), lambda h: (0, 0, 0, 0)),
    )
    other = fetch(part, "c", NC, 1)

    rows = shaped(TOK, WIDTH)
    local_out, inner_scores = call(
        local_kernel,
        [rows, shaped(HEADS, TOK, TOK, dtype=BF16)],
        2**27,
        (lin_query, lin_key, lin_value, decay),
    )
    raw, sums, entry, line_logs = call(
        read_kernel,
        [rows, shaped(8, TOK), shaped(HEAD_DIM, WIDTH, dtype=BF16), shaped(8, WIDTH)],
        2**27,
        (*place, lin_query, local_out, lin_grad, decay, entry_part, *totals),
        **placed(in_vmem(9), in_vmem(4)),
    )
    all_sums = [sums, *(fetch(sums, "head", NZ, o) for o in (1, 2, 3))]
    chip = call(chip_kernel, shaped(2, NY, 8, TOK), 2**20, (part, other))
    received = {o: fetch(chip, "y", NY, o) for o in OFFSETS}
    lin_out, lin_dq, dk_local, dv_local, read_grad = call(
        grad_kernel,
        [rows] * 4 + [shaped(HEAD_DIM, WIDTH, dtype=BF16)],
        2**28,
        (lin_query, lin_key, lin_value, lin_grad, decay, inner_scores, entry, raw, *all_sums),
    )
    stats, mine, theirs = call(
        line_kernel,
        [
            shaped(2, NY, 8, TOK),
            shaped(NY, TOK, WIDTH),
            shaped(NY * TOK, WIDTH, dtype=BF16),
        ],
        2**22,
        (part, chip, received[1], received[2], received[3], out_a, out_b),
    )
    from_core = fetch(theirs, "c", NC, 1)
    pair_read = fetch(read_grad, "c", NC, 1)

    grads = far_backward(place, 0, 1, qa, qb, ga, gb, kvs[1:], stats)
    own_out, *pays = call(
        join_kernel,
        [rows] + [shaped(2 * TOK, WIDTH, dtype=BF16)] * 3,
        2**22,
        (mine, from_core, read_grad, pair_read),
    )
    sent_out = {o: send(pays[o - 1], "y", NY, o) for o in OFFSETS}
    dq_a, dq_b, far_dkv = far_backward(place, 1, 2, qa, qb, ga, gb, kvs[1:], stats, tuple(grads))
    sent_dkv = [send(far_dkv[o - 1], "x", NX, o) for o in OFFSETS]
    dq_a, dq_b, near_dkv = near_backward(place, qa, qb, ga, gb, kvs[0], stats, dq_a, dq_b)
    dq_core = fetch(dq_b, "c", NC, 1)

    back_handed, leave_part = call(
        back_kernel,
        [shaped(HEAD_DIM, WIDTH, dtype=BF16), shaped(HEAD_DIM + 8, WIDTH)],
        2**24,
        (*place, logs, read_grad, pair_read, *(sent_out[NY - o] for o in (1, 2, 3))),
        **placed(in_vmem(6), in_vmem(2)),
    )
    back_totals = [back_handed, *(fetch(back_handed, "x", NX, o) for o in (1, 2, 3))]
    chip_dq = dq_a.astype(F32) + dq_core.astype(F32)
    soft_dq = chip_dq[0]
    for o in OFFSETS:
        soft_dq = soft_dq + send(chip_dq[o].astype(BF16), "y", NY, o).astype(F32)
    lin_dk, lin_dv = call(
        write_kernel,
        [rows, rows],
        2**26,
        (*place, lin_key, lin_value, decay, leave_part, line_logs, *back_totals, dk_local, dv_local),
        **placed(in_vmem(11), in_vmem(2)),
    )
    soft_out = own_out
    for o in OFFSETS:
        soft_out = soft_out + sent_out[o][:TOK].astype(F32)
    soft_out = soft_out.astype(BF16)
    dkv = near_dkv
    for sent in sent_dkv:
        dkv = dkv + sent.astype(F32)
    soft_dk, soft_dv = dkv[0].astype(BF16), dkv[1].astype(BF16)
    return (
        soft_out, soft_dq.astype(BF16), soft_dk, soft_dv, lin_out, lin_dq, lin_dk, lin_dv,
    )


def solution(mesh):
    grid = Mesh(mesh.devices.reshape(NX, NY, NC, NZ), (*SEQ, "head"))
    block = P(SEQ, "head")

    return jax.shard_map(
        on_device,
        mesh=grid,
        in_specs=(P(),) + (block,) * 9,
        out_specs=(block,) * 8,
        check_vma=False,
    )
```
